32 devices in a mesh: groups: 2 (over y), space: 4 (over z), tm: 2 (over x), chan: 2 (over core).
Axes of the slice: x: 2, y: 2, z: 4, core: 2. Of those that a mesh axis runs over, the one named last changes fastest.
Arguments:
- hidden_states: bfloat16 [8, 4, 64, 512], P(('groups', 'tm'), 'space', None, 'chan'), parts along dimension 0, may hold values from -25 to 25
- first_gain: float32 [512], P('chan'), may hold values from 0.1 to 1.9
- second_gain: float32 [512], P('chan'), may hold values from 0.1 to 1.9
- query_weight: bfloat16 [512, 512], replicated, may hold values from -0.4861359 to 0.4861359
- key_weight: bfloat16 [512, 512], replicated, may hold values from -0.4861359 to 0.4861359
- value_weight: bfloat16 [512, 512], replicated, may hold values from -0.25 to 0.25
- out_weight: bfloat16 [512, 512], replicated, may hold values from -0.25 to 0.25
- conv_kernel: bfloat16 [3, 3, 3, 512, 512], P(None, None, None, 'tm', 'chan'), may hold values from -0.0546875 to 0.0546875
Outputs:
- attended: bfloat16 [8, 4, 64, 512], P(('groups', 'tm'), 'space', None, 'chan'), parts along dimension 0
- convolved: bfloat16 [8, 4, 64, 512], P(('groups', 'tm'), 'space', None, 'chan'), parts along dimension 0
The draws below stay inside these ranges and needn't reach their ends.
There are 2 independent parts, one for each index of `groups`. The reference program is written for one: setup_inputs(seed, part) draws one part's arguments, and reference() takes and returns one part's arrays. A program takes and returns all parts, laid end to end along the dimension named above; an argument that names none is the same for every part. Nothing has to cross between parts.
All inputs are finite; a program needn't handle non-finite values.
Results may differ from the reference program's by a relative error of at most 0.012.
The reference program's roundings to bfloat16 on the way count: a program that leaves them out, or rounds other values in their place, can miss the bound.
Values may be sent and summed in bfloat16 or wider, within the bound.
A program may use at most 64 MiB of HBM per device.

```python
import jax
import jax.numpy as jnp
from jax import lax

D = 512
NGROUP = 32
W = 64
NF = 4
NH = 4


def draw_hidden_states(key, part):
    normal_key = jax.random.fold_in(key, 1)
    channel_key = jax.random.fold_in(key, 2)
    jitter_key = jax.random.fold_in(key, 3)
    frame_pos = jnp.arange(NF, dtype=jnp.float32) / (NF - 1)
    row_pos = jnp.arange(NH, dtype=jnp.float32) / (NH - 1)
    exponent = 0.5 * frame_pos[:, None] + 0.5 * row_pos[None, :] - 1.0
    jitter = jax.random.uniform(jitter_key, (NF, NH, W), minval=-0.1, maxval=0.1)
    token_scale = 10.0 ** (exponent[:, :, None] + jitter)
    channel_scale = jnp.exp(jax.random.uniform(channel_key, (D,), minval=jnp.log(0.5), maxval=jnp.log(5.0)))
    base = jnp.clip(jax.random.normal(normal_key, (NF, NH, W, D)), -3.5, 3.5)
    return (base * token_scale[:, :, :, None] * channel_scale).astype(jnp.bfloat16)


def drawn_pair(key):
    first = jnp.clip(jax.random.normal(jax.random.fold_in(key, 12), (D, D)), -4.5, 4.5)
    second = jnp.clip(jax.random.normal(jax.random.fold_in(key, 13), (D, D)), -4.5, 4.5)
    return (first, second)


def draw_query_weight(key, part):
    first, second = drawn_pair(key)
    result = first
    return (result * D ** (-0.5)).astype(jnp.bfloat16)


def draw_key_weight(key, part):
    first, second = drawn_pair(key)
    result = second
    return (result * D ** (-0.5)).astype(jnp.bfloat16)


def block_scale(own_key, extent, split, smallest, largest):
    def one(dim, parts):
        draws = jax.random.uniform(jax.random.fold_in(jax.random.fold_in(own_key, 6), dim), (parts,), jnp.float32, smallest / len(split), largest / len(split))
        return jnp.repeat(jnp.exp(draws), extent[dim] // parts).reshape((-1,) + (1,) * (len(extent) - dim - 1))

    loudness = one(*split[0])
    for cut in split[1:]:
        loudness = loudness * one(*cut)
    return loudness


def gaussian(rng, extent, scale, limit, split=(), held_as=jnp.bfloat16):
    gain = block_scale(rng, extent, split, -0.22, 0.18) if split else 1.0
    drawn = jax.random.normal(rng, extent, jnp.float32) * scale * gain
    return jnp.minimum(jnp.maximum(drawn, -limit), limit).astype(held_as)


def setup_inputs(seed: int = 0, part: int = 0) -> dict:
    arg_keys = jax.random.split(jax.random.key(seed), 9)
    own_keys = jax.random.split(jax.random.fold_in(arg_keys[8], part), 9)
    return {
        "hidden_states": draw_hidden_states(jax.random.fold_in(jax.random.fold_in(arg_keys[8], part), 71), part),
        "first_gain": jnp.clip(1.0 + 0.18 * jax.random.normal(arg_keys[1], (D,), jnp.float32), 0.1, 1.9),
        "second_gain": jnp.clip(1.0 + 0.18 * jax.random.normal(arg_keys[2], (D,), jnp.float32), 0.1, 1.9),
        "query_weight": draw_query_weight(jax.random.fold_in(arg_keys[8], 71), part),
        "key_weight": draw_key_weight(jax.random.fold_in(arg_keys[8], 71), part),
        "value_weight": gaussian(arg_keys[5], (D, D), D ** -0.5, 0.25),
        "out_weight": gaussian(arg_keys[6], (D, D), D ** -0.5, 0.25),
        "conv_kernel": gaussian(arg_keys[7], (3, 3, 3, D, D), (27 * D) ** -0.5, 0.0546875, ((3, 2), (4, 2))),
    }


EPSILON = 1e-06

def group_norm(source, gain_vector):
    grouped = source.reshape(-1, NGROUP, D // NGROUP)
    centre = lax.optimization_barrier(jnp.mean(grouped, axis=(0, 2)))
    shifted = grouped - centre[None, :, None]
    spread = lax.optimization_barrier(jnp.mean(shifted * shifted, axis=(0, 2)))
    scaled = shifted * lax.rsqrt(spread + EPSILON)[None, :, None]
    return scaled.reshape(source.shape) * gain_vector

def reference(hidden_states, first_gain, second_gain, query_weight, key_weight, value_weight, out_weight, conv_kernel):
    source = hidden_states.astype(jnp.float32)
    normed = group_norm(source, first_gain).astype(jnp.bfloat16)
    frame_tokens = normed.reshape(NF, NH * W, D)

    def frame_attention(tokens):
        queries = jnp.dot(tokens, query_weight, preferred_element_type=jnp.float32).astype(jnp.bfloat16)
        keyed = jnp.dot(tokens, key_weight, preferred_element_type=jnp.float32).astype(jnp.bfloat16)
        valued = jnp.dot(tokens, value_weight, preferred_element_type=jnp.float32).astype(jnp.bfloat16)
        scores = jnp.dot(queries, keyed.T, preferred_element_type=jnp.float32) * D ** (-0.5)
        peaked = lax.optimization_barrier(jnp.max(scores, axis=1))
        weights = jnp.exp(scores - peaked[:, None])
        mass = lax.optimization_barrier(jnp.sum(weights, axis=1))
        mixed = jnp.dot(weights.astype(jnp.bfloat16), valued, preferred_element_type=jnp.float32)
        mixed = (mixed / mass[:, None]).astype(jnp.bfloat16)
        return jnp.dot(mixed, out_weight, preferred_element_type=jnp.float32).astype(jnp.bfloat16)
    attended = lax.map(frame_attention, frame_tokens).reshape(source.shape)
    resid = source + attended.astype(jnp.float32)
    activated = jax.nn.silu(group_norm(resid, second_gain)).astype(jnp.bfloat16)
    convolved = lax.conv_general_dilated(activated.astype(jnp.float32)[None], conv_kernel.astype(jnp.float32), (1, 1, 1), [(2, 0), (1, 1), (1, 1)], dimension_numbers=('NDHWC', 'DHWIO', 'NDHWC'), precision=lax.Precision.HIGHEST)[0]
    return (attended, convolved.astype(jnp.bfloat16))
```

```python
import functools

import jax
import jax.numpy as jnp
from jax import lax
from jax.experimental import pallas as pl
from jax.experimental.pallas import tpu as pltpu
from jax.sharding import PartitionSpec as P

D = 512
NGROUP = 32
EPSILON = 1e-06
LANES = 128
CHUNKS = 2
GROUP = D // NGROUP
MESH = pl.DeviceIdType.MESH
F32 = jnp.float32
BF16 = jnp.bfloat16


def group_total(v):
    lane = lax.broadcasted_iota(jnp.int32, v.shape, 1)
    width = v.shape[1]
    step = 1
    while step < GROUP:
        above = pltpu.roll(v, width - step, 1)
        below = pltpu.roll(v, step, 1)
        v = v + jnp.where((lane // step) % 2 == 0, above, below)
        step *= 2
    return v


def channel_sums(values):
    return jnp.sum(values, axis=0, keepdims=True), jnp.sum(values * values, axis=0, keepdims=True)


def moments(totals, population):
    blocks = totals.shape[1] // LANES
    pieces = [totals[k : k + 1, b * LANES : (b + 1) * LANES] for k in range(2) for b in range(blocks)]
    rows = 8 * pl.cdiv(2 * blocks, 8)
    grouped = group_total(jnp.concatenate(pieces + pieces[:1] * (rows - 2 * blocks), axis=0)) / population
    mean = jnp.concatenate([grouped[b : b + 1] for b in range(blocks)], axis=1)
    square = jnp.concatenate([grouped[blocks + b : blocks + b + 1] for b in range(blocks)], axis=1)
    variance = jnp.maximum(square - mean * mean, 0.0)
    return mean, lax.rsqrt(variance + EPSILON)


def kernel(
    S, T, C, W,
    x_hbm, g1, g2, wq_hbm, wk_hbm, wv_hbm, wo_hbm, wc_hbm,
    att_out, conv_out,
    x, wq, wk, wv, wo, wc,
    stat1_src, stat1, stat2_src, stat2, gall1, gall2,
    xall, tokens, keyed, valued, att_src, att_in, dsrc, dall, act, own_total, part_src, part,
    xload, wsem, insem, send_sem, gsem, s1send, s1sem, xsend, xsem, s2sem,
    asend, asem, dsend, dsem, last_sem, share_sem, psend, psem,
):
    g = lax.axis_index("groups")
    h = lax.axis_index("space")
    t = lax.axis_index("tm")
    c = lax.axis_index("chan")
    n = S * T * C
    chip = h * T + t
    me = chip * C + c
    half = D // C
    Kc = D // T
    NF = T * C
    other = lax.rem(c + 1, C)
    inner = (h > 0) & (h < S - 1)
    attends = h < S - 1

    def rows_apart(sign, act_on):
        def row(d):
            @pl.when((h + sign * d >= 0) & (h + sign * d < S))
            def _():
                act_on(h + sign * d, d)

        pl.loop(1, S, unroll=S <= 4)(row)

    def row_devices(r, act_on):
        for dt in range(T):
            for dc in range(C):
                act_on((g, r, lax.rem(t + dt, T), lax.rem(c + dc, C)))

    def beside(sign, act_on):
        for dt in range(1, T):

            @pl.when((t + sign * dt >= 0) & (t + sign * dt < T))
            def _():
                for dc in range(C):
                    act_on((g, h, t + sign * dt, lax.rem(c + dc, C)))

    def mates(act_on):
        for dc in range(1, C):
            act_on((g, h, t, lax.rem(c + dc, C)))

    def signal(sem):
        return lambda where: pl.semaphore_signal(sem, inc=1, device_id=where, device_id_type=MESH)

    def drain(ref, sem):
        pltpu.make_async_copy(ref, ref, sem).wait()

    first = [
        pltpu.make_async_copy(src, dst, xload.at[i])
        for i, (src, dst) in enumerate([(x_hbm, x), (g1, gall1.at[c]), (g2, gall2.at[c])])
    ]
    for load in first:
        load.start()
    barrier = pltpu.get_barrier_semaphore()
    mates(signal(barrier))
    beside(1, signal(barrier))
    rows_apart(1, lambda r, d: row_devices(r, signal(barrier)))
    pl.semaphore_wait(barrier, chip * C + C - 1)

    def answer(r, d):
        for dt in range(T):
            for dc in range(C):
                signal(insem.at[min(dt, 1), d])((g, r, lax.rem(t + dt, T), lax.rem(c + dc, C)))

    rows_apart(-1, answer)
    beside(-1, signal(insem.at[0, 0]))

    loads = [
        pltpu.make_async_copy(src, dst, wsem.at[i])
        for i, (src, dst) in enumerate(
            [(wk_hbm, wk), (wq_hbm, wq), (wv_hbm, wv), (wo_hbm, wo), (wc_hbm, wc)]
        )
    ]
    pl.when(attends)(lambda: [load.start() for load in loads[:4]] and None)
    loads[4].start()

    for load in first:
        load.wait()
    sums, squares = channel_sums(x[...].reshape(C * W, half).astype(F32))
    stat1_src[0:1] = sums
    stat1_src[1:2] = squares
    stat1[me] = stat1_src[...]
    xall[h * C + c] = x[c, 0]

    def send_stat(where):
        pltpu.make_async_remote_copy(
            src_ref=stat1_src, dst_ref=stat1.at[me], send_sem=s1send.at[where[1]], recv_sem=s1sem,
            device_id=where, device_id_type=MESH,
        ).start()

    def send_x(r, dc):
        frame = lax.rem(c + dc, C)
        pltpu.make_async_remote_copy(
            src_ref=x.at[frame, 0], dst_ref=xall.at[h * C + c], send_sem=xsend.at[r], recv_sem=xsem.at[h * C + c],
            device_id=(g, r, t, frame), device_id_type=MESH,
        ).start()

    def column_x(r):
        for dc in range(C):
            send_x(r, dc)

    rows_apart(-1, lambda r, d: row_devices(r, send_stat))

    @pl.when(attends)
    def _():
        beside(-1, send_stat)
        mates(send_stat)
        for dc in range(1, C):
            send_x(h, dc)

    rows_apart(-1, lambda r, d: column_x(r))

    gains = [
        pltpu.make_async_remote_copy(
            src_ref=src, dst_ref=dst.at[c], send_sem=send_sem.at[1 + k], recv_sem=gsem.at[k],
            device_id=(g, h, t, other), device_id_type=MESH,
        )
        for k, (src, dst) in enumerate([(g1, gall1), (g2, gall2)])
    ]
    for copy in gains:
        copy.start()

    def wait_in(kind, d, count):
        if T > 1 or not kind:
            pl.semaphore_wait(insem.at[kind, d], count)

    def upward(r, d):
        @pl.when(r < S - 1)
        def _():
            wait_in(0, d, C)
            for dc in range(C):
                send_stat((g, r, t, lax.rem(c + dc, C)))
            column_x(r)
            wait_in(1, d, (T - 1) * C)
            for dt in range(1, T):
                for dc in range(C):
                    send_stat((g, r, lax.rem(t + dt, T), lax.rem(c + dc, C)))

    rows_apart(1, upward)

    @pl.when(t < T - 1)
    def _():
        pl.semaphore_wait(insem.at[0, 0], (T - 1 - t) * C)
        pl.when(attends)(lambda: beside(1, send_stat))


    def last_in(r, d):
        @pl.when(r == S - 1)
        def _():
            wait_in(0, d, C)
            wait_in(1, d, (T - 1) * C)

    rows_apart(1, last_in)

    for copy in gains:
        copy.wait()
    population = float(n * W * GROUP)
    frame_at = t * C + c

    def attend(R):
        drain(stat1.at[pl.ds(0, n - 1)], s1sem)
        totals = jnp.sum(stat1[...].reshape(S * T, C, 2, half), axis=0)
        mean1, scale1 = moments(jnp.concatenate([totals[k] for k in range(C)], axis=1), population)
        factor1 = scale1 * jnp.concatenate([gall1[k] for k in range(C)], axis=1)

        def row_tokens(r):
            pieces = []
            for k in range(C):
                lanes = slice(k * half, (k + 1) * half)
                value = xall[r * C + k].astype(F32)
                pieces.append(((value - mean1[:, lanes]) * factor1[:, lanes]).astype(BF16))
            return jnp.concatenate(pieces, axis=1)

        def project(weight, first, stop):
            rows = tokens[first:stop].reshape((stop - first) * W, D)
            return jnp.dot(rows, weight[...], preferred_element_type=F32).astype(BF16)

        for dc in range(1, C):
            slot = h * C + lax.rem(c + dc, C)
            drain(xall.at[slot], xsem.at[slot])
        if R == 2:
            for k in range(C):
                slot = (h + 1) * C + k
                drain(xall.at[slot], xsem.at[slot])
        for i in range(R):
            tokens[i] = row_tokens(h + i)
        for load in loads[:3]:
            load.wait()
        queries = project(wq, 0, R)
        for i in range(S - R):
            r = i + jnp.where(i >= h, R, 0)
            for k in range(C):
                drain(xall.at[r * C + k], xsem.at[r * C + k])
        for i in range(S - R):
            tokens[R + i] = row_tokens(i + jnp.where(i >= h, R, 0))
        keyed[...] = project(wk, 0, S)
        valued[...] = project(wv, 0, S)

        scores = lax.dot_general(
            queries, keyed[...], (((1,), (1,)), ((), ())), preferred_element_type=F32
        ) * (D ** (-0.5))
        weights = jnp.exp(scores - jnp.max(scores, axis=1, keepdims=True))
        mass = jnp.sum(weights, axis=1, keepdims=True)
        mixed = jnp.dot(weights.astype(BF16), valued[...], preferred_element_type=F32)
        mixed = (mixed / mass).astype(BF16)
        loads[3].wait()
        attended = jnp.dot(mixed, wo[...], preferred_element_type=F32).astype(BF16)

        source = jnp.concatenate(
            [jnp.concatenate([xall[(h + i) * C + k] for k in range(C)], axis=1) for i in range(R)], axis=0
        ).astype(F32)
        resid = (source - mean1) + attended.astype(F32)
        sums, squares = channel_sums(resid)
        for k in range(T):
            lanes = slice(k * Kc, (k + 1) * Kc)
            stat2_src[k, 0:1] = sums[:, lanes]
            stat2_src[k, 1:2] = squares[:, lanes]

        def send_stat2(where):
            pltpu.make_async_remote_copy(
                src_ref=stat2_src.at[where[2]], dst_ref=stat2.at[me], send_sem=send_sem.at[4], recv_sem=s2sem,
                device_id=where, device_id_type=MESH,
            ).start()

        rows_apart(-1, lambda r, d: row_devices(r, send_stat2))
        rows_apart(1, lambda r, d: row_devices(r, send_stat2))
        beside(-1, send_stat2)
        beside(1, send_stat2)
        mates(send_stat2)
        for i in range(R):
            for k in range(T):
                dsrc[i, k] = resid[i * W : (i + 1) * W, k * Kc : (k + 1) * Kc].astype(BF16)
            for k in range(C):
                att_src[i, k] = attended[i * W : (i + 1) * W, k * half : (k + 1) * half]

        def send_row(i, r, cores, sends, recv):
            for dt in range(T):
                for dc in cores:
                    if not (r is h and dt == 0 and dc == 0):
                        to = lax.rem(t + dt, T)
                        pltpu.make_async_remote_copy(
                            src_ref=dsrc.at[i, to], dst_ref=dall.at[h + i - r + 1, frame_at],
                            send_sem=sends, recv_sem=recv,
                            device_id=(g, r, to, lax.rem(c + dc, C)), device_id_type=MESH,
                        ).start()

        everyone = range(C)
        if R == 2:
            for i in range(2):
                send_row(i, h + 1, [0], dsend.at[i], last_sem.at[i, t])

        @pl.when(h > 0)
        def _():
            send_row(0, h - 1, everyone, dsend.at[2], dsem.at[2])

        if R == 1:
            send_row(0, h + 1, everyone, dsend.at[3], dsem.at[0])
        for i in range(R):
            send_row(i, h, everyone, dsend.at[4 + i], dsem.at[1 + i])
            dall[1 + i, frame_at] = dsrc[i, t]
        attended_copy(0, other, h, other).start()
        if R == 2:
            for k in range(C):
                attended_copy(1, k, h + 1, k).start()
        stat2[me] = stat2_src[t]
        att_out[c, 0] = att_src[0, c]

    def attended_copy(i, k, r, core):
        return pltpu.make_async_remote_copy(
            src_ref=att_src.at[i, k], dst_ref=att_in.at[c], send_sem=asend.at[i * C + k], recv_sem=asem.at[c],
            device_id=(g, r, t, core), device_id_type=MESH,
        )

    def attended_in(frame):
        drain(att_in.at[frame], asem.at[frame])
        att_out[frame, 0] = att_in[frame]

    pl.when(h < S - 2)(lambda: attend(1))
    pl.when(h == S - 2)(lambda: attend(2))
    act[0:2] = jnp.zeros((2,) + act.shape[1:], BF16)
    gain2 = jnp.concatenate([gall2[k] for k in range(C)], axis=1)

    def share(i, k):
        return [
            pltpu.make_async_remote_copy(
                src_ref=dall.at[i, k * C + c], dst_ref=dall.at[i, k * C + c],
                send_sem=share_sem.at[i, k], recv_sem=dsem.at[i],
                device_id=(g, h, t, lax.rem(c + dc, C)), device_id_type=MESH,
            )
            for dc in range(1, C)
        ]

    @pl.when(jnp.logical_not(attends))
    def _():
        for dt in range(T):
            k = lax.rem(t + dt, T)
            for i in range(2):
                drain(dall.at[i, k * C + c], last_sem.at[i, k])
                for copy in share(i, k):
                    copy.start()
        drain(stat2.at[pl.ds(0, n - T * C)], s2sem)

    @pl.when(attends)
    def _():
        drain(stat2.at[pl.ds(0, n - T * C - 1)], s2sem)


    def sliced(v):
        out = v[:, 0:Kc]
        for k in range(1, T):
            out = jnp.where(t == k, v[:, k * Kc : (k + 1) * Kc], out)
        return out

    mean2, scale2 = slice_moments(jnp.sum(stat2[0 : n - T * C], axis=0), population)
    factor2 = scale2 * sliced(gain2)
    column = lax.broadcasted_iota(jnp.int32, (W, Kc), 0)

    def activate(row):
        @pl.loop(0, NF, unroll=NF <= 4)
        def _(f):
            v = (dall[row, f].astype(F32) - mean2) * factor2
            a = v / (1.0 + jnp.exp(-v))
            left = jnp.where(column == 0, 0.0, pltpu.roll(a, 1, 0))
            right = jnp.where(column == W - 1, 0.0, pltpu.roll(a, W - 1, 0))
            for e, piece in enumerate((left, a, right)):
                k = row * 3 + e
                act[f + 2, :, k * Kc : (k + 1) * Kc] = piece.astype(BF16)

    skips = (3 * Kc) % LANES == 0

    def blank(row):
        act[2:, :, row * 3 * Kc : (row + 1) * 3 * Kc] = jnp.zeros((NF, W, 3 * Kc), BF16)

    @pl.when(attends)
    def _():
        drain(dall.at[1, pl.ds(0, NF - 1)], dsem.at[1])

    @pl.when(jnp.logical_not(attends))
    def _():
        for i in range(2):
            drain(dall.at[i, pl.ds(0, (C - 1) * T)], dsem.at[i])

    activate(1)

    @pl.when(h > 0)
    def _():
        pl.when(attends)(lambda: drain(dall.at[0], dsem.at[0]))
        activate(0)

    @pl.when(attends)
    def _():
        pl.when(h < S - 2)(lambda: drain(dall.at[2], dsem.at[2]))
        pl.when(h == S - 2)(lambda: drain(dall.at[2, pl.ds(0, NF - 1)], dsem.at[2]))
        activate(2)

    if not skips:
        pl.when(h == 0)(lambda: blank(0))
        pl.when(h == S - 1)(lambda: blank(2))

    loads[4].wait()
    wide = half // CHUNKS

    def product(to, a0, b0, b1, chunk):
        total = None
        taps = slice(b0 * 3 * Kc, b1 * 3 * Kc)
        for a in range(a0, 3):
            window = act[pl.ds(to * C + a, C), :, taps].reshape(C * W, (b1 - b0) * 3 * Kc)
            weight = wc[a, taps, chunk * wide : (chunk + 1) * wide]
            term = jnp.dot(window, weight, preferred_element_type=F32)
            total = term if total is None else total + term
        return total

    if not skips:
        edges = [(t >= 0, 0, 3)]
    elif S == 1:
        edges = [(t >= 0, 1, 2)]
    else:
        edges = [(h == 0, 1, 3), (h == S - 1, 0, 2), (inner, 0, 3)]

    def partial(to, store):
        for at_edge, b0, b1 in edges:
            for early, a0 in ((to == 0, max(0, 3 - C)), (to > 0, 0)):

                @pl.when(at_edge & early)
                def _():
                    for chunk in range(CHUNKS):
                        store(chunk, product(to, a0, b0, b1, chunk))

    def part_copy(dt, chunk):
        return pltpu.make_async_remote_copy(
            src_ref=part_src.at[dt - 1, chunk], dst_ref=part.at[dt - 1, chunk],
            send_sem=psend.at[dt - 1, chunk], recv_sem=psem.at[dt - 1, chunk],
            device_id=(g, h, lax.rem(t + dt, T), c), device_id_type=MESH,
        )

    for dt in range(1, T):

        def send_part(chunk, value):
            part_src[dt - 1, chunk] = value.astype(BF16)
            part_copy(dt, chunk).start()

        partial(lax.rem(t + dt, T), send_part)


    def keep(chunk, value):
        own_total[chunk] = value

    partial(t, keep)
    attended_in(other)
    pl.when(jnp.logical_not(attends))(lambda: attended_in(c))

    for r in range(S - 1):

        @pl.when(h != r)
        def _():
            drain(stat1.at[pl.ds(0, T * C)], s1send.at[r])
            drain(xall.at[pl.ds(0, C)], xsend.at[r])

        @pl.when(h == r)
        def _():
            drain(stat1.at[pl.ds(0, T * C - 1)], s1send.at[r])
            drain(xall.at[pl.ds(0, C - 1)], xsend.at[r])

    @pl.when(attends)
    def _():
        drain(stat2.at[pl.ds(0, n - 1)], send_sem.at[4])
        drain(dall.at[1, pl.ds(0, NF - 1)], dsend.at[4])
        drain(att_src.at[0, 0], asend.at[other])

    @pl.when(attends & (h > 0))
    def _():
        drain(dall.at[0], dsend.at[2])

    @pl.when(h < S - 2)
    def _():
        drain(dall.at[0], dsend.at[3])

    @pl.when(h == S - 2)
    def _():
        drain(dall.at[1, pl.ds(0, NF - 1)], dsend.at[5])
        for i in range(2):
            drain(dall.at[0, pl.ds(0, T)], dsend.at[i])
        for k in range(C):
            drain(att_src.at[1, k], asend.at[C + k])

    @pl.when(jnp.logical_not(attends))
    def _():
        for i in range(2):
            for k in range(T):
                drain(dall.at[0, pl.ds(0, C - 1)], share_sem.at[i, k])

    for chunk in range(CHUNKS):
        total = own_total[chunk]
        for dt in range(1, T):
            part_copy(dt, chunk).wait()
            total = total + part[dt - 1, chunk].astype(F32)
        conv_out[:, 0, :, chunk * wide : (chunk + 1) * wide] = total.reshape(C, W, wide).astype(BF16)


def slice_moments(totals, population):
    Kc = totals.shape[1]
    if Kc >= LANES:
        return moments(totals, population)
    padded = jnp.concatenate([totals] * (LANES // Kc), axis=1)
    mean, scale = moments(padded, population)
    return mean[:, :Kc], scale[:, :Kc]


def hand_over(att_in, conv_in, att_out, conv_out):
    att_out[...] = att_in[...]
    conv_out[...] = conv_in[...]


def on_device(S, T, C, x, g1, g2, wq, wk, wv, wo, wc):
    frames, rows, W, half = x.shape
    assert frames == C and rows == 1 and half * C == D
    Kc = wc.shape[3]
    assert Kc * T == D and S > 1
    n, NF = S * T * C, T * C
    wide = half // CHUNKS
    wc = wc.reshape(3, 9 * Kc, half)
    vmem = pl.BlockSpec(memory_space=pltpu.VMEM)
    hbm = pl.BlockSpec(memory_space=pl.ANY)
    out = jax.ShapeDtypeStruct(x.shape, BF16)
    dma = pltpu.SemaphoreType.DMA
    kept = pltpu.VMEM(x.shape, BF16)
    links = max(T - 1, 1)
    results = pl.pallas_call(
        functools.partial(kernel, S, T, C, W),
        out_shape=(kept, kept),
        in_specs=[hbm] * 8,
        out_specs=(vmem, vmem),
        scratch_shapes=[
            pltpu.VMEM(x.shape, BF16),
            *[pltpu.VMEM((D, D), BF16)] * 4,
            pltpu.VMEM(wc.shape, BF16),
            pltpu.VMEM((2, half), F32),
            pltpu.VMEM((n, 2, half), F32),
            pltpu.VMEM((T, 2, Kc), F32),
            pltpu.VMEM((n, 2, Kc), F32),
            pltpu.VMEM((C, 1, half), F32),
            pltpu.VMEM((C, 1, half), F32),
            pltpu.VMEM((S * C, W, half), BF16),
            pltpu.VMEM((S, W, D), BF16),
            pltpu.VMEM((S * W, D), BF16),
            pltpu.VMEM((S * W, D), BF16),
            pltpu.VMEM((2, C, W, half), BF16),
            pltpu.VMEM((C, W, half), BF16),
            pltpu.VMEM((2, T, W, Kc), BF16),
            pltpu.VMEM((3, NF, W, Kc), BF16),
            pltpu.VMEM((NF + 2, W, 9 * Kc), BF16),
            pltpu.VMEM((CHUNKS, C * W, wide), F32),
            pltpu.VMEM((links, CHUNKS, C * W, wide), BF16),
            pltpu.VMEM((links, CHUNKS, C * W, wide), BF16),
            dma((3,)),
            dma((5,)),
            pltpu.SemaphoreType.REGULAR((2, S)),
            dma((5,)),
            dma((2,)),
            dma((S,)),
            dma(()),
            dma((S,)),
            dma((S * C,)),
            dma(()),
            dma((2 * C,)),
            dma((C,)),
            dma((6,)),
            dma((3,)),
            dma((2, T)),
            dma((2, T)),
            dma((links, CHUNKS)),
            dma((links, CHUNKS)),
        ],
        compiler_params=pltpu.CompilerParams(collective_id=0, has_side_effects=True),
    )(x, g1.reshape(1, half), g2.reshape(1, half), wq, wk, wv, wo, wc)
    return pl.pallas_call(
        hand_over, out_shape=(out, out), in_specs=[vmem] * 2, out_specs=(vmem, vmem),
    )(*[pltpu.with_memory_space_constraint(r, pltpu.VMEM) for r in results])


def solution(mesh):
    S, T, C = mesh.shape["space"], mesh.shape["tm"], mesh.shape["chan"]
    placed = (
        P(("groups", "tm"), "space", None, "chan"),
        P("chan"),
        P("chan"),
        P(),
        P(),
        P(),
        P(),
        P(None, None, None, "tm", "chan"),
    )
    return jax.shard_map(
        functools.partial(on_device, S, T, C),
        mesh=mesh,
        in_specs=placed,
        out_specs=(
            P(("groups", "tm"), "space", None, "chan"),
            P(("groups", "tm"), "space", None, "chan"),
        ),
        check_vma=False,
    )
```

```python
import functools

import jax
import jax.numpy as jnp
from jax import lax
from jax.experimental import pallas as pl
from jax.experimental.pallas import tpu as pltpu
from jax.sharding import PartitionSpec as P

D = 512
NGROUP = 32
EPSILON = 1e-06
LANES = 128
CHUNKS = 2
GROUP = D // NGROUP
MESH = pl.DeviceIdType.MESH
F32 = jnp.float32
BF16 = jnp.bfloat16


def group_total(v):
    lane = lax.broadcasted_iota(jnp.int32, v.shape, 1)
    width = v.shape[1]
    step = 1
    while step < GROUP:
        above = pltpu.roll(v, width - step, 1)
        below = pltpu.roll(v, step, 1)
        v = v + jnp.where((lane // step) % 2 == 0, above, below)
        step *= 2
    return v


def channel_sums(values):
    return jnp.sum(values, axis=0, keepdims=True), jnp.sum(values * values, axis=0, keepdims=True)


def moments(totals, population):
    blocks = totals.shape[1] // LANES
    pieces = [totals[k : k + 1, b * LANES : (b + 1) * LANES] for k in range(2) for b in range(blocks)]
    rows = 8 * pl.cdiv(2 * blocks, 8)
    grouped = group_total(jnp.concatenate(pieces + pieces[:1] * (rows - 2 * blocks), axis=0)) / population
    mean = jnp.concatenate([grouped[b : b + 1] for b in range(blocks)], axis=1)
    square = jnp.concatenate([grouped[blocks + b : blocks + b + 1] for b in range(blocks)], axis=1)
    variance = jnp.maximum(square - mean * mean, 0.0)
    return mean, lax.rsqrt(variance + EPSILON)


def kernel(
    S, T, C, W,
    x_hbm, g1, g2, wq_hbm, wk_hbm, wv_hbm, wo_hbm, wc_hbm,
    att_out, conv_out,
    x, wq, wk, wv, wo, wc,
    stat1_src, row_sum, raw, last, stat1, tally, stat2_src, stat2, gall1, gall2,
    xall, tokens, keyed, valued, att_src, att_in, dsrc, dall, act, own_total, part_src, part,
    xload, wsem, insem, send_sem, gsem, raw_send, raw_sem, s1send, s1sem, xsend, xsem, s2sem,
    asend, asem, dsend, dsem, outer_sem, share_sem, psend, psem,
):
    g = lax.axis_index("groups")
    h = lax.axis_index("space")
    t = lax.axis_index("tm")
    c = lax.axis_index("chan")
    attending = (S - 2) * T * C
    me = (h * T + t) * C + c - T * C
    half = D // C
    Kc = D // T
    NF = T * C
    other = lax.rem(c + 1, C)
    attends = (h > 0) & (h < S - 1)
    at_edge = (h == 1) | (h == S - 2)
    side = jnp.where(h == 1, -1, 1)

    def rows_apart(sign, act_on):
        def row(d):
            @pl.when((h + sign * d >= 0) & (h + sign * d < S))
            def _():
                act_on(h + sign * d, d)

        pl.loop(1, S, unroll=S <= 4)(row)

    def row_devices(r, act_on):
        for dt in range(T):
            for dc in range(C):
                act_on((g, r, lax.rem(t + dt, T), lax.rem(c + dc, C)))

    def column(r, act_on):
        for dc in range(C):
            act_on((g, r, t, lax.rem(c + dc, C)))

    def beside(sign, cores, act_on):
        for dt in range(1, T):

            @pl.when((t + sign * dt >= 0) & (t + sign * dt < T))
            def _():
                for dc in cores:
                    act_on((g, h, t + sign * dt, lax.rem(c + dc, C)))

    def mates(act_on):
        for dc in range(1, C):
            act_on((g, h, t, lax.rem(c + dc, C)))

    def signal(sem):
        return lambda where: pl.semaphore_signal(sem, inc=1, device_id=where, device_id_type=MESH)

    def drain(ref, sem):
        pltpu.make_async_copy(ref, ref, sem).wait()

    def send(src, dst, sends, recvs, where):
        copy = pltpu.make_async_remote_copy(
            src_ref=src, dst_ref=dst, send_sem=sends, recv_sem=recvs, device_id=where, device_id_type=MESH,
        )
        copy.start()

    everyone = range(C)
    first = [
        pltpu.make_async_copy(src, dst, xload.at[i])
        for i, (src, dst) in enumerate([(x_hbm, x), (g1, gall1.at[c]), (g2, gall2.at[c])])
    ]
    for load in first:
        load.start()
    barrier = pltpu.get_barrier_semaphore()
    mates(signal(barrier))
    pl.when(h < S - 1)(lambda: beside(1, [0], signal(barrier)))

    def announce(r, d):
        @pl.when(r == S - 1)
        def _():
            row_devices(r, signal(barrier))

        @pl.when(r < S - 1)
        def _():
            column(r, signal(barrier))

    rows_apart(1, announce)
    pl.semaphore_wait(barrier, jnp.where(h == S - 1, (S - 1) * T * C, h * C + t) + C - 1)

    @pl.when(h < S - 1)
    def _():
        rows_apart(-1, lambda r, d: column(r, signal(insem.at[d])))
        beside(-1, [0], signal(insem.at[0]))

    loads = [
        pltpu.make_async_copy(src, dst, wsem.at[i])
        for i, (src, dst) in enumerate(
            [(wk_hbm, wk), (wq_hbm, wq), (wv_hbm, wv), (wo_hbm, wo), (wc_hbm, wc)]
        )
    ]

    @pl.when(attends)
    def _():
        for load in loads[:4]:
            load.start()

    loads[4].start()

    for load in first:
        load.wait()
    sums, squares = channel_sums(x[...].reshape(C * W, half).astype(F32))
    stat1_src[0:1] = sums
    stat1_src[1:2] = squares

    def send_x(r, dc):
        frame = lax.rem(c + dc, C)
        slot = h * C + c
        send(x.at[frame, 0], xall.at[slot], xsend.at[r], xsem.at[slot], (g, r, t, frame))

    def column_x(r):
        for dc in range(C):
            send_x(r, dc)

    def send_raw(where):
        send(stat1_src, raw.at[t], raw_send, raw_sem.at[t], where)

    @pl.when(h == S - 1)
    def _():
        for r in range(1, S - 1):
            row_devices(r, lambda where: send(stat1_src, last.at[t, c], s1send.at[r], s1sem, where))

    pl.when(h < S - 1)(lambda: beside(-1, [0], send_raw))

    @pl.when(attends)
    def _():
        xall[h * C + c] = x[c, 0]
        for dc in range(1, C):
            send_x(h, dc)

    for r in range(1, S - 1):
        pl.when(r < h)(lambda: column_x(r))

    gains = [
        pltpu.make_async_remote_copy(
            src_ref=src, dst_ref=dst.at[c], send_sem=send_sem.at[1 + k], recv_sem=gsem.at[k],
            device_id=(g, h, t, other), device_id_type=MESH,
        )
        for k, (src, dst) in enumerate([(g1, gall1), (g2, gall2)])
    ]
    for copy in gains:
        copy.start()

    @pl.when(h < S - 2)
    def _():
        pl.semaphore_wait(insem.at[1], C)
        column_x(h + 1)

    @pl.when(h < S - 1)
    def _():
        @pl.when(t < T - 1)
        def _():
            pl.semaphore_wait(insem.at[0], T - 1 - t)
            beside(1, [0], send_raw)

        total = stat1_src[...]
        for dt in range(1, T):
            k = lax.rem(t + dt, T)
            drain(raw.at[k], raw_sem.at[k])
            total = total + raw[k]
        row_sum[...] = total


    def send_sum(where):
        send(row_sum, stat1.at[h, c], s1send.at[where[1]], s1sem, where)

    @pl.when(attends)
    def _():
        stat1[h, c] = row_sum[...]
        mates(send_sum)
        for r in range(1, S - 1):
            pl.when(r < h)(lambda: column(r, send_sum))

    pl.when(h < S - 2)(lambda: column(h + 1, send_sum))

    def upward(d):
        @pl.when(h + d < S - 1)
        def _():
            pl.semaphore_wait(insem.at[d], C)
            column(h + d, send_sum)
            column_x(h + d)

    pl.loop(2, S - 1, unroll=S <= 4)(upward)
    for copy in gains:
        copy.wait()
    population = float(S * T * C * W * GROUP)
    frame_at = t * C + c

    def attended_copy(i, k, r, core):
        return pltpu.make_async_remote_copy(
            src_ref=att_src.at[i, k], dst_ref=att_in.at[c], send_sem=asend.at[i * C + k], recv_sem=asem.at[c],
            device_id=(g, r, t, core), device_id_type=MESH,
        )

    def attend(R):
        outer = h + side
        mine = [h, outer][:R]
        skipped = jnp.where(h == 1, R, 0) if R == 2 else None

        def rest(i):
            return i + skipped if R == 2 else i + jnp.where(i >= h, 1, 0)

        drain(tally, s1sem)
        totals = jnp.sum(stat1[0 : S - 1], axis=0) + jnp.sum(last[...], axis=0)
        mean1, scale1 = moments(jnp.concatenate([totals[k] for k in range(C)], axis=1), population)
        factor1 = scale1 * jnp.concatenate([gall1[k] for k in range(C)], axis=1)

        def row_tokens(r):
            pieces = []
            for k in range(C):
                lanes = slice(k * half, (k + 1) * half)
                value = xall[r * C + k].astype(F32)
                pieces.append(((value - mean1[:, lanes]) * factor1[:, lanes]).astype(BF16))
            return jnp.concatenate(pieces, axis=1)

        def project(weight, first, stop):
            rows = tokens[first:stop].reshape((stop - first) * W, D)
            return jnp.dot(rows, weight[...], preferred_element_type=F32).astype(BF16)

        def slots_in(r):
            for k in range(C):
                drain(xall.at[r * C + k], xsem.at[r * C + k])

        for dc in range(1, C):
            slot = h * C + lax.rem(c + dc, C)
            drain(xall.at[slot], xsem.at[slot])
        if R == 2:
            slots_in(outer)
        for i in range(R):
            tokens[i] = row_tokens(mine[i])
        for load in loads[:3]:
            load.wait()
        queries = project(wq, 0, R)
        for i in range(S - R):
            slots_in(rest(i))
        for i in range(S - R):
            tokens[R + i] = row_tokens(rest(i))
        keyed[...] = project(wk, 0, S)
        valued[...] = project(wv, 0, S)

        scores = lax.dot_general(
            queries, keyed[...], (((1,), (1,)), ((), ())), preferred_element_type=F32
        ) * (D ** (-0.5))
        weights = jnp.exp(scores - jnp.max(scores, axis=1, keepdims=True))
        mass = jnp.sum(weights, axis=1, keepdims=True)
        mixed = jnp.dot(weights.astype(BF16), valued[...], preferred_element_type=F32)
        mixed = (mixed / mass).astype(BF16)
        loads[3].wait()
        attended = jnp.dot(mixed, wo[...], preferred_element_type=F32).astype(BF16)

        source = jnp.concatenate(
            [jnp.concatenate([xall[r * C + k] for k in range(C)], axis=1) for r in mine], axis=0
        ).astype(F32)
        resid = (source - mean1) + attended.astype(F32)
        sums, squares = channel_sums(resid)
        for k in range(T):
            lanes = slice(k * Kc, (k + 1) * Kc)
            stat2_src[k, 0:1] = sums[:, lanes]
            stat2_src[k, 1:2] = squares[:, lanes]

        def send_stat2(where):
            send(stat2_src.at[where[2]], stat2.at[me], send_sem.at[4], s2sem, where)

        rows_apart(-1, lambda r, d: row_devices(r, send_stat2))
        rows_apart(1, lambda r, d: row_devices(r, send_stat2))
        beside(-1, everyone, send_stat2)
        beside(1, everyone, send_stat2)
        mates(send_stat2)
        for i in range(R):
            for k in range(T):
                dsrc[i, k] = resid[i * W : (i + 1) * W, k * Kc : (k + 1) * Kc].astype(BF16)
            for k in range(C):
                att_src[i, k] = attended[i * W : (i + 1) * W, k * half : (k + 1) * half]

        def send_row(i, r, cores, sends, recv, skip_self=False):
            for dt in range(T):
                for dc in cores:
                    if not (skip_self and dt == 0 and dc == 0):
                        to = lax.rem(t + dt, T)
                        send(
                            dsrc.at[i, to], dall.at[mine[i] - r + 1, frame_at], sends, recv,
                            (g, r, to, lax.rem(c + dc, C)),
                        )

        if R == 2:
            for i in range(2):
                send_row(i, outer, [0], dsend.at[i], outer_sem.at[i, t])
            send_row(0, h - side, everyone, dsend.at[2], dsem.at[1 + side])
        else:
            send_row(0, h - 1, everyone, dsend.at[2], dsem.at[2])
            send_row(0, h + 1, everyone, dsend.at[3], dsem.at[0])
        for i in range(R):
            send_row(i, h, everyone, dsend.at[4 + i], dsem.at[mine[i] - h + 1], skip_self=True)
            dall[mine[i] - h + 1, frame_at] = dsrc[i, t]
        attended_copy(0, other, h, other).start()
        if R == 2:
            for k in range(C):
                attended_copy(1, k, outer, k).start()
        stat2[me] = stat2_src[t]
        att_out[c, 0] = att_src[0, c]

    def attended_in(frame):
        drain(att_in.at[frame], asem.at[frame])
        att_out[frame, 0] = att_in[frame]

    if S > 4:
        pl.when(attends & jnp.logical_not(at_edge))(lambda: attend(1))
    pl.when(at_edge)(lambda: attend(2))
    act[0:2] = jnp.zeros((2,) + act.shape[1:], BF16)
    gain2 = jnp.concatenate([gall2[k] for k in range(C)], axis=1)

    def share(i, k):
        return [
            pltpu.make_async_remote_copy(
                src_ref=dall.at[i, k * C + c], dst_ref=dall.at[i, k * C + c],
                send_sem=share_sem.at[i, k], recv_sem=dsem.at[i],
                device_id=(g, h, t, lax.rem(c + dc, C)), device_id_type=MESH,
            )
            for dc in range(1, C)
        ]

    beyond = jnp.where(h == 0, 1, 0)

    @pl.when(jnp.logical_not(attends))
    def _():
        for dt in range(T):
            k = lax.rem(t + dt, T)
            for i in range(2):
                row = beyond + i
                drain(dall.at[row, k * C + c], outer_sem.at[jnp.where(h == 0, 1 - i, i), k])
                for copy in share(row, k):
                    copy.start()
        drain(stat2.at[pl.ds(0, attending)], s2sem)

    @pl.when(attends)
    def _():
        drain(stat2.at[pl.ds(0, attending - 1)], s2sem)


    def sliced(v):
        out = v[:, 0:Kc]
        for k in range(1, T):
            out = jnp.where(t == k, v[:, k * Kc : (k + 1) * Kc], out)
        return out

    mean2, scale2 = slice_moments(jnp.sum(stat2[0:attending], axis=0), population)
    factor2 = scale2 * sliced(gain2)
    column = lax.broadcasted_iota(jnp.int32, (W, Kc), 0)

    def activate(row):
        @pl.loop(0, NF, unroll=NF <= 4)
        def _(f):
            v = (dall[row, f].astype(F32) - mean2) * factor2
            a = v / (1.0 + jnp.exp(-v))
            left = jnp.where(column == 0, 0.0, pltpu.roll(a, 1, 0))
            right = jnp.where(column == W - 1, 0.0, pltpu.roll(a, W - 1, 0))
            for e, piece in enumerate((left, a, right)):
                k = row * 3 + e
                act[f + 2, :, k * Kc : (k + 1) * Kc] = piece.astype(BF16)

    skips = (3 * Kc) % LANES == 0

    def blank(row):
        act[2:, :, row * 3 * Kc : (row + 1) * 3 * Kc] = jnp.zeros((NF, W, 3 * Kc), BF16)

    @pl.when(attends)
    def _():
        drain(dall.at[1, pl.ds(0, NF - 1)], dsem.at[1])

    @pl.when(jnp.logical_not(attends))
    def _():
        drain(dall.at[1, pl.ds(0, (C - 1) * T)], dsem.at[1])

    activate(1)

    def neighbour(row, edge, outermost):
        @pl.when(edge)
        def _():
            drain(dall.at[row, pl.ds(0, NF - 1)], dsem.at[row])

        @pl.when(outermost)
        def _():
            drain(dall.at[row, pl.ds(0, (C - 1) * T)], dsem.at[row])

        @pl.when(jnp.logical_not(edge | outermost))
        def _():
            drain(dall.at[row], dsem.at[row])

        activate(row)

    pl.when(h > 0)(lambda: neighbour(0, h == 1, h == S - 1))
    pl.when(h < S - 1)(lambda: neighbour(2, h == S - 2, h == 0))

    if not skips:
        pl.when(h == 0)(lambda: blank(0))
        pl.when(h == S - 1)(lambda: blank(2))

    loads[4].wait()
    wide = half // CHUNKS

    def product(to, a0, b0, b1, chunk):
        total = None
        taps = slice(b0 * 3 * Kc, b1 * 3 * Kc)
        for a in range(a0, 3):
            window = act[pl.ds(to * C + a, C), :, taps].reshape(C * W, (b1 - b0) * 3 * Kc)
            weight = wc[a, taps, chunk * wide : (chunk + 1) * wide]
            term = jnp.dot(window, weight, preferred_element_type=F32)
            total = term if total is None else total + term
        return total

    if not skips:
        edges = [(t >= 0, 0, 3)]
    else:
        edges = [(h == 0, 1, 3), (h == S - 1, 0, 2), (attends, 0, 3)]

    def partial(to, store):
        for here, b0, b1 in edges:
            for early, a0 in ((to == 0, max(0, 3 - C)), (to > 0, 0)):

                @pl.when(here & early)
                def _():
                    for chunk in range(CHUNKS):
                        store(chunk, product(to, a0, b0, b1, chunk))

    def part_copy(dt, chunk):
        return pltpu.make_async_remote_copy(
            src_ref=part_src.at[dt - 1, chunk], dst_ref=part.at[dt - 1, chunk],
            send_sem=psend.at[dt - 1, chunk], recv_sem=psem.at[dt - 1, chunk],
            device_id=(g, h, lax.rem(t + dt, T), c), device_id_type=MESH,
        )

    for dt in range(1, T):

        def send_part(chunk, value):
            part_src[dt - 1, chunk] = value.astype(BF16)
            part_copy(dt, chunk).start()

        partial(lax.rem(t + dt, T), send_part)


    def keep(chunk, value):
        own_total[chunk] = value

    partial(t, keep)
    attended_in(other)
    pl.when(jnp.logical_not(attends))(lambda: attended_in(c))

    @pl.when(h < S - 1)
    def _():
        if T > 1:
            drain(raw.at[pl.ds(0, T - 1)], raw_send)

    for r in range(1, S - 1):

        @pl.when(h == S - 1)
        def _():
            drain(last.at[pl.ds(0, T)], s1send.at[r])
            drain(xall.at[pl.ds(0, C)], xsend.at[r])

        @pl.when((h < S - 1) & (h != r))
        def _():
            drain(stat1.at[0], s1send.at[r])
            drain(xall.at[pl.ds(0, C)], xsend.at[r])

        @pl.when(h == r)
        def _():
            drain(stat1.at[0, pl.ds(0, C - 1)], s1send.at[r])
            drain(xall.at[pl.ds(0, C - 1)], xsend.at[r])

    @pl.when(attends)
    def _():
        drain(stat2.at[pl.ds(0, S * T * C - 1)], send_sem.at[4])
        drain(dall.at[0], dsend.at[2])
        drain(dall.at[1, pl.ds(0, NF - 1)], dsend.at[4])
        drain(att_src.at[0, 0], asend.at[other])

    @pl.when(attends & jnp.logical_not(at_edge))
    def _():
        drain(dall.at[0], dsend.at[3])

    @pl.when(at_edge)
    def _():
        drain(dall.at[1, pl.ds(0, NF - 1)], dsend.at[5])
        for i in range(2):
            drain(dall.at[0, pl.ds(0, T)], dsend.at[i])
        for k in range(C):
            drain(att_src.at[1, k], asend.at[C + k])

    @pl.when(jnp.logical_not(attends))
    def _():
        for i in range(2):
            for k in range(T):
                drain(dall.at[0, pl.ds(0, C - 1)], share_sem.at[beyond + i, k])

    for chunk in range(CHUNKS):
        total = own_total[chunk]
        for dt in range(1, T):
            part_copy(dt, chunk).wait()
            total = total + part[dt - 1, chunk].astype(F32)
        conv_out[:, 0, :, chunk * wide : (chunk + 1) * wide] = total.reshape(C, W, wide).astype(BF16)


def slice_moments(totals, population):
    Kc = totals.shape[1]
    if Kc >= LANES:
        return moments(totals, population)
    padded = jnp.concatenate([totals] * (LANES // Kc), axis=1)
    mean, scale = moments(padded, population)
    return mean[:, :Kc], scale[:, :Kc]


def hand_over(att_in, conv_in, att_out, conv_out):
    att_out[...] = att_in[...]
    conv_out[...] = conv_in[...]


def on_device(S, T, C, x, g1, g2, wq, wk, wv, wo, wc):
    frames, rows, W, half = x.shape
    assert frames == C and rows == 1 and half * C == D
    Kc = wc.shape[3]
    assert Kc * T == D and S > 3
    n, NF = S * T * C, T * C
    wide = half // CHUNKS
    wc = wc.reshape(3, 9 * Kc, half)
    vmem = pl.BlockSpec(memory_space=pltpu.VMEM)
    hbm = pl.BlockSpec(memory_space=pl.ANY)
    out = jax.ShapeDtypeStruct(x.shape, BF16)
    dma = pltpu.SemaphoreType.DMA
    kept = pltpu.VMEM(x.shape, BF16)
    links = max(T - 1, 1)
    results = pl.pallas_call(
        functools.partial(kernel, S, T, C, W),
        out_shape=(kept, kept),
        in_specs=[hbm] * 8,
        out_specs=(vmem, vmem),
        scratch_shapes=[
            pltpu.VMEM(x.shape, BF16),
            *[pltpu.VMEM((D, D), BF16)] * 4,
            pltpu.VMEM(wc.shape, BF16),
            pltpu.VMEM((2, half), F32),
            pltpu.VMEM((2, half), F32),
            pltpu.VMEM((T, 2, half), F32),
            pltpu.VMEM((T, C, 2, half), F32),
            pltpu.VMEM((S - 1, C, 2, half), F32),
            pltpu.VMEM(((S - 1 + T) * C - 1, 2, half), F32),
            pltpu.VMEM((T, 2, Kc), F32),
            pltpu.VMEM((n, 2, Kc), F32),
            pltpu.VMEM((C, 1, half), F32),
            pltpu.VMEM((C, 1, half), F32),
            pltpu.VMEM((S * C, W, half), BF16),
            pltpu.VMEM((S, W, D), BF16),
            pltpu.VMEM((S * W, D), BF16),
            pltpu.VMEM((S * W, D), BF16),
            pltpu.VMEM((2, C, W, half), BF16),
            pltpu.VMEM((C, W, half), BF16),
            pltpu.VMEM((2, T, W, Kc), BF16),
            pltpu.VMEM((3, NF, W, Kc), BF16),
            pltpu.VMEM((NF + 2, W, 9 * Kc), BF16),
            pltpu.VMEM((CHUNKS, C * W, wide), F32),
            pltpu.VMEM((links, CHUNKS, C * W, wide), BF16),
            pltpu.VMEM((links, CHUNKS, C * W, wide), BF16),
            dma((3,)),
            dma((5,)),
            pltpu.SemaphoreType.REGULAR((S,)),
            dma((5,)),
            dma((2,)),
            dma(()),
            dma((T,)),
            dma((S,)),
            dma(()),
            dma((S,)),
            dma((S * C,)),
            dma(()),
            dma((2 * C,)),
            dma((C,)),
            dma((6,)),
            dma((3,)),
            dma((2, T)),
            dma((3, T)),
            dma((links, CHUNKS)),
            dma((links, CHUNKS)),
        ],
        compiler_params=pltpu.CompilerParams(collective_id=0, has_side_effects=True),
    )(x, g1.reshape(1, half), g2.reshape(1, half), wq, wk, wv, wo, wc)
    return pl.pallas_call(
        hand_over, out_shape=(out, out), in_specs=[vmem] * 2, out_specs=(vmem, vmem),
    )(*[pltpu.with_memory_space_constraint(r, pltpu.VMEM) for r in results])


def solution(mesh):
    S, T, C = mesh.shape["space"], mesh.shape["tm"], mesh.shape["chan"]
    placed = (
        P(("groups", "tm"), "space", None, "chan"),
        P("chan"),
        P("chan"),
        P(),
        P(),
        P(),
        P(),
        P(None, None, None, "tm", "chan"),
    )
    return jax.shard_map(
        functools.partial(on_device, S, T, C),
        mesh=mesh,
        in_specs=placed,
        out_specs=(
            P(("groups", "tm"), "space", None, "chan"),
            P(("groups", "tm"), "space", None, "chan"),
        ),
        check_vma=False,
    )
```

```python
import functools

import jax
import jax.numpy as jnp
from jax import lax
from jax.experimental import pallas as pl
from jax.experimental.pallas import tpu as pltpu
from jax.sharding import PartitionSpec as P

D = 512
NGROUP = 32
EPSILON = 1e-06
LANES = 128
CHUNKS = 2
GROUP = D // NGROUP
MESH = pl.DeviceIdType.MESH
F32 = jnp.float32
BF16 = jnp.bfloat16


def group_total(v):
    lane = lax.broadcasted_iota(jnp.int32, v.shape, 1)
    width = v.shape[1]
    step = 1
    while step < GROUP:
        above = pltpu.roll(v, width - step, 1)
        below = pltpu.roll(v, step, 1)
        v = v + jnp.where((lane // step) % 2 == 0, above, below)
        step *= 2
    return v


def channel_sums(values):
    return jnp.sum(values, axis=0, keepdims=True), jnp.sum(values * values, axis=0, keepdims=True)


def moments(totals, population):
    blocks = totals.shape[1] // LANES
    pieces = [totals[k : k + 1, b * LANES : (b + 1) * LANES] for k in range(2) for b in range(blocks)]
    rows = 8 * pl.cdiv(2 * blocks, 8)
    grouped = group_total(jnp.concatenate(pieces + pieces[:1] * (rows - 2 * blocks), axis=0)) / population
    mean = jnp.concatenate([grouped[b : b + 1] for b in range(blocks)], axis=1)
    square = jnp.concatenate([grouped[blocks + b : blocks + b + 1] for b in range(blocks)], axis=1)
    variance = jnp.maximum(square - mean * mean, 0.0)
    return mean, lax.rsqrt(variance + EPSILON)


def kernel(
    S, T, C, W,
    x_hbm, g1, g2, wq_hbm, wk_hbm, wv_hbm, wo_hbm, wc_hbm,
    att_out, conv_out,
    x, projections, wo, wc,
    stat1_src, stat1, stat2_src, stat2, gall,
    xall, tokens, keyed, valued, att_src, att_in, dsrc, dall, act, own_total, part_src, part,
    xload, wsem, insem, gsend, gsem, s1send, s1sem, xsend, xsem, s2send, s2sem,
    asend, asem, dsend, dsem, outer_sem, share_sem, psend, psem,
):
    g = lax.axis_index("groups")
    h = lax.axis_index("space")
    t = lax.axis_index("tm")
    c = lax.axis_index("chan")
    attending = (S - 2) * T * C
    me = (h * T + t) * C + c - T * C
    half = D // C
    Kc = D // T
    NF = T * C
    other = lax.rem(c + 1, C)
    attends = (h > 0) & (h < S - 1)
    at_edge = (h == 1) | (h == S - 2)
    side = jnp.where(h == 1, -1, 1)

    def rows_apart(sign, act_on):
        def row(d):
            @pl.when((h + sign * d >= 0) & (h + sign * d < S))
            def _():
                act_on(h + sign * d, d)

        pl.loop(1, S, unroll=S <= 4)(row)

    def row_devices(r, act_on):
        for dt in range(T):
            for dc in range(C):
                act_on((g, r, lax.rem(t + dt, T), lax.rem(c + dc, C)))

    def beside(sign, act_on):
        for dt in range(1, T):

            @pl.when((t + sign * dt >= 0) & (t + sign * dt < T))
            def _():
                for dc in range(C):
                    act_on((g, h, t + sign * dt, lax.rem(c + dc, C)))

    def mates(act_on):
        for dc in range(1, C):
            act_on((g, h, t, lax.rem(c + dc, C)))

    def signal(sem):
        return lambda where: pl.semaphore_signal(sem, inc=1, device_id=where, device_id_type=MESH)

    def drain(ref, sem):
        pltpu.make_async_copy(ref, ref, sem).wait()

    def send(src, dst, sends, recvs, where):
        copy = pltpu.make_async_remote_copy(
            src_ref=src, dst_ref=dst, send_sem=sends, recv_sem=recvs, device_id=where, device_id_type=MESH,
        )
        copy.start()

    everyone = range(C)
    x_load = pltpu.make_async_copy(x_hbm, x, xload.at[0])
    x_load.start()
    for k, gain in enumerate((g1, g2)):
        pltpu.make_async_copy(gain, gall.at[c, k], xload.at[1]).start()
    barrier = pltpu.get_barrier_semaphore()
    mates(signal(barrier))
    beside(1, signal(barrier))
    rows_apart(1, lambda r, d: row_devices(r, signal(barrier)))
    pl.semaphore_wait(barrier, (h * T + t) * C + C - 1)

    def answer(r, d):
        for dt in range(T):
            for dc in range(C):
                signal(insem.at[min(dt, 1), d])((g, r, lax.rem(t + dt, T), lax.rem(c + dc, C)))

    @pl.when(h < S - 1)
    def _():
        rows_apart(-1, answer)
        pl.when(h > 0)(lambda: beside(-1, signal(insem.at[0, 0])))

    loads = [
        pltpu.make_async_copy(src, dst, wsem.at[i])
        for i, (src, dst) in zip((0, 0, 0, 1, 2), [(wq_hbm, projections.at[0]), (wk_hbm, projections.at[1]), (wv_hbm, projections.at[2]), (wo_hbm, wo), (wc_hbm, wc)])
    ]

    @pl.when(attends)
    def _():
        for load in loads[:4]:
            load.start()

    loads[4].start()

    x_load.wait()
    sums, squares = channel_sums(x[...].reshape(C * W, half).astype(F32))
    stat1_src[0:1] = sums
    stat1_src[1:2] = squares
    at = (h * T + t) * C + c

    def send_stat(where):
        send(stat1_src, stat1.at[at], s1send, s1sem, where)

    def send_x(r, dc):
        frame = lax.rem(c + dc, C)
        send(x.at[frame, 0], xall.at[h * C + c], xsend, xsem.at[h], (g, r, t, frame))

    def column_x(r):
        for dc in range(C):
            send_x(r, dc)

    for r in range(1, S - 1):
        pl.when(r < h)(lambda: row_devices(r, send_stat))

    @pl.when(attends)
    def _():
        stat1[at] = stat1_src[...]
        beside(-1, send_stat)
        mates(send_stat)
        xall[h * C + c] = x[c, 0]
        for dc in range(1, C):
            send_x(h, dc)

    for r in range(1, S - 1):
        pl.when(r < h)(lambda: column_x(r))

    drain(gall.at[c], xload.at[1])
    mates(lambda where: send(gall.at[c], gall.at[c], gsend, gsem, where))

    def upward(r, d):
        @pl.when(r < S - 1)
        def _():
            pl.semaphore_wait(insem.at[0, d], C)
            for dc in range(C):
                send_stat((g, r, t, lax.rem(c + dc, C)))
            column_x(r)
            if T > 1:
                pl.semaphore_wait(insem.at[1, d], (T - 1) * C)
            for dt in range(1, T):
                for dc in range(C):
                    send_stat((g, r, lax.rem(t + dt, T), lax.rem(c + dc, C)))

    @pl.when(attends & (t < T - 1))
    def _():
        pl.semaphore_wait(insem.at[0, 0], (T - 1 - t) * C)
        beside(1, send_stat)

    rows_apart(1, upward)
    drain(gall.at[pl.ds(0, C - 1)], gsem)
    population = float(S * T * C * W * GROUP)
    frame_at = t * C + c

    def send_attended(i, k, r, core):
        send(att_src.at[i, k], att_in.at[c], asend, asem, (g, r, t, core))

    def attend(R):
        outer = h + side
        mine = [h, outer][:R]
        skipped = jnp.where(h == 1, R, 0) if R == 2 else None

        def rest(i):
            return i + skipped if R == 2 else i + jnp.where(i >= h, 1, 0)

        drain(stat1.at[pl.ds(0, S * T * C - 1)], s1sem)
        totals = jnp.sum(stat1[...].reshape(S * T, C, 2, half), axis=0)
        mean1, scale1 = moments(jnp.concatenate([totals[k] for k in range(C)], axis=1), population)
        factor1 = scale1 * jnp.concatenate([gall[k, 0] for k in range(C)], axis=1)

        def row_tokens(r):
            pieces = []
            for k in range(C):
                lanes = slice(k * half, (k + 1) * half)
                value = xall[r * C + k].astype(F32)
                pieces.append(((value - mean1[:, lanes]) * factor1[:, lanes]).astype(BF16))
            return jnp.concatenate(pieces, axis=1)

        def project(weight, first, stop):
            rows = tokens[first:stop].reshape((stop - first) * W, D)
            return jnp.dot(rows, weight[...], preferred_element_type=F32).astype(BF16)

        def slots_in(r):
            drain(xall.at[pl.ds(r * C, C)], xsem.at[r])

        drain(xall.at[pl.ds(0, C - 1)], xsem.at[h])
        if R == 2:
            slots_in(outer)
        for i in range(R):
            tokens[i] = row_tokens(mine[i])
        drain(projections, wsem.at[0])
        queries = project(projections.at[0], 0, R)
        for i in range(S - R):
            slots_in(rest(i))
        for i in range(S - R):
            tokens[R + i] = row_tokens(rest(i))
        keyed[...] = project(projections.at[1], 0, S)
        valued[...] = project(projections.at[2], 0, S)

        scores = lax.dot_general(
            queries, keyed[...], (((1,), (1,)), ((), ())), preferred_element_type=F32
        ) * (D ** (-0.5))
        weights = jnp.exp(scores - jnp.max(scores, axis=1, keepdims=True))
        mass = jnp.sum(weights, axis=1, keepdims=True)
        mixed = jnp.dot(weights.astype(BF16), valued[...], preferred_element_type=F32)
        mixed = (mixed / mass).astype(BF16)
        loads[3].wait()
        attended = jnp.dot(mixed, wo[...], preferred_element_type=F32).astype(BF16)

        source = jnp.concatenate(
            [jnp.concatenate([xall[r * C + k] for k in range(C)], axis=1) for r in mine], axis=0
        ).astype(F32)
        resid = (source - mean1) + attended.astype(F32)
        for i in range(R):
            for k in range(T):
                dsrc[i, k] = resid[i * W : (i + 1) * W, k * Kc : (k + 1) * Kc].astype(BF16)

        def send_row(i, r, cores, sends, recv, skip_self=False):
            for dt in range(T):
                for dc in cores:
                    if not (skip_self and dt == 0 and dc == 0):
                        to = lax.rem(t + dt, T)
                        send(
                            dsrc.at[i, to], dall.at[(mine[i] - r + 1) * NF + frame_at], sends, recv,
                            (g, r, to, lax.rem(c + dc, C)),
                        )

        if R == 2:
            for i in range(2):
                send_row(i, outer, [0], dsend.at[0], outer_sem.at[i, t])
        sums, squares = channel_sums(resid)
        for k in range(T):
            lanes = slice(k * Kc, (k + 1) * Kc)
            stat2_src[k, 0:1] = sums[:, lanes]
            stat2_src[k, 1:2] = squares[:, lanes]

        def send_stat2(where):
            send(stat2_src.at[where[2]], stat2.at[me], s2send, s2sem, where)

        rows_apart(-1, lambda r, d: row_devices(r, send_stat2))
        rows_apart(1, lambda r, d: row_devices(r, send_stat2))
        beside(-1, send_stat2)
        beside(1, send_stat2)
        mates(send_stat2)
        if R == 2:
            send_row(0, h - side, everyone, dsend.at[1], dsem.at[1 + side])
        else:
            send_row(0, h - 1, everyone, dsend.at[1], dsem.at[2])
            send_row(0, h + 1, everyone, dsend.at[1], dsem.at[0])
        for i in range(R):
            row = mine[i] - h + 1
            send_row(i, h, everyone, dsend.at[1], dsem.at[row], skip_self=True)
            dall[row * NF + frame_at] = dsrc[i, t]
        for i in range(R):
            for k in range(C):
                att_src[i, k] = attended[i * W : (i + 1) * W, k * half : (k + 1) * half]
        send_attended(0, other, h, other)
        if R == 2:
            for k in range(C):
                send_attended(1, k, outer, k)
        stat2[me] = stat2_src[t]
        att_out[c, 0] = att_src[0, c]

    if S > 4:
        pl.when(attends & jnp.logical_not(at_edge))(lambda: attend(1))
    pl.when(at_edge)(lambda: attend(2))
    act[0:2] = jnp.zeros((2,) + act.shape[1:], BF16)
    gain2 = jnp.concatenate([gall[k, 1] for k in range(C)], axis=1)

    beyond = jnp.where(h == 0, 1, 0)

    @pl.when(jnp.logical_not(attends))
    def _():
        for dt in range(T):
            k = lax.rem(t + dt, T)
            for i in range(2):
                row = beyond + i
                slot = row * NF + k * C + c
                drain(dall.at[slot], outer_sem.at[jnp.where(h == 0, 1 - i, i), k])
                mates(lambda where: send(dall.at[slot], dall.at[slot], share_sem, dsem.at[row], where))
        drain(stat2.at[pl.ds(0, attending)], s2sem)

    @pl.when(attends)
    def _():
        drain(stat2.at[pl.ds(0, attending - 1)], s2sem)


    def sliced(v):
        out = v[:, 0:Kc]
        for k in range(1, T):
            out = jnp.where(t == k, v[:, k * Kc : (k + 1) * Kc], out)
        return out

    mean2, scale2 = slice_moments(jnp.sum(stat2[0:attending], axis=0), population)
    factor2 = scale2 * sliced(gain2)
    column = lax.broadcasted_iota(jnp.int32, (W, Kc), 0)

    def activate(row):
        @pl.loop(0, NF, unroll=NF <= 4)
        def _(f):
            v = (dall[row * NF + f].astype(F32) - mean2) * factor2
            a = v / (1.0 + jnp.exp(-v))
            left = jnp.where(column == 0, 0.0, pltpu.roll(a, 1, 0))
            right = jnp.where(column == W - 1, 0.0, pltpu.roll(a, W - 1, 0))
            for e, piece in enumerate((left, a, right)):
                k = row * 3 + e
                act[f + 2, :, k * Kc : (k + 1) * Kc] = piece.astype(BF16)

    skips = (3 * Kc) % LANES == 0

    def blank(row):
        act[2:, :, row * 3 * Kc : (row + 1) * 3 * Kc] = jnp.zeros((NF, W, 3 * Kc), BF16)

    @pl.when(attends)
    def _():
        drain(dall.at[pl.ds(0, NF - 1)], dsem.at[1])

    @pl.when(jnp.logical_not(attends))
    def _():
        drain(dall.at[pl.ds(0, (C - 1) * T)], dsem.at[1])

    activate(1)

    def neighbour(row, edge, outermost):
        @pl.when(edge)
        def _():
            drain(dall.at[pl.ds(0, NF - 1)], dsem.at[row])

        @pl.when(outermost)
        def _():
            drain(dall.at[pl.ds(0, (C - 1) * T)], dsem.at[row])

        @pl.when(jnp.logical_not(edge | outermost))
        def _():
            drain(dall.at[pl.ds(0, NF)], dsem.at[row])

        activate(row)

    pl.when(h > 0)(lambda: neighbour(0, h == 1, h == S - 1))
    pl.when(h < S - 1)(lambda: neighbour(2, h == S - 2, h == 0))

    if not skips:
        pl.when(h == 0)(lambda: blank(0))
        pl.when(h == S - 1)(lambda: blank(2))

    loads[4].wait()
    wide = half // CHUNKS

    def product(to, a0, b0, b1, chunk):
        total = None
        taps = slice(b0 * 3 * Kc, b1 * 3 * Kc)
        for a in range(a0, 3):
            window = act[pl.ds(to * C + a, C), :, taps].reshape(C * W, (b1 - b0) * 3 * Kc)
            weight = wc[a, taps, chunk * wide : (chunk + 1) * wide]
            term = jnp.dot(window, weight, preferred_element_type=F32)
            total = term if total is None else total + term
        return total

    if not skips:
        edges = [(t >= 0, 0, 3)]
    else:
        edges = [(h == 0, 1, 3), (h == S - 1, 0, 2), (attends, 0, 3)]

    def partial(to, store):
        for here, b0, b1 in edges:
            for early, a0 in ((to == 0, max(0, 3 - C)), (to > 0, 0)):

                @pl.when(here & early)
                def _():
                    for chunk in range(CHUNKS):
                        store(chunk, product(to, a0, b0, b1, chunk))

    for dt in range(1, T):

        def send_part(chunk, value):
            part_src[dt - 1, chunk] = value.astype(BF16)
            send(
                part_src.at[dt - 1, chunk], part.at[dt - 1, chunk], psend, psem.at[dt - 1, chunk],
                (g, h, lax.rem(t + dt, T), c),
            )

        partial(lax.rem(t + dt, T), send_part)


    def keep(chunk, value):
        own_total[chunk] = value

    partial(t, keep)
    @pl.when(attends)
    def _():
        drain(att_in.at[pl.ds(0, C - 1)], asem)
        att_out[other, 0] = att_in[other]
        drain(stat1.at[pl.ds(0, attending - 1)], s1send)
        drain(xall.at[pl.ds(0, (S - 2) * C - 1)], xsend)
        drain(stat2.at[pl.ds(0, S * T * C - 1)], s2send)

    @pl.when(jnp.logical_not(attends))
    def _():
        drain(att_in, asem)
        for k in range(C):
            att_out[k, 0] = att_in[k]
        drain(stat1.at[pl.ds(0, attending)], s1send)
        drain(xall.at[pl.ds(0, (S - 2) * C)], xsend)
        drain(dall.at[pl.ds(0, 2 * T * (C - 1))], share_sem)

    @pl.when(attends & jnp.logical_not(at_edge))
    def _():
        drain(dall.at[pl.ds(0, 3 * NF - 1)], dsend.at[1])
        drain(att_src.at[0, 0], asend)

    @pl.when(at_edge)
    def _():
        drain(dall.at[pl.ds(0, 2 * T)], dsend.at[0])
        drain(dall.at[pl.ds(0, 3 * NF - 2)], dsend.at[1])
        drain(xall.at[pl.ds(0, C + 1)], asend)

    drain(gall.at[pl.ds(0, C - 1)], gsend)
    for chunk in range(CHUNKS):
        total = own_total[chunk]
        for dt in range(1, T):
            drain(part.at[dt - 1, chunk], psem.at[dt - 1, chunk])
            total = total + part[dt - 1, chunk].astype(F32)
        conv_out[:, 0, :, chunk * wide : (chunk + 1) * wide] = total.reshape(C, W, wide).astype(BF16)
    if T > 1:
        drain(part_src, psend)


def slice_moments(totals, population):
    Kc = totals.shape[1]
    if Kc >= LANES:
        return moments(totals, population)
    padded = jnp.concatenate([totals] * (LANES // Kc), axis=1)
    mean, scale = moments(padded, population)
    return mean[:, :Kc], scale[:, :Kc]


def hand_over(att_in, conv_in, att_out, conv_out):
    att_out[...] = att_in[...]
    conv_out[...] = conv_in[...]


def on_device(S, T, C, x, g1, g2, wq, wk, wv, wo, wc):
    frames, rows, W, half = x.shape
    assert frames == C and rows == 1 and half * C == D
    Kc = wc.shape[3]
    assert Kc * T == D and S > 3
    n, NF = S * T * C, T * C
    wide = half // CHUNKS
    wc = wc.reshape(3, 9 * Kc, half)
    vmem = pl.BlockSpec(memory_space=pltpu.VMEM)
    hbm = pl.BlockSpec(memory_space=pl.ANY)
    out = jax.ShapeDtypeStruct(x.shape, BF16)
    dma = pltpu.SemaphoreType.DMA
    kept = pltpu.VMEM(x.shape, BF16)
    links = max(T - 1, 1)
    results = pl.pallas_call(
        functools.partial(kernel, S, T, C, W),
        out_shape=(kept, kept),
        in_specs=[hbm] * 8,
        out_specs=(vmem, vmem),
        scratch_shapes=[
            pltpu.VMEM(x.shape, BF16),
            pltpu.VMEM((3, D, D), BF16),
            pltpu.VMEM((D, D), BF16),
            pltpu.VMEM(wc.shape, BF16),
            pltpu.VMEM((2, half), F32),
            pltpu.VMEM((n, 2, half), F32),
            pltpu.VMEM((T, 2, Kc), F32),
            pltpu.VMEM((n, 2, Kc), F32),
            pltpu.VMEM((C, 2, 1, half), F32),
            pltpu.VMEM((S * C, W, half), BF16),
            pltpu.VMEM((S, W, D), BF16),
            pltpu.VMEM((S * W, D), BF16),
            pltpu.VMEM((S * W, D), BF16),
            pltpu.VMEM((2, C, W, half), BF16),
            pltpu.VMEM((C, W, half), BF16),
            pltpu.VMEM((2, T, W, Kc), BF16),
            pltpu.VMEM((3 * NF, W, Kc), BF16),
            pltpu.VMEM((NF + 2, W, 9 * Kc), BF16),
            pltpu.VMEM((CHUNKS, C * W, wide), F32),
            pltpu.VMEM((links, CHUNKS, C * W, wide), BF16),
            pltpu.VMEM((links, CHUNKS, C * W, wide), BF16),
            dma((2,)),
            dma((3,)),
            pltpu.SemaphoreType.REGULAR((2, S - 1)),
            dma(()),
            dma(()),
            dma(()),
            dma(()),
            dma(()),
            dma((S,)),
            dma(()),
            dma(()),
            dma(()),
            dma(()),
            dma((2,)),
            dma((3,)),
            dma((2, T)),
            dma(()),
            dma(()),
            dma((links, CHUNKS)),
        ],
        compiler_params=pltpu.CompilerParams(collective_id=0, has_side_effects=True),
    )(x, g1.reshape(1, half), g2.reshape(1, half), wq, wk, wv, wo, wc)
    return pl.pallas_call(
        hand_over, out_shape=(out, out), in_specs=[vmem] * 2, out_specs=(vmem, vmem),
    )(*[pltpu.with_memory_space_constraint(r, pltpu.VMEM) for r in results])


def solution(mesh):
    S, T, C = mesh.shape["space"], mesh.shape["tm"], mesh.shape["chan"]
    placed = (
        P(("groups", "tm"), "space", None, "chan"),
        P("chan"),
        P("chan"),
        P(),
        P(),
        P(),
        P(),
        P(None, None, None, "tm", "chan"),
    )
    return jax.shard_map(
        functools.partial(on_device, S, T, C),
        mesh=mesh,
        in_specs=placed,
        out_specs=(
            P(("groups", "tm"), "space", None, "chan"),
            P(("groups", "tm"), "space", None, "chan"),
        ),
        check_vma=False,
    )
```

```python
import functools

import jax
import jax.numpy as jnp
from jax import lax
from jax.experimental import pallas as pl
from jax.experimental.pallas import tpu as pltpu
from jax.sharding import PartitionSpec as P

D = 512
NGROUP = 32
EPSILON = 1e-06
LANES = 128
CHUNKS = 2
GROUP = D // NGROUP
MESH = pl.DeviceIdType.MESH
F32 = jnp.float32
BF16 = jnp.bfloat16


def group_total(v):
    lane = lax.broadcasted_iota(jnp.int32, v.shape, 1)
    width = v.shape[1]
    step = 1
    while step < GROUP:
        above = pltpu.roll(v, width - step, 1)
        below = pltpu.roll(v, step, 1)
        v = v + jnp.where((lane // step) % 2 == 0, above, below)
        step *= 2
    return v


def channel_sums(values):
    return jnp.sum(values, axis=0, keepdims=True), jnp.sum(values * values, axis=0, keepdims=True)


def moments(totals, population):
    blocks = totals.shape[1] // LANES
    pieces = [totals[k : k + 1, b * LANES : (b + 1) * LANES] for k in range(2) for b in range(blocks)]
    rows = 8 * pl.cdiv(2 * blocks, 8)
    grouped = group_total(jnp.concatenate(pieces + pieces[:1] * (rows - 2 * blocks), axis=0)) / population
    mean = jnp.concatenate([grouped[b : b + 1] for b in range(blocks)], axis=1)
    square = jnp.concatenate([grouped[blocks + b : blocks + b + 1] for b in range(blocks)], axis=1)
    variance = jnp.maximum(square - mean * mean, 0.0)
    return mean, lax.rsqrt(variance + EPSILON)


def kernel(
    S, T, C, W,
    x_hbm, g1, g2, wq_hbm, wk_hbm, wv_hbm, wo_hbm, wc_hbm,
    att_out, conv_out,
    x, projections, wo, wc,
    stat1_src, stat1, stat2_src, stat2, gall,
    xall, tokens, keyed, valued, att_src, att_in, dsrc, dall, act, own_total, part_src, part,
    xload, wsem, insem, gsend, gsem, s1send, s1sem, xsend, xsem, s2send, s2sem,
    asend, asem, dsend, dsem, outer_sem, share_sem, psend, psem,
):
    g = lax.axis_index("groups")
    h = lax.axis_index("space")
    t = lax.axis_index("tm")
    c = lax.axis_index("chan")
    attending = (S - 2) * T * C
    me = (h * T + t) * C + c - T * C
    half = D // C
    Kc = D // T
    NF = T * C
    other = lax.rem(c + 1, C)
    attends = (h > 0) & (h < S - 1)
    at_edge = (h == 1) | (h == S - 2)
    side = jnp.where(h == 1, -1, 1)

    def rows_apart(sign, act_on):
        def row(d):
            @pl.when((h + sign * d >= 0) & (h + sign * d < S))
            def _():
                act_on(h + sign * d, d)

        pl.loop(1, S, unroll=S <= 4)(row)

    def row_devices(r, act_on):
        for dt in range(T):
            for dc in range(C):
                act_on((g, r, lax.rem(t + dt, T), lax.rem(c + dc, C)))

    def beside(sign, act_on):
        for dt in range(1, T):

            @pl.when((t + sign * dt >= 0) & (t + sign * dt < T))
            def _():
                for dc in range(C):
                    act_on((g, h, t + sign * dt, lax.rem(c + dc, C)))

    def mates(act_on):
        for dc in range(1, C):
            act_on((g, h, t, lax.rem(c + dc, C)))

    def signal(sem):
        return lambda where: pl.semaphore_signal(sem, inc=1, device_id=where, device_id_type=MESH)

    def drain(ref, sem):
        pltpu.make_async_copy(ref, ref, sem).wait()

    def send(src, dst, sends, recvs, where):
        copy = pltpu.make_async_remote_copy(
            src_ref=src, dst_ref=dst, send_sem=sends, recv_sem=recvs, device_id=where, device_id_type=MESH,
        )
        copy.start()

    everyone = range(C)
    x_load = pltpu.make_async_copy(x_hbm, x, xload.at[0])
    x_load.start()
    for k, gain in enumerate((g1, g2)):
        pltpu.make_async_copy(gain, gall.at[c, k], xload.at[1]).start()
    barrier = pltpu.get_barrier_semaphore()
    mates(signal(barrier))
    pl.when(attends)(lambda: beside(-1, signal(barrier)))
    rows_apart(1, lambda r, d: row_devices(r, signal(barrier)))
    pl.semaphore_wait(barrier, (h * T + jnp.where(attends, T - 1 - t, 0)) * C + C - 1)

    def answer(r, d):
        for dt in range(T):
            for dc in range(C):
                signal(insem.at[min(dt, 1), d])((g, r, lax.rem(t + dt, T), lax.rem(c + dc, C)))

    @pl.when(h < S - 1)
    def _():
        rows_apart(-1, answer)
        pl.when(h > 0)(lambda: beside(1, signal(insem.at[0, 0])))

    loads = [
        pltpu.make_async_copy(src, dst, wsem.at[i])
        for i, (src, dst) in zip((0, 0, 0, 1, 2), [(wq_hbm, projections.at[0]), (wk_hbm, projections.at[1]), (wv_hbm, projections.at[2]), (wo_hbm, wo), (wc_hbm, wc)])
    ]

    @pl.when(attends)
    def _():
        for load in loads[:4]:
            load.start()

    loads[4].start()

    x_load.wait()
    sums, squares = channel_sums(x[...].reshape(C * W, half).astype(F32))
    stat1_src[0:1] = sums
    stat1_src[1:2] = squares
    at = (h * T + t) * C + c

    def send_stat(where):
        send(stat1_src, stat1.at[at], s1send, s1sem, where)

    def send_x(r, dc):
        frame = lax.rem(c + dc, C)
        send(x.at[frame, 0], xall.at[h * C + c], xsend, xsem.at[h], (g, r, t, frame))

    def column_x(r):
        for dc in range(C):
            send_x(r, dc)

    for r in range(1, S - 1):
        pl.when(r < h)(lambda: row_devices(r, send_stat))

    @pl.when(attends)
    def _():
        stat1[at] = stat1_src[...]
        beside(1, send_stat)
        mates(send_stat)
        xall[h * C + c] = x[c, 0]
        for dc in range(1, C):
            send_x(h, dc)

    for r in range(1, S - 1):
        pl.when(r < h)(lambda: column_x(r))

    drain(gall.at[c], xload.at[1])
    mates(lambda where: send(gall.at[c], gall.at[c], gsend, gsem, where))

    def upward(r, d):
        @pl.when(r < S - 1)
        def _():
            pl.semaphore_wait(insem.at[0, d], C)
            for dc in range(C):
                send_stat((g, r, t, lax.rem(c + dc, C)))
            column_x(r)
            if T > 1:
                pl.semaphore_wait(insem.at[1, d], (T - 1) * C)
            for dt in range(1, T):
                for dc in range(C):
                    send_stat((g, r, lax.rem(t + dt, T), lax.rem(c + dc, C)))

    rows_apart(1, upward)

    @pl.when(attends & (t > 0))
    def _():
        pl.semaphore_wait(insem.at[0, 0], t * C)
        beside(-1, send_stat)

    drain(gall.at[pl.ds(0, C - 1)], gsem)
    population = float(S * T * C * W * GROUP)
    frame_at = t * C + c

    def send_attended(i, k, r, core):
        send(att_src.at[i, k], att_in.at[c], asend, asem, (g, r, t, core))

    def attend(R):
        outer = h + side
        mine = [h, outer][:R]
        skipped = jnp.where(h == 1, R, 0) if R == 2 else None

        def rest(i):
            return i + skipped if R == 2 else i + jnp.where(i >= h, 1, 0)

        drain(stat1.at[pl.ds(0, S * T * C - 1)], s1sem)
        totals = jnp.sum(stat1[...].reshape(S * T, C, 2, half), axis=0)
        mean1, scale1 = moments(jnp.concatenate([totals[k] for k in range(C)], axis=1), population)
        factor1 = scale1 * jnp.concatenate([gall[k, 0] for k in range(C)], axis=1)

        def row_tokens(r):
            pieces = []
            for k in range(C):
                lanes = slice(k * half, (k + 1) * half)
                value = xall[r * C + k].astype(F32)
                pieces.append(((value - mean1[:, lanes]) * factor1[:, lanes]).astype(BF16))
            return jnp.concatenate(pieces, axis=1)

        def project(weight, first, stop):
            rows = tokens[first:stop].reshape((stop - first) * W, D)
            return jnp.dot(rows, weight[...], preferred_element_type=F32).astype(BF16)

        def slots_in(r):
            drain(xall.at[pl.ds(r * C, C)], xsem.at[r])

        drain(xall.at[pl.ds(0, C - 1)], xsem.at[h])
        if R == 2:
            slots_in(outer)
        for i in range(R):
            tokens[i] = row_tokens(mine[i])
        drain(projections, wsem.at[0])
        queries = project(projections.at[0], 0, R)
        for i in range(S - R):
            slots_in(rest(i))
        for i in range(S - R):
            tokens[R + i] = row_tokens(rest(i))
        keyed[...] = project(projections.at[1], 0, S)
        valued[...] = project(projections.at[2], 0, S)

        scores = lax.dot_general(
            queries, keyed[...], (((1,), (1,)), ((), ())), preferred_element_type=F32
        ) * (D ** (-0.5))
        weights = jnp.exp(scores - jnp.max(scores, axis=1, keepdims=True))
        mass = jnp.sum(weights, axis=1, keepdims=True)
        mixed = jnp.dot(weights.astype(BF16), valued[...], preferred_element_type=F32)
        mixed = (mixed / mass).astype(BF16)
        loads[3].wait()
        attended = jnp.dot(mixed, wo[...], preferred_element_type=F32).astype(BF16)

        source = jnp.concatenate(
            [jnp.concatenate([xall[r * C + k] for k in range(C)], axis=1) for r in mine], axis=0
        ).astype(F32)
        resid = (source - mean1) + attended.astype(F32)
        for i in range(R):
            for k in range(T):
                dsrc[i, k] = resid[i * W : (i + 1) * W, k * Kc : (k + 1) * Kc].astype(BF16)

        def send_row(i, r, cores, sends, recv, skip_self=False, own=None):
            for dt in {None: [*range(1, T), 0], False: range(1, T), True: [0]}[own]:
                for dc in cores:
                    if not (skip_self and dt == 0 and dc == 0):
                        to = lax.rem(t + dt, T)
                        send(
                            dsrc.at[i, to], dall.at[(mine[i] - r + 1) * NF + frame_at], sends, recv,
                            (g, r, to, lax.rem(c + dc, C)),
                        )

        if R == 2:
            for own in (False, True):
                for i in range(2):
                    send_row(i, outer, [0], dsend.at[0], outer_sem.at[i, t], own=own)
        sums, squares = channel_sums(resid)
        for k in range(T):
            lanes = slice(k * Kc, (k + 1) * Kc)
            stat2_src[k, 0:1] = sums[:, lanes]
            stat2_src[k, 1:2] = squares[:, lanes]

        def send_stat2(where):
            send(stat2_src.at[where[2]], stat2.at[me], s2send, s2sem, where)

        rows_apart(-1, lambda r, d: row_devices(r, send_stat2))
        rows_apart(1, lambda r, d: row_devices(r, send_stat2))
        beside(-1, send_stat2)
        beside(1, send_stat2)
        mates(send_stat2)
        if R == 2:
            send_row(0, h - side, everyone, dsend.at[1], dsem.at[1 + side, t])
        else:
            send_row(0, h - 1, everyone, dsend.at[1], dsem.at[2, t])
            send_row(0, h + 1, everyone, dsend.at[1], dsem.at[0, t])
        for i in range(R):
            row = mine[i] - h + 1
            send_row(i, h, everyone, dsend.at[1], dsem.at[row, t], skip_self=True)
            dall[row * NF + frame_at] = dsrc[i, t]
        for i in range(R):
            for k in range(C):
                att_src[i, k] = attended[i * W : (i + 1) * W, k * half : (k + 1) * half]
        send_attended(0, other, h, other)
        if R == 2:
            for k in range(C):
                send_attended(1, k, outer, k)
        stat2[me] = stat2_src[t]
        att_out[c, 0] = att_src[0, c]

    if S > 4:
        pl.when(attends & jnp.logical_not(at_edge))(lambda: attend(1))
    pl.when(at_edge)(lambda: attend(2))
    act[0:2] = jnp.zeros((2,) + act.shape[1:], BF16)
    gain2 = jnp.concatenate([gall[k, 1] for k in range(C)], axis=1)

    beyond = jnp.where(h == 0, 1, 0)

    def forward(k):
        for i in range(2):
            row = beyond + i
            slot = row * NF + k * C + c
            drain(dall.at[slot], outer_sem.at[jnp.where(h == 0, 1 - i, i), k])
            mates(lambda where: send(dall.at[slot], dall.at[slot], share_sem, dsem.at[row, k], where))

    @pl.when(jnp.logical_not(attends))
    def _():
        forward(0)
        for k in range(1, T):
            pl.when(t < k)(lambda: forward(k))
        drain(stat2.at[pl.ds(0, attending)], s2sem)

    @pl.when(attends)
    def _():
        drain(stat2.at[pl.ds(0, attending - 1)], s2sem)


    def sliced(v):
        out = v[:, 0:Kc]
        for k in range(1, T):
            out = jnp.where(t == k, v[:, k * Kc : (k + 1) * Kc], out)
        return out

    mean2, scale2 = slice_moments(jnp.sum(stat2[0:attending], axis=0), population)
    factor2 = scale2 * sliced(gain2)
    column = lax.broadcasted_iota(jnp.int32, (W, Kc), 0)

    def activate(row, k):
        for f in range(k * C, (k + 1) * C):
            v = (dall[row * NF + f].astype(F32) - mean2) * factor2
            a = v / (1.0 + jnp.exp(-v))
            left = jnp.where(column == 0, 0.0, pltpu.roll(a, 1, 0))
            right = jnp.where(column == W - 1, 0.0, pltpu.roll(a, W - 1, 0))
            for e, piece in enumerate((left, a, right)):
                place = row * 3 + e
                act[f + 2, :, place * Kc : (place + 1) * Kc] = piece.astype(BF16)

    skips = (3 * Kc) % LANES == 0

    def blank(row):
        act[2:, :, row * 3 * Kc : (row + 1) * 3 * Kc] = jnp.zeros((NF, W, 3 * Kc), BF16)

    if not skips:
        pl.when(h == 0)(lambda: blank(0))
        pl.when(h == S - 1)(lambda: blank(2))

    def row_in(row, k, own, outermost):
        lacks_one = outermost | (own & (t == k))

        @pl.when(lacks_one)
        def _():
            drain(dall.at[pl.ds(0, C - 1)], dsem.at[row, k])

        @pl.when(jnp.logical_not(lacks_one))
        def _():
            drain(dall.at[pl.ds(0, C)], dsem.at[row, k])

        activate(row, k)

    def block_in(k):
        if k:
            pl.when(jnp.logical_not(attends) & (t >= k))(lambda: forward(k))
        row_in(1, k, attends, jnp.logical_not(attends))
        pl.when(h > 0)(lambda: row_in(0, k, h == 1, h == S - 1))
        pl.when(h < S - 1)(lambda: row_in(2, k, h == S - 2, h == 0))

    wide = half // CHUNKS

    def product(to, b0, b1, chunk):
        total = None
        taps = slice(b0 * 3 * Kc, b1 * 3 * Kc)
        for a in range(0 if to else max(0, 3 - C), 3):
            window = act[to * C + a : to * C + a + C, :, taps].reshape(C * W, (b1 - b0) * 3 * Kc)
            weight = wc[a, taps, chunk * wide : (chunk + 1) * wide]
            term = jnp.dot(window, weight, preferred_element_type=F32)
            total = term if total is None else total + term
        return total

    if not skips:
        edges = [(t >= 0, 0, 3)]
    else:
        edges = [(h == 0, 1, 3), (h == S - 1, 0, 2), (attends, 0, 3)]

    def store(to, chunk, value):
        @pl.when(t == to)
        def _():
            own_total[chunk] = value

        @pl.when(t != to)
        def _():
            away = lax.rem(to - t + T, T) - 1
            part_src[away, chunk] = value.astype(BF16)
            send(part_src.at[away, chunk], part.at[away, chunk], psend, psem.at[away, chunk], (g, h, to, c))

    for k in range(T):
        block_in(k)
        if not k:
            loads[4].wait()
        for here, b0, b1 in edges:

            @pl.when(here)
            def _():
                for chunk in range(CHUNKS):
                    store(k, chunk, product(k, b0, b1, chunk))


    @pl.when(attends)
    def _():
        drain(att_in.at[pl.ds(0, C - 1)], asem)
        att_out[other, 0] = att_in[other]
        drain(stat1.at[pl.ds(0, attending - 1)], s1send)
        drain(xall.at[pl.ds(0, (S - 2) * C - 1)], xsend)
        drain(stat2.at[pl.ds(0, S * T * C - 1)], s2send)

    @pl.when(jnp.logical_not(attends))
    def _():
        drain(att_in, asem)
        for k in range(C):
            att_out[k, 0] = att_in[k]
        drain(stat1.at[pl.ds(0, attending)], s1send)
        drain(xall.at[pl.ds(0, (S - 2) * C)], xsend)
        drain(dall.at[pl.ds(0, 2 * T * (C - 1))], share_sem)

    @pl.when(attends & jnp.logical_not(at_edge))
    def _():
        drain(dall.at[pl.ds(0, 3 * NF - 1)], dsend.at[1])
        drain(att_src.at[0, 0], asend)

    @pl.when(at_edge)
    def _():
        drain(dall.at[pl.ds(0, 2 * T)], dsend.at[0])
        drain(dall.at[pl.ds(0, 3 * NF - 2)], dsend.at[1])
        drain(xall.at[pl.ds(0, C + 1)], asend)

    drain(gall.at[pl.ds(0, C - 1)], gsend)
    for chunk in range(CHUNKS):
        total = own_total[chunk]
        for dt in range(1, T):
            drain(part.at[dt - 1, chunk], psem.at[dt - 1, chunk])
            total = total + part[dt - 1, chunk].astype(F32)
        conv_out[:, 0, :, chunk * wide : (chunk + 1) * wide] = total.reshape(C, W, wide).astype(BF16)
    if T > 1:
        drain(part_src, psend)


def slice_moments(totals, population):
    Kc = totals.shape[1]
    if Kc >= LANES:
        return moments(totals, population)
    padded = jnp.concatenate([totals] * (LANES // Kc), axis=1)
    mean, scale = moments(padded, population)
    return mean[:, :Kc], scale[:, :Kc]


def hand_over(att_in, conv_in, att_out, conv_out):
    att_out[...] = att_in[...]
    conv_out[...] = conv_in[...]


def on_device(S, T, C, x, g1, g2, wq, wk, wv, wo, wc):
    frames, rows, W, half = x.shape
    assert frames == C and rows == 1 and half * C == D
    Kc = wc.shape[3]
    assert Kc * T == D and S > 3
    n, NF = S * T * C, T * C
    wide = half // CHUNKS
    wc = wc.reshape(3, 9 * Kc, half)
    vmem = pl.BlockSpec(memory_space=pltpu.VMEM)
    hbm = pl.BlockSpec(memory_space=pl.ANY)
    out = jax.ShapeDtypeStruct(x.shape, BF16)
    dma = pltpu.SemaphoreType.DMA
    kept = pltpu.VMEM(x.shape, BF16)
    links = max(T - 1, 1)
    results = pl.pallas_call(
        functools.partial(kernel, S, T, C, W),
        out_shape=(kept, kept),
        in_specs=[hbm] * 8,
        out_specs=(vmem, vmem),
        scratch_shapes=[
            pltpu.VMEM(x.shape, BF16),
            pltpu.VMEM((3, D, D), BF16),
            pltpu.VMEM((D, D), BF16),
            pltpu.VMEM(wc.shape, BF16),
            pltpu.VMEM((2, half), F32),
            pltpu.VMEM((n, 2, half), F32),
            pltpu.VMEM((T, 2, Kc), F32),
            pltpu.VMEM((n, 2, Kc), F32),
            pltpu.VMEM((C, 2, 1, half), F32),
            pltpu.VMEM((S * C, W, half), BF16),
            pltpu.VMEM((S, W, D), BF16),
            pltpu.VMEM((S * W, D), BF16),
            pltpu.VMEM((S * W, D), BF16),
            pltpu.VMEM((2, C, W, half), BF16),
            pltpu.VMEM((C, W, half), BF16),
            pltpu.VMEM((2, T, W, Kc), BF16),
            pltpu.VMEM((3 * NF, W, Kc), BF16),
            pltpu.VMEM((NF + 2, W, 9 * Kc), BF16),
            pltpu.VMEM((CHUNKS, C * W, wide), F32),
            pltpu.VMEM((links, CHUNKS, C * W, wide), BF16),
            pltpu.VMEM((links, CHUNKS, C * W, wide), BF16),
            dma((2,)),
            dma((3,)),
            pltpu.SemaphoreType.REGULAR((2, S - 1)),
            dma(()),
            dma(()),
            dma(()),
            dma(()),
            dma(()),
            dma((S,)),
            dma(()),
            dma(()),
            dma(()),
            dma(()),
            dma((2,)),
            dma((3, T)),
            dma((2, T)),
            dma(()),
            dma(()),
            dma((links, CHUNKS)),
        ],
        compiler_params=pltpu.CompilerParams(collective_id=0, has_side_effects=True),
    )(x, g1.reshape(1, half), g2.reshape(1, half), wq, wk, wv, wo, wc)
    return pl.pallas_call(
        hand_over, out_shape=(out, out), in_specs=[vmem] * 2, out_specs=(vmem, vmem),
    )(*[pltpu.with_memory_space_constraint(r, pltpu.VMEM) for r in results])


def solution(mesh):
    S, T, C = mesh.shape["space"], mesh.shape["tm"], mesh.shape["chan"]
    placed = (
        P(("groups", "tm"), "space", None, "chan"),
        P("chan"),
        P("chan"),
        P(),
        P(),
        P(),
        P(),
        P(None, None, None, "tm", "chan"),
    )
    return jax.shard_map(
        functools.partial(on_device, S, T, C),
        mesh=mesh,
        in_specs=placed,
        out_specs=(
            P(("groups", "tm"), "space", None, "chan"),
            P(("groups", "tm"), "space", None, "chan"),
        ),
        check_vma=False,
    )
```

```python
import functools

import jax
import jax.numpy as jnp
from jax import lax
from jax.experimental import pallas as pl
from jax.experimental.pallas import tpu as pltpu
from jax.sharding import PartitionSpec as P

D = 512
NGROUP = 32
EPSILON = 1e-06
LANES = 128
CHUNKS = 2
GROUP = D // NGROUP
MESH = pl.DeviceIdType.MESH
F32 = jnp.float32
BF16 = jnp.bfloat16


def group_total(v):
    lane = lax.broadcasted_iota(jnp.int32, v.shape, 1)
    width = v.shape[1]
    step = 1
    while step < GROUP:
        place = (lane // step) % 4
        terms = [v]
        for d in range(1, 4):
            terms.append(jnp.where(place < 4 - d, pltpu.roll(v, width - d * step, 1), 0.0))
            terms.append(jnp.where(place >= d, pltpu.roll(v, d * step, 1), 0.0))
        while len(terms) > 1:
            terms = [sum(terms[i : i + 2]) for i in range(0, len(terms), 2)]
        v = terms[0]
        step *= 4
    return v


def store_sums(ref, values):
    sums = jnp.sum(values, axis=0, keepdims=True)
    squares = jnp.sum(values * values, axis=0, keepdims=True)
    blocks, width = ref.shape[0] // 2, ref.shape[1]
    for b in range(blocks):
        ref[b : b + 1] = sums[:, b * width : (b + 1) * width]
        ref[blocks + b : blocks + b + 1] = squares[:, b * width : (b + 1) * width]


def moments(stacks, population):
    size = stacks[0].shape[0]
    blocks = size // 2
    count = len(stacks) * size
    rows = 8 * pl.cdiv(count, 8)
    padding = [jnp.zeros((rows - count, LANES), F32)] if rows > count else []
    grouped = group_total(jnp.concatenate([*stacks, *padding], axis=0)) / population
    variance = jnp.maximum(pltpu.roll(grouped, rows - blocks, 0) - grouped * grouped, 0.0)
    scale = lax.rsqrt(variance + EPSILON)
    picks = [i * size + b for i in range(len(stacks)) for b in range(blocks)]
    return [jnp.concatenate([v[k : k + 1] for k in picks], axis=1) for v in (grouped, scale)]


def kernel(
    S, T, C, W,
    x_hbm, g1, g2, wq_hbm, wk_hbm, wv_hbm, wo_hbm, wc_hbm,
    att_out, conv_out,
    x, projections, wo, wc,
    stat1_src, row_sum, stat1, stat2_src, stat2, gall,
    xall, tokens, keyed, valued, att_src, att_in, dsrc, dall, act, own_total, part_src, part,
    xload, wsem, insem, gsend, gsem, raw_sem, s1send, s1sem, xsend, xsem, s2send, s2sem,
    asend, asem, dsend, dsem, outer_sem, share_sem, psend, psem,
):
    g = lax.axis_index("groups")
    h = lax.axis_index("space")
    t = lax.axis_index("tm")
    c = lax.axis_index("chan")
    attending = (S - 2) * T * C
    me = (h * T + t) * C + c - T * C
    half = D // C
    Kc = D // T
    NF = T * C
    other = lax.rem(c + 1, C)
    attends = (h > 0) & (h < S - 1)
    at_edge = (h == 1) | (h == S - 2)
    side = jnp.where(h == 1, -1, 1)

    def rows_apart(sign, act_on):
        def row(d):
            @pl.when((h + sign * d >= 0) & (h + sign * d < S))
            def _():
                act_on(h + sign * d, d)

        pl.loop(1, S, unroll=S <= 4)(row)

    def row_devices(r, act_on):
        for dt in range(T):
            for dc in range(C):
                act_on((g, r, lax.rem(t + dt, T), lax.rem(c + dc, C)))

    def row_where(r, sign, act_on):
        for dt in range(1, T):

            @pl.when((t + sign * dt >= 0) & (t + sign * dt < T))
            def _():
                for dc in range(C):
                    act_on((g, r, t + sign * dt, lax.rem(c + dc, C)))

    def beside(sign, act_on):
        row_where(h, sign, act_on)

    def mates(act_on):
        for dc in range(1, C):
            act_on((g, h, t, lax.rem(c + dc, C)))

    def signal(sem):
        return lambda where: pl.semaphore_signal(sem, inc=1, device_id=where, device_id_type=MESH)

    def drain(ref, sem):
        pltpu.make_async_copy(ref, ref, sem).wait()

    def send(src, dst, sends, recvs, where):
        copy = pltpu.make_async_remote_copy(
            src_ref=src, dst_ref=dst, send_sem=sends, recv_sem=recvs, device_id=where, device_id_type=MESH,
        )
        copy.start()

    everyone = range(C)
    x_load = pltpu.make_async_copy(x_hbm, x, xload.at[0])
    x_load.start()
    for k, gain in enumerate((g1, g2)):
        pltpu.make_async_copy(gain, gall.at[c, k], xload.at[1]).start()
    stat1[...] = jnp.zeros(stat1.shape, F32)
    barrier = pltpu.get_barrier_semaphore()
    mates(signal(barrier))
    beside(1, signal(barrier))

    def column(r, act_on):
        for dc in range(C):
            act_on((g, r, t, lax.rem(c + dc, C)))

    def greet(r, d):
        column(r, signal(barrier))
        row_where(r, 1, signal(barrier))

    rows_apart(1, greet)
    pl.semaphore_wait(barrier, (h * (t + 1) + t) * C + C - 1)
    pl.when(h < S - 1)(lambda: rows_apart(-1, lambda r, d: column(r, signal(insem.at[d]))))
    beside(-1, signal(insem.at[0]))

    loads = [
        pltpu.make_async_copy(src, dst, wsem.at[i])
        for i, (src, dst) in zip((0, 0, 0, 1, 2), [(wq_hbm, projections.at[0]), (wk_hbm, projections.at[1]), (wv_hbm, projections.at[2]), (wo_hbm, wo), (wc_hbm, wc)])
    ]

    @pl.when(attends)
    def _():
        for load in loads[:4]:
            load.start()

    loads[4].start()

    x_load.wait()
    store_sums(stat1_src, x[...].reshape(C * W, half).astype(F32))
    at = (h * T + t) * C + c

    def send_stat(where, src=stat1_src, recvs=s1sem):
        send(src, stat1.at[at], s1send, recvs, where)

    def same_row(sign):
        for dt in range(1, T):

            @pl.when((t + sign * dt >= 0) & (t + sign * dt < T))
            def _():
                send_stat((g, h, t + sign * dt, c), recvs=raw_sem)

                @pl.when(attends)
                def _():
                    for dc in range(1, C):
                        send_stat((g, h, t + sign * dt, lax.rem(c + dc, C)))

    def send_x(r, dc):
        frame = lax.rem(c + dc, C)
        send(x.at[frame, 0], xall.at[h * C + c], xsend, xsem.at[h], (g, r, t, frame))

    def column_x(r):
        for dc in range(C):
            send_x(r, dc)

    for r in range(1, S - 1):

        @pl.when(r < h)
        def _():
            column(r, send_stat)
            row_where(r, -1, send_stat)

    pl.when(h < S - 1)(lambda: same_row(-1))
    stat1[at] = stat1_src[...]

    @pl.when(attends)
    def _():
        mates(send_stat)
        xall[h * C + c] = x[c, 0]
        for dc in range(1, C):
            send_x(h, dc)

    for r in range(1, S - 1):
        pl.when(r < h)(lambda: column_x(r))

    drain(gall.at[c], xload.at[1])
    mates(lambda where: send(gall.at[c], gall.at[c], gsend, gsem, where))

    @pl.when(h < S - 2)
    def _():
        pl.semaphore_wait(insem.at[1], C)
        column_x(h + 1)

    @pl.when(t < T - 1)
    def _():
        pl.semaphore_wait(insem.at[0], (T - 1 - t) * C)
        for r in range(1, S - 1):
            pl.when(r < h)(lambda: row_where(r, 1, send_stat))
        pl.when(h < S - 1)(lambda: same_row(1))

    @pl.when(h < S - 1)
    def _():
        if T > 1:
            drain(stat1.at[pl.ds(0, T - 1)], raw_sem)

    @pl.when(h < S - 2)
    def _():
        total = stat1_src[...]
        for dt in range(1, T):
            total = total + stat1[(h * T + lax.rem(t + dt, T)) * C + c]
        row_sum[...] = total

        def send_sum(where):
            send_stat(where, src=row_sum)

        column(h + 1, send_sum)

        def upward(d):
            @pl.when(h + d < S - 1)
            def _():
                pl.semaphore_wait(insem.at[d], C)
                column(h + d, send_sum)
                column_x(h + d)

        pl.loop(2, S - 1, unroll=S <= 4)(upward)

    drain(gall.at[pl.ds(0, C - 1)], gsem)
    population = float(S * T * C * W * GROUP)
    frame_at = t * C + c

    def send_attended(i, k, r, core):
        send(att_src.at[i, k], att_in.at[c], asend, asem, (g, r, t, core))

    def attend(R):
        outer = h + side
        mine = [h, outer][:R]
        skipped = jnp.where(h == 1, R, 0) if R == 2 else None

        def rest(i):
            return i + skipped if R == 2 else i + jnp.where(i >= h, 1, 0)

        def slots_in(r):
            drain(xall.at[pl.ds(r * C, C)], xsem.at[r])

        for r in range(1, S - 1):

            @pl.when(h == r)
            def _():
                drain(stat1.at[pl.ds(0, r * C + T * (C - 1) + (S - 1 - r) * T * C)], s1sem)

        drain(xall.at[pl.ds(0, C - 1)], xsem.at[h])
        if R == 2:
            slots_in(outer)
        for i in range(S - R):
            slots_in(rest(i))
        drain(projections, wsem.at[0])
        drain(wo, wsem.at[1])
        totals = jnp.sum(stat1[...].reshape(S * T, C, *stat1.shape[1:]), axis=0)
        mean1, scale1 = moments([totals[k] for k in range(C)], population)
        factor1 = scale1 * jnp.concatenate([gall[k, 0] for k in range(C)], axis=1)

        def row_tokens(r):
            pieces = []
            for k in range(C):
                lanes = slice(k * half, (k + 1) * half)
                value = xall[r * C + k].astype(F32)
                pieces.append(((value - mean1[:, lanes]) * factor1[:, lanes]).astype(BF16))
            return jnp.concatenate(pieces, axis=1)

        def project(weight, first, stop):
            rows = tokens[first:stop].reshape((stop - first) * W, D)
            return jnp.dot(rows, weight[...], preferred_element_type=F32).astype(BF16)

        for i in range(R):
            tokens[i] = row_tokens(mine[i])
        for i in range(S - R):
            tokens[R + i] = row_tokens(rest(i))
        queries = project(projections.at[0], 0, R)
        keyed[...] = project(projections.at[1], 0, S)
        valued[...] = project(projections.at[2], 0, S)

        scores = lax.dot_general(
            queries, keyed[...], (((1,), (1,)), ((), ())), preferred_element_type=F32
        ) * (D ** (-0.5))
        weights = jnp.exp(scores - jnp.max(scores, axis=1, keepdims=True))
        mass = jnp.sum(weights, axis=1, keepdims=True)
        mixed = jnp.dot(weights.astype(BF16), valued[...], preferred_element_type=F32)
        mixed = (mixed * (1.0 / mass)).astype(BF16)
        attended = jnp.dot(mixed, wo[...], preferred_element_type=F32).astype(BF16)

        source = jnp.concatenate(
            [jnp.concatenate([xall[r * C + k] for k in range(C)], axis=1) for r in mine], axis=0
        ).astype(F32)
        resid = (source - mean1) + attended.astype(F32)
        for i in range(R):
            for k in range(T):
                dsrc[i, k] = resid[i * W : (i + 1) * W, k * Kc : (k + 1) * Kc].astype(BF16)

        def send_row(i, r, cores, sends, recv, skip_self=False, own=None):
            for dt in {None: [*range(1, T), 0], False: range(1, T), True: [0]}[own]:
                for dc in cores:
                    if not (skip_self and dt == 0 and dc == 0):
                        to = lax.rem(t + dt, T)
                        send(
                            dsrc.at[i, to], dall.at[(mine[i] - r + 1) * NF + frame_at], sends, recv,
                            (g, r, to, lax.rem(c + dc, C)),
                        )

        if R == 2:
            for own in (False, True):
                for i in range(2):
                    send_row(i, outer, [0], dsend.at[0], outer_sem.at[i, t], own=own)
        for k in range(T):
            store_sums(stat2_src.at[k], resid[:, k * Kc : (k + 1) * Kc])

        def send_stat2(where):
            send(stat2_src.at[where[2]], stat2.at[me], s2send, s2sem, where)

        rows_apart(-1, lambda r, d: row_devices(r, send_stat2))
        rows_apart(1, lambda r, d: row_devices(r, send_stat2))
        beside(-1, send_stat2)
        beside(1, send_stat2)
        mates(send_stat2)
        if R == 2:
            send_row(0, h - side, everyone, dsend.at[1], dsem.at[1 + side, t])
        else:
            send_row(0, h - 1, everyone, dsend.at[1], dsem.at[2, t])
            send_row(0, h + 1, everyone, dsend.at[1], dsem.at[0, t])
        for i in range(R):
            row = mine[i] - h + 1
            send_row(i, h, everyone, dsend.at[1], dsem.at[row, t], skip_self=True)
            dall[row * NF + frame_at] = dsrc[i, t]
        for i in range(R):
            for k in range(C):
                att_src[i, k] = attended[i * W : (i + 1) * W, k * half : (k + 1) * half]
        send_attended(0, other, h, other)
        if R == 2:
            for k in range(C):
                send_attended(1, k, outer, k)
        stat2[me] = stat2_src[t]
        att_out[c, 0] = att_src[0, c]

    if S > 4:
        pl.when(attends & jnp.logical_not(at_edge))(lambda: attend(1))
    pl.when(at_edge)(lambda: attend(2))
    act[0:2] = jnp.zeros((2,) + act.shape[1:], BF16)
    gain2 = jnp.concatenate([gall[k, 1] for k in range(C)], axis=1)

    beyond = jnp.where(h == 0, 1, 0)

    def forward(k):
        for i in range(2):
            row = beyond + i
            slot = row * NF + k * C + c
            drain(dall.at[slot], outer_sem.at[jnp.where(h == 0, 1 - i, i), k])
            mates(lambda where: send(dall.at[slot], dall.at[slot], share_sem, dsem.at[row, k], where))

    @pl.when(jnp.logical_not(attends))
    def _():
        forward(0)
        for k in range(1, T):
            pl.when(t < k)(lambda: forward(k))
        drain(stat2.at[pl.ds(0, attending)], s2sem)

    @pl.when(attends)
    def _():
        drain(stat2.at[pl.ds(0, attending - 1)], s2sem)


    def sliced(v):
        out = v[:, 0:Kc]
        for k in range(1, T):
            out = jnp.where(t == k, v[:, k * Kc : (k + 1) * Kc], out)
        return out

    mean2, scale2 = slice_moments(jnp.sum(stat2[0:attending], axis=0), population)
    factor2 = scale2 * sliced(gain2)
    column = lax.broadcasted_iota(jnp.int32, (W, Kc), 0)

    def activate(row, k):
        for f in range(k * C, (k + 1) * C):
            v = (dall[row * NF + f].astype(F32) - mean2) * factor2
            a = v / (1.0 + jnp.exp(-v))
            left = jnp.where(column == 0, 0.0, pltpu.roll(a, 1, 0))
            right = jnp.where(column == W - 1, 0.0, pltpu.roll(a, W - 1, 0))
            for e, piece in enumerate((left, a, right)):
                place = row * 3 + e
                act[f + 2, :, place * Kc : (place + 1) * Kc] = piece.astype(BF16)

    skips = (3 * Kc) % LANES == 0

    def blank(row):
        act[2:, :, row * 3 * Kc : (row + 1) * 3 * Kc] = jnp.zeros((NF, W, 3 * Kc), BF16)

    if not skips:
        pl.when(h == 0)(lambda: blank(0))
        pl.when(h == S - 1)(lambda: blank(2))

    def row_in(row, k, own, outermost):
        lacks_one = outermost | (own & (t == k))

        @pl.when(lacks_one)
        def _():
            drain(dall.at[pl.ds(0, C - 1)], dsem.at[row, k])

        @pl.when(jnp.logical_not(lacks_one))
        def _():
            drain(dall.at[pl.ds(0, C)], dsem.at[row, k])

        activate(row, k)

    def block_in(k):
        if k:
            pl.when(jnp.logical_not(attends) & (t >= k))(lambda: forward(k))
        row_in(1, k, attends, jnp.logical_not(attends))
        pl.when(h > 0)(lambda: row_in(0, k, h == 1, h == S - 1))
        pl.when(h < S - 1)(lambda: row_in(2, k, h == S - 2, h == 0))

    wide = half // CHUNKS

    def product(to, b0, b1, chunk):
        total = None
        taps = slice(b0 * 3 * Kc, b1 * 3 * Kc)
        for a in range(0 if to else max(0, 3 - C), 3):
            window = act[to * C + a : to * C + a + C, :, taps].reshape(C * W, (b1 - b0) * 3 * Kc)
            weight = wc[a, taps, chunk * wide : (chunk + 1) * wide]
            term = jnp.dot(window, weight, preferred_element_type=F32)
            total = term if total is None else total + term
        return total

    if not skips:
        edges = [(t >= 0, 0, 3)]
    else:
        edges = [(h == 0, 1, 3), (h == S - 1, 0, 2), (attends, 0, 3)]

    def store(to, chunk, value):
        @pl.when(t == to)
        def _():
            own_total[chunk] = value

        @pl.when(t != to)
        def _():
            away = lax.rem(to - t + T, T) - 1
            part_src[away, chunk] = value.astype(BF16)
            send(part_src.at[away, chunk], part.at[away, chunk], psend, psem.at[away, chunk], (g, h, to, c))

    for k in range(T):
        block_in(k)
        if not k:
            loads[4].wait()
        for here, b0, b1 in edges:

            @pl.when(here)
            def _():
                for chunk in range(CHUNKS):
                    store(k, chunk, product(k, b0, b1, chunk))


    @pl.when(attends)
    def _():
        drain(att_in.at[pl.ds(0, C - 1)], asem)
        att_out[other, 0] = att_in[other]
        drain(xall.at[pl.ds(0, (S - 2) * C - 1)], xsend)
        drain(stat2.at[pl.ds(0, S * T * C - 1)], s2send)

    @pl.when(jnp.logical_not(attends))
    def _():
        drain(att_in, asem)
        for k in range(C):
            att_out[k, 0] = att_in[k]
        drain(xall.at[pl.ds(0, (S - 2) * C)], xsend)
        drain(dall.at[pl.ds(0, 2 * T * (C - 1))], share_sem)

    for r in range(S):

        @pl.when(h == r)
        def _():
            below = max(r - 1, 0) if r < S - 1 else S - 2
            level = (T - 1 if r == 0 else T * C - 1) if r < S - 1 else 0
            above = max(S - 2 - r, 0)
            drain(stat1.at[pl.ds(0, below * T * C + level + above * C)], s1send)

    @pl.when(attends & jnp.logical_not(at_edge))
    def _():
        drain(dall.at[pl.ds(0, 3 * NF - 1)], dsend.at[1])
        drain(att_src.at[0, 0], asend)

    @pl.when(at_edge)
    def _():
        drain(dall.at[pl.ds(0, 2 * T)], dsend.at[0])
        drain(dall.at[pl.ds(0, 3 * NF - 2)], dsend.at[1])
        drain(xall.at[pl.ds(0, C + 1)], asend)

    drain(gall.at[pl.ds(0, C - 1)], gsend)
    for chunk in range(CHUNKS):
        total = own_total[chunk]
        for dt in range(1, T):
            drain(part.at[dt - 1, chunk], psem.at[dt - 1, chunk])
            total = total + part[dt - 1, chunk].astype(F32)
        conv_out[:, 0, :, chunk * wide : (chunk + 1) * wide] = total.reshape(C, W, wide).astype(BF16)
    if T > 1:
        drain(part_src, psend)


def slice_moments(totals, population):
    width = totals.shape[1]
    if width == LANES:
        return moments([totals], population)
    mean, scale = moments([jnp.concatenate([totals] * (LANES // width), axis=1)], population)
    return mean[:, :width], scale[:, :width]


def hand_over(att_in, conv_in, att_out, conv_out):
    att_out[...] = att_in[...]
    conv_out[...] = conv_in[...]


def on_device(S, T, C, x, g1, g2, wq, wk, wv, wo, wc):
    frames, rows, W, half = x.shape
    assert frames == C and rows == 1 and half * C == D
    Kc = wc.shape[3]
    assert Kc * T == D and S > 3
    n, NF = S * T * C, T * C
    wide = half // CHUNKS
    wc = wc.reshape(3, 9 * Kc, half)
    vmem = pl.BlockSpec(memory_space=pltpu.VMEM)
    hbm = pl.BlockSpec(memory_space=pl.ANY)
    out = jax.ShapeDtypeStruct(x.shape, BF16)
    dma = pltpu.SemaphoreType.DMA
    kept = pltpu.VMEM(x.shape, BF16)
    links = max(T - 1, 1)
    stats = (2 * max(Kc // LANES, 1), min(Kc, LANES))
    results = pl.pallas_call(
        functools.partial(kernel, S, T, C, W),
        out_shape=(kept, kept),
        in_specs=[hbm] * 8,
        out_specs=(vmem, vmem),
        scratch_shapes=[
            pltpu.VMEM(x.shape, BF16),
            pltpu.VMEM((3, D, D), BF16),
            pltpu.VMEM((D, D), BF16),
            pltpu.VMEM(wc.shape, BF16),
            pltpu.VMEM((half // 64, LANES), F32),
            pltpu.VMEM((half // 64, LANES), F32),
            pltpu.VMEM((n, half // 64, LANES), F32),
            pltpu.VMEM((T, *stats), F32),
            pltpu.VMEM((n, *stats), F32),
            pltpu.VMEM((C, 2, 1, half), F32),
            pltpu.VMEM((S * C, W, half), BF16),
            pltpu.VMEM((S, W, D), BF16),
            pltpu.VMEM((S * W, D), BF16),
            pltpu.VMEM((S * W, D), BF16),
            pltpu.VMEM((2, C, W, half), BF16),
            pltpu.VMEM((C, W, half), BF16),
            pltpu.VMEM((2, T, W, Kc), BF16),
            pltpu.VMEM((3 * NF, W, Kc), BF16),
            pltpu.VMEM((NF + 2, W, 9 * Kc), BF16),
            pltpu.VMEM((CHUNKS, C * W, wide), F32),
            pltpu.VMEM((links, CHUNKS, C * W, wide), BF16),
            pltpu.VMEM((links, CHUNKS, C * W, wide), BF16),
            dma((2,)),
            dma((3,)),
            pltpu.SemaphoreType.REGULAR((S - 1,)),
            dma(()),
            dma(()),
            dma(()),
            dma(()),
            dma(()),
            dma(()),
            dma((S,)),
            dma(()),
            dma(()),
            dma(()),
            dma(()),
            dma((2,)),
            dma((3, T)),
            dma((2, T)),
            dma(()),
            dma(()),
            dma((links, CHUNKS)),
        ],
        compiler_params=pltpu.CompilerParams(collective_id=0, has_side_effects=True),
    )(x, g1.reshape(1, half), g2.reshape(1, half), wq, wk, wv, wo, wc)
    return pl.pallas_call(
        hand_over, out_shape=(out, out), in_specs=[vmem] * 2, out_specs=(vmem, vmem),
    )(*[pltpu.with_memory_space_constraint(r, pltpu.VMEM) for r in results])


def solution(mesh):
    S, T, C = mesh.shape["space"], mesh.shape["tm"], mesh.shape["chan"]
    placed = (
        P(("groups", "tm"), "space", None, "chan"),
        P("chan"),
        P("chan"),
        P(),
        P(),
        P(),
        P(),
        P(None, None, None, "tm", "chan"),
    )
    return jax.shard_map(
        functools.partial(on_device, S, T, C),
        mesh=mesh,
        in_specs=placed,
        out_specs=(
            P(("groups", "tm"), "space", None, "chan"),
            P(("groups", "tm"), "space", None, "chan"),
        ),
        check_vma=False,
    )
```

```python
import functools

import jax
import jax.numpy as jnp
from jax import lax
from jax.experimental import pallas as pl
from jax.experimental.pallas import tpu as pltpu
from jax.sharding import PartitionSpec as P

D = 512
NGROUP = 32
EPSILON = 1e-06
LANES = 128
CHUNKS = 2
GROUP = D // NGROUP
MESH = pl.DeviceIdType.MESH
F32 = jnp.float32
BF16 = jnp.bfloat16


def group_total(v):
    lane = lax.broadcasted_iota(jnp.int32, v.shape, 1)
    width = v.shape[1]
    step = 1
    while step < GROUP:
        place = (lane // step) % 4
        terms = [v]
        for d in range(1, 4):
            terms.append(jnp.where(place < 4 - d, pltpu.roll(v, width - d * step, 1), 0.0))
            terms.append(jnp.where(place >= d, pltpu.roll(v, d * step, 1), 0.0))
        while len(terms) > 1:
            terms = [sum(terms[i : i + 2]) for i in range(0, len(terms), 2)]
        v = terms[0]
        step *= 4
    return v


def store_sums(ref, values):
    sums = jnp.sum(values, axis=0, keepdims=True)
    squares = jnp.sum(values * values, axis=0, keepdims=True)
    blocks, width = ref.shape[0] // 2, ref.shape[1]
    for b in range(blocks):
        ref[b : b + 1] = sums[:, b * width : (b + 1) * width]
        ref[blocks + b : blocks + b + 1] = squares[:, b * width : (b + 1) * width]


def moments(stacks, population):
    size = stacks[0].shape[0]
    blocks = size // 2
    count = len(stacks) * size
    rows = 8 * pl.cdiv(count, 8)
    padding = [jnp.zeros((rows - count, LANES), F32)] if rows > count else []
    grouped = group_total(jnp.concatenate([*stacks, *padding], axis=0)) / population
    variance = jnp.maximum(pltpu.roll(grouped, rows - blocks, 0) - grouped * grouped, 0.0)
    scale = lax.rsqrt(variance + EPSILON)
    picks = [i * size + b for i in range(len(stacks)) for b in range(blocks)]
    return [jnp.concatenate([v[k : k + 1] for k in picks], axis=1) for v in (grouped, scale)]


def kernel(
    S, T, C, W,
    x_hbm, g1, g2, wq_hbm, wk_hbm, wv_hbm, wo_hbm, wc_hbm,
    att_out, conv_out,
    x, projections, wo, wc,
    stat1_src, row_sum, stat1, stat2_src, stat2, gall,
    xall, tokens, keyed, valued, att_src, att_in, dsrc, dall, act, own_total, part_src, part,
    xload, wsem, insem, gsend, gsem, raw_sem, s1send, s1sem, xsend, xsem, s2send, s2sem,
    asend, asem, dsend, dsem, outer_sem, share_sem, psend, psem,
):
    g = lax.axis_index("groups")
    h = lax.axis_index("space")
    t = lax.axis_index("tm")
    c = lax.axis_index("chan")
    attending = (S - 2) * T * C
    me = (h * T + t) * C + c - T * C
    half = D // C
    Kc = D // T
    NF = T * C
    other = lax.rem(c + 1, C)
    attends = (h > 0) & (h < S - 1)
    at_edge = (h == 1) | (h == S - 2)
    side = jnp.where(h == 1, -1, 1)

    def rows_apart(sign, act_on):
        def row(d):
            @pl.when((h + sign * d >= 0) & (h + sign * d < S))
            def _():
                act_on(h + sign * d, d)

        pl.loop(1, S, unroll=S <= 4)(row)

    def row_devices(r, act_on):
        for dt in range(T):
            for dc in range(C):
                act_on((g, r, lax.rem(t + dt, T), lax.rem(c + dc, C)))

    def row_where(r, sign, act_on):
        for dt in range(1, T):

            @pl.when((t + sign * dt >= 0) & (t + sign * dt < T))
            def _():
                for dc in range(C):
                    act_on((g, r, t + sign * dt, lax.rem(c + dc, C)))

    def beside(sign, act_on):
        row_where(h, sign, act_on)

    def mates(act_on):
        for dc in range(1, C):
            act_on((g, h, t, lax.rem(c + dc, C)))

    def signal(sem):
        return lambda where: pl.semaphore_signal(sem, inc=1, device_id=where, device_id_type=MESH)

    def drain(ref, sem):
        pltpu.make_async_copy(ref, ref, sem).wait()

    def send(src, dst, sends, recvs, where):
        copy = pltpu.make_async_remote_copy(
            src_ref=src, dst_ref=dst, send_sem=sends, recv_sem=recvs, device_id=where, device_id_type=MESH,
        )
        copy.start()

    everyone = range(C)
    x_load = pltpu.make_async_copy(x_hbm, x, xload.at[0])
    x_load.start()
    for k, gain in enumerate((g1, g2)):
        pltpu.make_async_copy(gain, gall.at[c, k], xload.at[1]).start()
    stat1[...] = jnp.zeros(stat1.shape, F32)
    barrier = pltpu.get_barrier_semaphore()
    mates(signal(barrier))
    beside(1, signal(barrier))

    def column(r, act_on):
        for dc in range(C):
            act_on((g, r, t, lax.rem(c + dc, C)))

    def greet(r, d):
        column(r, signal(barrier))
        row_where(r, 1, signal(barrier))

    rows_apart(1, greet)
    pl.semaphore_wait(barrier, (h * (t + 1) + t) * C + C - 1)
    pl.when(h < S - 1)(lambda: rows_apart(-1, lambda r, d: column(r, signal(insem.at[d]))))
    beside(-1, signal(insem.at[0]))

    loads = [
        pltpu.make_async_copy(src, dst, wsem.at[i])
        for i, (src, dst) in zip((0, 0, 0, 1, 2), [(wq_hbm, projections.at[0]), (wk_hbm, projections.at[1]), (wv_hbm, projections.at[2]), (wo_hbm, wo), (wc_hbm, wc)])
    ]

    @pl.when(attends)
    def _():
        for load in loads[:4]:
            load.start()

    loads[4].start()

    x_load.wait()
    store_sums(stat1_src, x[...].reshape(C * W, half).astype(F32))
    at = (h * T + t) * C + c

    def send_stat(where, src=stat1_src, recvs=s1sem):
        send(src, stat1.at[at], s1send, recvs, where)

    def same_row(sign):
        for dt in range(1, T):

            @pl.when((t + sign * dt >= 0) & (t + sign * dt < T))
            def _():
                send_stat((g, h, t + sign * dt, c), recvs=raw_sem)

                @pl.when(attends)
                def _():
                    for dc in range(1, C):
                        send_stat((g, h, t + sign * dt, lax.rem(c + dc, C)))

    def send_x(r, dc):
        frame = lax.rem(c + dc, C)
        send(x.at[frame, 0], xall.at[h * C + c], xsend, xsem.at[h], (g, r, t, frame))

    def column_x(r):
        for dc in range(C):
            send_x(r, dc)

    for r in range(1, S - 1):

        @pl.when(r < h)
        def _():
            column(r, send_stat)
            row_where(r, -1, send_stat)

    pl.when(h < S - 1)(lambda: same_row(-1))
    stat1[at] = stat1_src[...]

    @pl.when(attends)
    def _():
        mates(send_stat)
        xall[h * C + c] = x[c, 0]
        for dc in range(1, C):
            send_x(h, dc)

    for r in range(1, S - 1):
        pl.when(r < h)(lambda: column_x(r))

    drain(gall.at[c], xload.at[1])
    mates(lambda where: send(gall.at[c], gall.at[c], gsend, gsem, where))

    @pl.when(h < S - 2)
    def _():
        pl.semaphore_wait(insem.at[1], C)
        column_x(h + 1)

    @pl.when(t < T - 1)
    def _():
        pl.semaphore_wait(insem.at[0], (T - 1 - t) * C)
        for r in range(1, S - 1):
            pl.when(r < h)(lambda: row_where(r, 1, send_stat))
        pl.when(h < S - 1)(lambda: same_row(1))

    @pl.when(h < S - 1)
    def _():
        if T > 1:
            drain(stat1.at[pl.ds(0, T - 1)], raw_sem)

    @pl.when(h < S - 2)
    def _():
        total = stat1_src[...]
        for dt in range(1, T):
            total = total + stat1[(h * T + lax.rem(t + dt, T)) * C + c]
        row_sum[...] = total

        def send_sum(where):
            send_stat(where, src=row_sum)

        column(h + 1, send_sum)

        def upward(d):
            @pl.when(h + d < S - 1)
            def _():
                pl.semaphore_wait(insem.at[d], C)
                column(h + d, send_sum)
                column_x(h + d)

        pl.loop(2, S - 1, unroll=S <= 4)(upward)

    drain(gall.at[pl.ds(0, C - 1)], gsem)
    population = float(S * T * C * W * GROUP)
    frame_at = t * C + c

    def send_attended(i, k, r, core):
        send(att_src.at[i, k], att_in.at[c], asend, asem, (g, r, t, core))

    def attend(R):
        outer = h + side
        mine = [h, outer][:R]
        skipped = jnp.where(h == 1, R, 0) if R == 2 else None

        def rest(i):
            return i + skipped if R == 2 else i + jnp.where(i >= h, 1, 0)

        def slots_in(r):
            drain(xall.at[pl.ds(r * C, C)], xsem.at[r])

        for r in range(1, S - 1):

            @pl.when(h == r)
            def _():
                drain(stat1.at[pl.ds(0, r * C + T * (C - 1) + (S - 1 - r) * T * C)], s1sem)

        drain(xall.at[pl.ds(0, C - 1)], xsem.at[h])
        if R == 2:
            slots_in(outer)
        for i in range(S - R):
            slots_in(rest(i))
        drain(projections, wsem.at[0])
        drain(wo, wsem.at[1])
        totals = jnp.sum(stat1[...].reshape(S * T, C, *stat1.shape[1:]), axis=0)
        mean1, scale1 = moments([totals[k] for k in range(C)], population)
        factor1 = scale1 * jnp.concatenate([gall[k, 0] for k in range(C)], axis=1)

        def row_tokens(r):
            pieces = []
            for k in range(C):
                lanes = slice(k * half, (k + 1) * half)
                value = xall[r * C + k].astype(F32)
                pieces.append(((value - mean1[:, lanes]) * factor1[:, lanes]).astype(BF16))
            return jnp.concatenate(pieces, axis=1)

        def project(weight, first, stop):
            rows = tokens[first:stop].reshape((stop - first) * W, D)
            return jnp.dot(rows, weight[...], preferred_element_type=F32).astype(BF16)

        for i in range(R):
            tokens[i] = row_tokens(mine[i])
        for i in range(S - R):
            tokens[R + i] = row_tokens(rest(i))
        queries = project(projections.at[0], 0, R)
        keyed[...] = project(projections.at[1], 0, S)
        valued[...] = project(projections.at[2], 0, S)

        scores = lax.dot_general(
            queries, keyed[...], (((1,), (1,)), ((), ())), preferred_element_type=F32
        ) * (D ** (-0.5))
        weights = jnp.exp(scores - jnp.max(scores, axis=1, keepdims=True))
        mass = jnp.sum(weights, axis=1, keepdims=True)
        mixed = jnp.dot(weights.astype(BF16), valued[...], preferred_element_type=F32)
        mixed = (mixed * (1.0 / mass)).astype(BF16)
        attended = jnp.dot(mixed, wo[...], preferred_element_type=F32).astype(BF16)

        source = jnp.concatenate(
            [jnp.concatenate([xall[r * C + k] for k in range(C)], axis=1) for r in mine], axis=0
        ).astype(F32)
        resid = (source - mean1) + attended.astype(F32)
        for i in range(R):
            for k in range(T):
                dsrc[i, k] = resid[i * W : (i + 1) * W, k * Kc : (k + 1) * Kc].astype(BF16)

        def send_row(i, r, cores, sends, recv, skip_self=False, own=None):
            for dt in {None: [*range(1, T), 0], False: range(1, T), True: [0]}[own]:
                for dc in cores:
                    if not (skip_self and dt == 0 and dc == 0):
                        to = lax.rem(t + dt, T)
                        send(
                            dsrc.at[i, to], dall.at[(mine[i] - r + 1) * NF + frame_at], sends, recv,
                            (g, r, to, lax.rem(c + dc, C)),
                        )

        for k in range(T):
            store_sums(stat2_src.at[k], resid[:, k * Kc : (k + 1) * Kc])

        def send_stat2(where):
            send(stat2_src.at[where[2]], stat2.at[me], s2send, s2sem, where)

        rows_apart(-1, lambda r, d: row_devices(r, send_stat2))
        rows_apart(1, lambda r, d: row_devices(r, send_stat2))
        beside(-1, send_stat2)
        beside(1, send_stat2)
        mates(send_stat2)
        if R == 2:
            for own in (False, True):
                for i in range(2):
                    send_row(i, outer, [0], dsend.at[0], outer_sem.at[i, t], own=own)
        if R == 2:
            send_row(0, h - side, everyone, dsend.at[1], dsem.at[1 + side, t])
        else:
            send_row(0, h - 1, everyone, dsend.at[1], dsem.at[2, t])
            send_row(0, h + 1, everyone, dsend.at[1], dsem.at[0, t])
        for i in range(R):
            row = mine[i] - h + 1
            send_row(i, h, everyone, dsend.at[1], dsem.at[row, t], skip_self=True)
            dall[row * NF + frame_at] = dsrc[i, t]
        for i in range(R):
            for k in range(C):
                att_src[i, k] = attended[i * W : (i + 1) * W, k * half : (k + 1) * half]
        send_attended(0, other, h, other)
        if R == 2:
            for k in range(C):
                send_attended(1, k, outer, k)
        stat2[me] = stat2_src[t]
        att_out[c, 0] = att_src[0, c]

    if S > 4:
        pl.when(attends & jnp.logical_not(at_edge))(lambda: attend(1))
    pl.when(at_edge)(lambda: attend(2))
    act[0:2] = jnp.zeros((2,) + act.shape[1:], BF16)
    gain2 = jnp.concatenate([gall[k, 1] for k in range(C)], axis=1)

    beyond = jnp.where(h == 0, 1, 0)

    def forward(k):
        for i in range(2):
            row = beyond + i
            slot = row * NF + k * C + c
            drain(dall.at[slot], outer_sem.at[jnp.where(h == 0, 1 - i, i), k])
            mates(lambda where: send(dall.at[slot], dall.at[slot], share_sem, dsem.at[row, k], where))

    @pl.when(jnp.logical_not(attends))
    def _():
        forward(0)
        for k in range(1, T):
            pl.when(t < k)(lambda: forward(k))
        drain(stat2.at[pl.ds(0, attending)], s2sem)

    @pl.when(attends)
    def _():
        drain(stat2.at[pl.ds(0, attending - 1)], s2sem)


    def sliced(v):
        out = v[:, 0:Kc]
        for k in range(1, T):
            out = jnp.where(t == k, v[:, k * Kc : (k + 1) * Kc], out)
        return out

    mean2, scale2 = slice_moments(jnp.sum(stat2[0:attending], axis=0), population)
    factor2 = scale2 * sliced(gain2)
    column = lax.broadcasted_iota(jnp.int32, (W, Kc), 0)

    def activate(row, k):
        for f in range(k * C, (k + 1) * C):
            v = (dall[row * NF + f].astype(F32) - mean2) * factor2
            a = v / (1.0 + jnp.exp(-v))
            left = jnp.where(column == 0, 0.0, pltpu.roll(a, 1, 0))
            right = jnp.where(column == W - 1, 0.0, pltpu.roll(a, W - 1, 0))
            for e, piece in enumerate((left, a, right)):
                place = row * 3 + e
                act[f + 2, :, place * Kc : (place + 1) * Kc] = piece.astype(BF16)

    skips = (3 * Kc) % LANES == 0

    def blank(row):
        act[2:, :, row * 3 * Kc : (row + 1) * 3 * Kc] = jnp.zeros((NF, W, 3 * Kc), BF16)

    if not skips:
        pl.when(h == 0)(lambda: blank(0))
        pl.when(h == S - 1)(lambda: blank(2))

    def row_in(row, k, own, outermost):
        lacks_one = outermost | (own & (t == k))

        @pl.when(lacks_one)
        def _():
            drain(dall.at[pl.ds(0, C - 1)], dsem.at[row, k])

        @pl.when(jnp.logical_not(lacks_one))
        def _():
            drain(dall.at[pl.ds(0, C)], dsem.at[row, k])

        activate(row, k)

    def block_in(k):
        if k:
            pl.when(jnp.logical_not(attends) & (t >= k))(lambda: forward(k))
        row_in(1, k, attends, jnp.logical_not(attends))
        pl.when(h > 0)(lambda: row_in(0, k, h == 1, h == S - 1))
        pl.when(h < S - 1)(lambda: row_in(2, k, h == S - 2, h == 0))

    wide = half // CHUNKS

    def product(to, b0, b1, chunk):
        total = None
        taps = slice(b0 * 3 * Kc, b1 * 3 * Kc)
        for a in range(0 if to else max(0, 3 - C), 3):
            window = act[to * C + a : to * C + a + C, :, taps].reshape(C * W, (b1 - b0) * 3 * Kc)
            weight = wc[a, taps, chunk * wide : (chunk + 1) * wide]
            term = jnp.dot(window, weight, preferred_element_type=F32)
            total = term if total is None else total + term
        return total

    if not skips:
        edges = [(t >= 0, 0, 3)]
    else:
        edges = [(h == 0, 1, 3), (h == S - 1, 0, 2), (attends, 0, 3)]

    def store(to, chunk, value):
        @pl.when(t == to)
        def _():
            own_total[chunk] = value

        @pl.when(t != to)
        def _():
            away = lax.rem(to - t + T, T) - 1
            part_src[away, chunk] = value.astype(BF16)
            send(part_src.at[away, chunk], part.at[away, chunk], psend, psem.at[away, chunk], (g, h, to, c))

    for k in range(T):
        block_in(k)
        if not k:
            loads[4].wait()
        for here, b0, b1 in edges:

            @pl.when(here)
            def _():
                for chunk in range(CHUNKS):
                    store(k, chunk, product(k, b0, b1, chunk))


    @pl.when(attends)
    def _():
        drain(att_in.at[pl.ds(0, C - 1)], asem)
        att_out[other, 0] = att_in[other]
        drain(xall.at[pl.ds(0, (S - 2) * C - 1)], xsend)
        drain(stat2.at[pl.ds(0, S * T * C - 1)], s2send)

    @pl.when(jnp.logical_not(attends))
    def _():
        drain(att_in, asem)
        for k in range(C):
            att_out[k, 0] = att_in[k]
        drain(xall.at[pl.ds(0, (S - 2) * C)], xsend)
        drain(dall.at[pl.ds(0, 2 * T * (C - 1))], share_sem)

    for r in range(S):

        @pl.when(h == r)
        def _():
            below = max(r - 1, 0) if r < S - 1 else S - 2
            level = (T - 1 if r == 0 else T * C - 1) if r < S - 1 else 0
            above = max(S - 2 - r, 0)
            drain(stat1.at[pl.ds(0, below * T * C + level + above * C)], s1send)

    @pl.when(attends & jnp.logical_not(at_edge))
    def _():
        drain(dall.at[pl.ds(0, 3 * NF - 1)], dsend.at[1])
        drain(att_src.at[0, 0], asend)

    @pl.when(at_edge)
    def _():
        drain(dall.at[pl.ds(0, 2 * T)], dsend.at[0])
        drain(dall.at[pl.ds(0, 3 * NF - 2)], dsend.at[1])
        drain(xall.at[pl.ds(0, C + 1)], asend)

    drain(gall.at[pl.ds(0, C - 1)], gsend)
    for chunk in range(CHUNKS):
        total = own_total[chunk]
        for dt in range(1, T):
            drain(part.at[dt - 1, chunk], psem.at[dt - 1, chunk])
            total = total + part[dt - 1, chunk].astype(F32)
        conv_out[:, 0, :, chunk * wide : (chunk + 1) * wide] = total.reshape(C, W, wide).astype(BF16)
    if T > 1:
        drain(part_src, psend)


def slice_moments(totals, population):
    width = totals.shape[1]
    if width == LANES:
        return moments([totals], population)
    mean, scale = moments([jnp.concatenate([totals] * (LANES // width), axis=1)], population)
    return mean[:, :width], scale[:, :width]


def hand_over(att_in, conv_in, att_out, conv_out):
    att_out[...] = att_in[...]
    conv_out[...] = conv_in[...]


def on_device(S, T, C, x, g1, g2, wq, wk, wv, wo, wc):
    frames, rows, W, half = x.shape
    assert frames == C and rows == 1 and half * C == D
    Kc = wc.shape[3]
    assert Kc * T == D and S > 3
    n, NF = S * T * C, T * C
    wide = half // CHUNKS
    wc = wc.reshape(3, 9 * Kc, half)
    vmem = pl.BlockSpec(memory_space=pltpu.VMEM)
    hbm = pl.BlockSpec(memory_space=pl.ANY)
    out = jax.ShapeDtypeStruct(x.shape, BF16)
    dma = pltpu.SemaphoreType.DMA
    kept = pltpu.VMEM(x.shape, BF16)
    links = max(T - 1, 1)
    stats = (2 * max(Kc // LANES, 1), min(Kc, LANES))
    results = pl.pallas_call(
        functools.partial(kernel, S, T, C, W),
        out_shape=(kept, kept),
        in_specs=[hbm] * 8,
        out_specs=(vmem, vmem),
        scratch_shapes=[
            pltpu.VMEM(x.shape, BF16),
            pltpu.VMEM((3, D, D), BF16),
            pltpu.VMEM((D, D), BF16),
            pltpu.VMEM(wc.shape, BF16),
            pltpu.VMEM((half // 64, LANES), F32),
            pltpu.VMEM((half // 64, LANES), F32),
            pltpu.VMEM((n, half // 64, LANES), F32),
            pltpu.VMEM((T, *stats), F32),
            pltpu.VMEM((n, *stats), F32),
            pltpu.VMEM((C, 2, 1, half), F32),
            pltpu.VMEM((S * C, W, half), BF16),
            pltpu.VMEM((S, W, D), BF16),
            pltpu.VMEM((S * W, D), BF16),
            pltpu.VMEM((S * W, D), BF16),
            pltpu.VMEM((2, C, W, half), BF16),
            pltpu.VMEM((C, W, half), BF16),
            pltpu.VMEM((2, T, W, Kc), BF16),
            pltpu.VMEM((3 * NF, W, Kc), BF16),
            pltpu.VMEM((NF + 2, W, 9 * Kc), BF16),
            pltpu.VMEM((CHUNKS, C * W, wide), F32),
            pltpu.VMEM((links, CHUNKS, C * W, wide), BF16),
            pltpu.VMEM((links, CHUNKS, C * W, wide), BF16),
            dma((2,)),
            dma((3,)),
            pltpu.SemaphoreType.REGULAR((S - 1,)),
            dma(()),
            dma(()),
            dma(()),
            dma(()),
            dma(()),
            dma(()),
            dma((S,)),
            dma(()),
            dma(()),
            dma(()),
            dma(()),
            dma((2,)),
            dma((3, T)),
            dma((2, T)),
            dma(()),
            dma(()),
            dma((links, CHUNKS)),
        ],
        compiler_params=pltpu.CompilerParams(collective_id=0, has_side_effects=True),
    )(x, g1.reshape(1, half), g2.reshape(1, half), wq, wk, wv, wo, wc)
    return pl.pallas_call(
        hand_over, out_shape=(out, out), in_specs=[vmem] * 2, out_specs=(vmem, vmem),
    )(*[pltpu.with_memory_space_constraint(r, pltpu.VMEM) for r in results])


def solution(mesh):
    S, T, C = mesh.shape["space"], mesh.shape["tm"], mesh.shape["chan"]
    placed = (
        P(("groups", "tm"), "space", None, "chan"),
        P("chan"),
        P("chan"),
        P(),
        P(),
        P(),
        P(),
        P(None, None, None, "tm", "chan"),
    )
    return jax.shard_map(
        functools.partial(on_device, S, T, C),
        mesh=mesh,
        in_specs=placed,
        out_specs=(
            P(("groups", "tm"), "space", None, "chan"),
            P(("groups", "tm"), "space", None, "chan"),
        ),
        check_vma=False,
    )
```

```python
import functools

import jax
import jax.numpy as jnp
from jax import lax
from jax.experimental import pallas as pl
from jax.experimental.pallas import tpu as pltpu
from jax.sharding import PartitionSpec as P

D = 512
NGROUP = 32
EPSILON = 1e-06
LANES = 128
CHUNKS = 2
GROUP = D // NGROUP
MESH = pl.DeviceIdType.MESH
F32 = jnp.float32
BF16 = jnp.bfloat16


def group_total(v):
    lane = lax.broadcasted_iota(jnp.int32, v.shape, 1)
    width = v.shape[1]
    step = 1
    while step < GROUP:
        place = (lane // step) % 4
        terms = [v]
        for d in range(1, 4):
            terms.append(jnp.where(place < 4 - d, pltpu.roll(v, width - d * step, 1), 0.0))
            terms.append(jnp.where(place >= d, pltpu.roll(v, d * step, 1), 0.0))
        while len(terms) > 1:
            terms = [sum(terms[i : i + 2]) for i in range(0, len(terms), 2)]
        v = terms[0]
        step *= 4
    return v


def store_sums(ref, values):
    sums = jnp.sum(values, axis=0, keepdims=True)
    squares = jnp.sum(values * values, axis=0, keepdims=True)
    blocks, width = ref.shape[0] // 2, ref.shape[1]
    for b in range(blocks):
        ref[b : b + 1] = sums[:, b * width : (b + 1) * width]
        ref[blocks + b : blocks + b + 1] = squares[:, b * width : (b + 1) * width]


def moments(stacks, population):
    size = stacks[0].shape[0]
    blocks = size // 2
    count = len(stacks) * size
    rows = 8 * pl.cdiv(count, 8)
    padding = [jnp.zeros((rows - count, LANES), F32)] if rows > count else []
    grouped = group_total(jnp.concatenate([*stacks, *padding], axis=0)) / population
    variance = jnp.maximum(pltpu.roll(grouped, rows - blocks, 0) - grouped * grouped, 0.0)
    scale = lax.rsqrt(variance + EPSILON)
    picks = [i * size + b for i in range(len(stacks)) for b in range(blocks)]
    return [jnp.concatenate([v[k : k + 1] for k in picks], axis=1) for v in (grouped, scale)]


def kernel(
    S, T, C, W,
    x_hbm, g1, g2, wq_hbm, wk_hbm, wv_hbm, wo_hbm, wc_hbm,
    att_out, conv_out,
    x, projections, wo, wc,
    stat1_src, row_sum, stat1, stat2_src, stat2, gall,
    xall, tokens, keyed, valued, att_src, att_in, dsrc, dall, act, own_total, part_src, part,
    xload, wsem, insem, gsend, gsem, raw_sem, s1send, s1sem, xsend, xsem, s2send, s2sem,
    asend, asem, dsend, dsem, outer_sem, share_sem, psend, psem,
):
    g = lax.axis_index("groups")
    h = lax.axis_index("space")
    t = lax.axis_index("tm")
    c = lax.axis_index("chan")
    attending = (S - 2) * T * C
    me = (h * T + t) * C + c - T * C
    half = D // C
    Kc = D // T
    NF = T * C
    other = lax.rem(c + 1, C)
    attends = (h > 0) & (h < S - 1)
    at_edge = (h == 1) | (h == S - 2)
    side = jnp.where(h == 1, -1, 1)

    def rows_apart(sign, act_on):
        def row(d):
            @pl.when((h + sign * d >= 0) & (h + sign * d < S))
            def _():
                act_on(h + sign * d, d)

        pl.loop(1, S, unroll=S <= 4)(row)

    def row_devices(r, act_on):
        for dt in range(T):
            for dc in range(C):
                act_on((g, r, lax.rem(t + dt, T), lax.rem(c + dc, C)))

    def row_where(r, sign, act_on):
        for dt in range(1, T):

            @pl.when((t + sign * dt >= 0) & (t + sign * dt < T))
            def _():
                for dc in range(C):
                    act_on((g, r, t + sign * dt, lax.rem(c + dc, C)))

    def beside(sign, act_on):
        row_where(h, sign, act_on)

    def mates(act_on):
        for dc in range(1, C):
            act_on((g, h, t, lax.rem(c + dc, C)))

    def signal(sem):
        return lambda where: pl.semaphore_signal(sem, inc=1, device_id=where, device_id_type=MESH)

    def drain(ref, sem):
        pltpu.make_async_copy(ref, ref, sem).wait()

    def send(src, dst, sends, recvs, where):
        copy = pltpu.make_async_remote_copy(
            src_ref=src, dst_ref=dst, send_sem=sends, recv_sem=recvs, device_id=where, device_id_type=MESH,
        )
        copy.start()

    everyone = range(C)
    x_load = pltpu.make_async_copy(x_hbm, x, xload.at[0])
    x_load.start()
    for k, gain in enumerate((g1, g2)):
        pltpu.make_async_copy(gain, gall.at[c, k], xload.at[1]).start()
    stat1[...] = jnp.zeros(stat1.shape, F32)
    barrier = pltpu.get_barrier_semaphore()
    mates(signal(barrier))
    beside(1, signal(barrier))

    def column(r, act_on):
        for dc in range(C):
            act_on((g, r, t, lax.rem(c + dc, C)))

    def greet(r, d):
        column(r, signal(barrier))
        row_where(r, 1, signal(barrier))

    rows_apart(1, greet)
    pl.semaphore_wait(barrier, (h * (t + 1) + t) * C + C - 1)
    pl.when(h < S - 1)(lambda: rows_apart(-1, lambda r, d: column(r, signal(insem.at[d]))))
    beside(-1, signal(insem.at[0]))

    loads = [
        pltpu.make_async_copy(src, dst, wsem.at[i])
        for i, (src, dst) in zip((0, 0, 0, 1, 2), [(wq_hbm, projections.at[0]), (wk_hbm, projections.at[1]), (wv_hbm, projections.at[2]), (wo_hbm, wo), (wc_hbm, wc)])
    ]

    @pl.when(attends)
    def _():
        for load in loads[:4]:
            load.start()

    loads[4].start()

    x_load.wait()
    store_sums(stat1_src, x[...].reshape(C * W, half).astype(F32))
    at = (h * T + t) * C + c

    def send_stat(where, src=stat1_src, recvs=s1sem):
        send(src, stat1.at[at], s1send, recvs, where)

    def same_row(sign):
        for dt in range(1, T):

            @pl.when((t + sign * dt >= 0) & (t + sign * dt < T))
            def _():
                send_stat((g, h, t + sign * dt, c), recvs=raw_sem)

                @pl.when(attends)
                def _():
                    for dc in range(1, C):
                        send_stat((g, h, t + sign * dt, lax.rem(c + dc, C)))

    def send_x(r, dc):
        frame = lax.rem(c + dc, C)
        send(x.at[frame, 0], xall.at[h * C + c], xsend, xsem.at[h], (g, r, t, frame))

    def column_x(r):
        for dc in range(C):
            send_x(r, dc)

    for r in range(1, S - 1):

        @pl.when(r < h)
        def _():
            column(r, send_stat)
            row_where(r, -1, send_stat)

    pl.when(h < S - 1)(lambda: same_row(-1))
    stat1[at] = stat1_src[...]

    @pl.when(attends)
    def _():
        mates(send_stat)
        xall[h * C + c] = x[c, 0]
        for dc in range(1, C):
            send_x(h, dc)

    for r in range(1, S - 1):
        pl.when(r < h)(lambda: column_x(r))

    drain(gall.at[c], xload.at[1])
    mates(lambda where: send(gall.at[c], gall.at[c], gsend, gsem, where))

    @pl.when(h < S - 2)
    def _():
        pl.semaphore_wait(insem.at[1], C)
        column_x(h + 1)

    @pl.when(t < T - 1)
    def _():
        pl.semaphore_wait(insem.at[0], (T - 1 - t) * C)
        for r in range(1, S - 1):
            pl.when(r < h)(lambda: row_where(r, 1, send_stat))
        pl.when(h < S - 1)(lambda: same_row(1))

    @pl.when(h < S - 1)
    def _():
        if T > 1:
            drain(stat1.at[pl.ds(0, T - 1)], raw_sem)

    @pl.when(h < S - 2)
    def _():
        total = stat1_src[...]
        for dt in range(1, T):
            total = total + stat1[(h * T + lax.rem(t + dt, T)) * C + c]
        row_sum[...] = total

        def send_sum(where):
            send_stat(where, src=row_sum)

        column(h + 1, send_sum)

        def upward(d):
            @pl.when(h + d < S - 1)
            def _():
                pl.semaphore_wait(insem.at[d], C)
                column(h + d, send_sum)
                column_x(h + d)

        pl.loop(2, S - 1, unroll=S <= 4)(upward)

    drain(gall.at[pl.ds(0, C - 1)], gsem)
    population = float(S * T * C * W * GROUP)
    frame_at = t * C + c

    def send_attended(i, k, r, core):
        send(att_src.at[i, k], att_in.at[c], asend, asem, (g, r, t, core))

    def attend(R):
        outer = h + side
        mine = [h, outer][:R]
        skipped = jnp.where(h == 1, R, 0) if R == 2 else None

        def rest(i):
            return i + skipped if R == 2 else i + jnp.where(i >= h, 1, 0)

        def slots_in(r):
            drain(xall.at[pl.ds(r * C, C)], xsem.at[r])

        for r in range(1, S - 1):

            @pl.when(h == r)
            def _():
                drain(stat1.at[pl.ds(0, r * C + T * (C - 1) + (S - 1 - r) * T * C)], s1sem)

        drain(xall.at[pl.ds(0, C - 1)], xsem.at[h])
        if R == 2:
            slots_in(outer)
        for i in range(S - R):
            slots_in(rest(i))
        drain(projections, wsem.at[0])
        drain(wo, wsem.at[1])
        totals = jnp.sum(stat1[...].reshape(S * T, C, *stat1.shape[1:]), axis=0)
        mean1, scale1 = moments([totals[k] for k in range(C)], population)
        factor1 = scale1 * jnp.concatenate([gall[k, 0] for k in range(C)], axis=1)

        def row_tokens(r):
            pieces = []
            for k in range(C):
                lanes = slice(k * half, (k + 1) * half)
                value = xall[r * C + k].astype(F32)
                pieces.append(((value - mean1[:, lanes]) * factor1[:, lanes]).astype(BF16))
            return jnp.concatenate(pieces, axis=1)

        def project(weight, first, stop):
            rows = tokens[first:stop].reshape((stop - first) * W, D)
            return jnp.dot(rows, weight[...], preferred_element_type=F32).astype(BF16)

        for i in range(R):
            tokens[i] = row_tokens(mine[i])
        for i in range(S - R):
            tokens[R + i] = row_tokens(rest(i))
        queries = project(projections.at[0], 0, R)
        keyed[...] = project(projections.at[1], 0, S)
        valued[...] = project(projections.at[2], 0, S)

        scores = lax.dot_general(
            queries, keyed[...], (((1,), (1,)), ((), ())), preferred_element_type=F32
        ) * (D ** (-0.5))
        weights = jnp.exp(scores - jnp.max(scores, axis=1, keepdims=True))
        mass = jnp.sum(weights, axis=1, keepdims=True)
        mixed = jnp.dot(weights.astype(BF16), valued[...], preferred_element_type=F32)
        mixed = (mixed * (1.0 / mass)).astype(BF16)
        attended = jnp.dot(mixed, wo[...], preferred_element_type=F32).astype(BF16)

        source = jnp.concatenate(
            [jnp.concatenate([xall[r * C + k] for k in range(C)], axis=1) for r in mine], axis=0
        ).astype(F32)
        resid = (source - mean1) + attended.astype(F32)
        for i in range(R):
            for k in range(T):
                dsrc[i, k] = resid[i * W : (i + 1) * W, k * Kc : (k + 1) * Kc].astype(BF16)

        def send_row(i, r, cores, sends, recv, skip_self=False, own=None):
            for dt in {None: [*range(1, T), 0], False: range(1, T), True: [0]}[own]:
                for dc in cores:
                    if not (skip_self and dt == 0 and dc == 0):
                        to = lax.rem(t + dt, T)
                        send(
                            dsrc.at[i, to], dall.at[(mine[i] - r + 1) * NF + frame_at], sends, recv,
                            (g, r, to, lax.rem(c + dc, C)),
                        )

        for k in range(T):
            store_sums(stat2_src.at[k], resid[:, k * Kc : (k + 1) * Kc])

        def send_stat2(where):
            send(stat2_src.at[where[2]], stat2.at[me], s2send, s2sem, where)

        rows_apart(-1, lambda r, d: row_devices(r, send_stat2))
        rows_apart(1, lambda r, d: row_devices(r, send_stat2))
        beside(-1, send_stat2)
        beside(1, send_stat2)
        mates(send_stat2)
        if R == 2:
            for own in (False, True):
                for i in range(2):
                    send_row(i, outer, [0], dsend.at[0], outer_sem.at[i, t], own=own)
        if R == 2:
            send_row(0, h - side, everyone, dsend.at[1], dsem.at[1 + side, t])
        else:
            send_row(0, h - 1, everyone, dsend.at[1], dsem.at[2, t])
            send_row(0, h + 1, everyone, dsend.at[1], dsem.at[0, t])
        for i in range(R):
            row = mine[i] - h + 1
            send_row(i, h, everyone, dsend.at[1], dsem.at[row, t], skip_self=True)
            dall[row * NF + frame_at] = dsrc[i, t]
        for i in range(R):
            for k in range(C):
                att_src[i, k] = attended[i * W : (i + 1) * W, k * half : (k + 1) * half]
        send_attended(0, other, h, other)
        if R == 2:
            for k in range(C):
                send_attended(1, k, outer, k)
        stat2[me] = stat2_src[t]
        att_out[c, 0] = att_src[0, c]

    if S > 4:
        pl.when(attends & jnp.logical_not(at_edge))(lambda: attend(1))
    pl.when(at_edge)(lambda: attend(2))
    act[0:2] = jnp.zeros((2,) + act.shape[1:], BF16)
    gain2 = jnp.concatenate([gall[k, 1] for k in range(C)], axis=1)

    beyond = jnp.where(h == 0, 1, 0)

    def forward(k):
        for i in range(2):
            row = beyond + i
            slot = row * NF + k * C + c
            drain(dall.at[slot], outer_sem.at[jnp.where(h == 0, 1 - i, i), k])
            mates(lambda where: send(dall.at[slot], dall.at[slot], share_sem, dsem.at[row, k], where))

    @pl.when(jnp.logical_not(attends))
    def _():
        forward(0)
        for k in range(1, T):
            pl.when(t < k)(lambda: forward(k))
        drain(stat2.at[pl.ds(0, attending)], s2sem)

    @pl.when(attends)
    def _():
        drain(stat2.at[pl.ds(0, attending - 1)], s2sem)


    def sliced(v):
        out = v[:, 0:Kc]
        for k in range(1, T):
            out = jnp.where(t == k, v[:, k * Kc : (k + 1) * Kc], out)
        return out

    mean2, scale2 = slice_moments(jnp.sum(stat2[0:attending], axis=0), population)
    factor2 = scale2 * sliced(gain2)
    column = lax.broadcasted_iota(jnp.int32, (W, Kc), 0)

    def activate(row, k):
        for f in range(k * C, (k + 1) * C):
            v = (dall[row * NF + f].astype(F32) - mean2) * factor2
            a = v / (1.0 + jnp.exp(-v))
            left = jnp.where(column == 0, 0.0, pltpu.roll(a, 1, 0))
            right = jnp.where(column == W - 1, 0.0, pltpu.roll(a, W - 1, 0))
            for e, piece in enumerate((left, a, right)):
                place = row * 3 + e
                act[f + 2, :, place * Kc : (place + 1) * Kc] = piece.astype(BF16)

    skips = (3 * Kc) % LANES == 0

    def blank(row):
        act[2:, :, row * 3 * Kc : (row + 1) * 3 * Kc] = jnp.zeros((NF, W, 3 * Kc), BF16)

    if not skips:
        pl.when(h == 0)(lambda: blank(0))
        pl.when(h == S - 1)(lambda: blank(2))

    def row_in(row, k, own, outermost):
        lacks_one = outermost | (own & (t == k))

        @pl.when(lacks_one)
        def _():
            drain(dall.at[pl.ds(0, C - 1)], dsem.at[row, k])

        @pl.when(jnp.logical_not(lacks_one))
        def _():
            drain(dall.at[pl.ds(0, C)], dsem.at[row, k])

        activate(row, k)

    def block_in(k):
        if k:
            pl.when(jnp.logical_not(attends) & (t >= k))(lambda: forward(k))
        row_in(1, k, attends, jnp.logical_not(attends))
        pl.when(h > 0)(lambda: row_in(0, k, h == 1, h == S - 1))
        pl.when(h < S - 1)(lambda: row_in(2, k, h == S - 2, h == 0))

    wide = half // CHUNKS

    def product(to, b0, b1, chunk):
        total = None
        taps = slice(b0 * 3 * Kc, b1 * 3 * Kc)
        for a in range(0 if to else max(0, 3 - C), 3):
            window = act[to * C + a : to * C + a + C, :, taps].reshape(C * W, (b1 - b0) * 3 * Kc)
            weight = wc[a, taps, chunk * wide : (chunk + 1) * wide]
            term = jnp.dot(window, weight, preferred_element_type=F32)
            total = term if total is None else total + term
        return total

    if not skips:
        edges = [(t >= 0, 0, 3)]
    else:
        edges = [(h == 0, 1, 3), (h == S - 1, 0, 2), (attends, 0, 3)]

    def convolve(to, store):
        for here, b0, b1 in edges:

            @pl.when(here)
            def _():
                for chunk in range(CHUNKS):
                    store(chunk, product(to, b0, b1, chunk))

    def convolve_away(to):
        away = lax.rem(to - t + T, T) - 1

        def store(chunk, value):
            part_src[away, chunk] = value.astype(BF16)
            send(part_src.at[away, chunk], part.at[away, chunk], psend, psem.at[away, chunk], (g, h, to, c))

        convolve(to, store)

    def keep(chunk, value):
        own_total[chunk] = value

    loads[4].wait()
    for k in range(T):
        block_in(k)
        pl.when(t != k)(lambda: convolve_away(k))

    for k in range(T):
        pl.when(t == k)(lambda: convolve(k, keep))

    @pl.when(attends)
    def _():
        drain(att_in.at[pl.ds(0, C - 1)], asem)
        att_out[other, 0] = att_in[other]
        drain(xall.at[pl.ds(0, (S - 2) * C - 1)], xsend)
        drain(stat2.at[pl.ds(0, S * T * C - 1)], s2send)

    @pl.when(jnp.logical_not(attends))
    def _():
        drain(att_in, asem)
        for k in range(C):
            att_out[k, 0] = att_in[k]
        drain(xall.at[pl.ds(0, (S - 2) * C)], xsend)
        drain(dall.at[pl.ds(0, 2 * T * (C - 1))], share_sem)

    for r in range(S):

        @pl.when(h == r)
        def _():
            below = max(r - 1, 0) if r < S - 1 else S - 2
            level = (T - 1 if r == 0 else T * C - 1) if r < S - 1 else 0
            above = max(S - 2 - r, 0)
            drain(stat1.at[pl.ds(0, below * T * C + level + above * C)], s1send)

    @pl.when(attends & jnp.logical_not(at_edge))
    def _():
        drain(dall.at[pl.ds(0, 3 * NF - 1)], dsend.at[1])
        drain(att_src.at[0, 0], asend)

    @pl.when(at_edge)
    def _():
        drain(dall.at[pl.ds(0, 2 * T)], dsend.at[0])
        drain(dall.at[pl.ds(0, 3 * NF - 2)], dsend.at[1])
        drain(xall.at[pl.ds(0, C + 1)], asend)

    drain(gall.at[pl.ds(0, C - 1)], gsend)
    for chunk in range(CHUNKS):
        total = own_total[chunk]
        for dt in range(1, T):
            drain(part.at[dt - 1, chunk], psem.at[dt - 1, chunk])
            total = total + part[dt - 1, chunk].astype(F32)
        conv_out[:, 0, :, chunk * wide : (chunk + 1) * wide] = total.reshape(C, W, wide).astype(BF16)
    if T > 1:
        drain(part_src, psend)


def slice_moments(totals, population):
    width = totals.shape[1]
    if width == LANES:
        return moments([totals], population)
    mean, scale = moments([jnp.concatenate([totals] * (LANES // width), axis=1)], population)
    return mean[:, :width], scale[:, :width]


def hand_over(att_in, conv_in, att_out, conv_out):
    att_out[...] = att_in[...]
    conv_out[...] = conv_in[...]


def on_device(S, T, C, x, g1, g2, wq, wk, wv, wo, wc):
    frames, rows, W, half = x.shape
    assert frames == C and rows == 1 and half * C == D
    Kc = wc.shape[3]
    assert Kc * T == D and S > 3
    n, NF = S * T * C, T * C
    wide = half // CHUNKS
    wc = wc.reshape(3, 9 * Kc, half)
    vmem = pl.BlockSpec(memory_space=pltpu.VMEM)
    hbm = pl.BlockSpec(memory_space=pl.ANY)
    out = jax.ShapeDtypeStruct(x.shape, BF16)
    dma = pltpu.SemaphoreType.DMA
    kept = pltpu.VMEM(x.shape, BF16)
    links = max(T - 1, 1)
    stats = (2 * max(Kc // LANES, 1), min(Kc, LANES))
    results = pl.pallas_call(
        functools.partial(kernel, S, T, C, W),
        out_shape=(kept, kept),
        in_specs=[hbm] * 8,
        out_specs=(vmem, vmem),
        scratch_shapes=[
            pltpu.VMEM(x.shape, BF16),
            pltpu.VMEM((3, D, D), BF16),
            pltpu.VMEM((D, D), BF16),
            pltpu.VMEM(wc.shape, BF16),
            pltpu.VMEM((half // 64, LANES), F32),
            pltpu.VMEM((half // 64, LANES), F32),
            pltpu.VMEM((n, half // 64, LANES), F32),
            pltpu.VMEM((T, *stats), F32),
            pltpu.VMEM((n, *stats), F32),
            pltpu.VMEM((C, 2, 1, half), F32),
            pltpu.VMEM((S * C, W, half), BF16),
            pltpu.VMEM((S, W, D), BF16),
            pltpu.VMEM((S * W, D), BF16),
            pltpu.VMEM((S * W, D), BF16),
            pltpu.VMEM((2, C, W, half), BF16),
            pltpu.VMEM((C, W, half), BF16),
            pltpu.VMEM((2, T, W, Kc), BF16),
            pltpu.VMEM((3 * NF, W, Kc), BF16),
            pltpu.VMEM((NF + 2, W, 9 * Kc), BF16),
            pltpu.VMEM((CHUNKS, C * W, wide), F32),
            pltpu.VMEM((links, CHUNKS, C * W, wide), BF16),
            pltpu.VMEM((links, CHUNKS, C * W, wide), BF16),
            dma((2,)),
            dma((3,)),
            pltpu.SemaphoreType.REGULAR((S - 1,)),
            dma(()),
            dma(()),
            dma(()),
            dma(()),
            dma(()),
            dma(()),
            dma((S,)),
            dma(()),
            dma(()),
            dma(()),
            dma(()),
            dma((2,)),
            dma((3, T)),
            dma((2, T)),
            dma(()),
            dma(()),
            dma((links, CHUNKS)),
        ],
        compiler_params=pltpu.CompilerParams(collective_id=0, has_side_effects=True),
    )(x, g1.reshape(1, half), g2.reshape(1, half), wq, wk, wv, wo, wc)
    return pl.pallas_call(
        hand_over, out_shape=(out, out), in_specs=[vmem] * 2, out_specs=(vmem, vmem),
    )(*[pltpu.with_memory_space_constraint(r, pltpu.VMEM) for r in results])


def solution(mesh):
    S, T, C = mesh.shape["space"], mesh.shape["tm"], mesh.shape["chan"]
    placed = (
        P(("groups", "tm"), "space", None, "chan"),
        P("chan"),
        P("chan"),
        P(),
        P(),
        P(),
        P(),
        P(None, None, None, "tm", "chan"),
    )
    return jax.shard_map(
        functools.partial(on_device, S, T, C),
        mesh=mesh,
        in_specs=placed,
        out_specs=(
            P(("groups", "tm"), "space", None, "chan"),
            P(("groups", "tm"), "space", None, "chan"),
        ),
        check_vma=False,
    )
```

```python
import functools

import jax
import jax.numpy as jnp
from jax import lax
from jax.experimental import pallas as pl
from jax.experimental.pallas import tpu as pltpu
from jax.sharding import PartitionSpec as P

D = 512
NGROUP = 32
EPSILON = 1e-06
LANES = 128
CHUNKS = 2
GROUP = D // NGROUP
MESH = pl.DeviceIdType.MESH
F32 = jnp.float32
BF16 = jnp.bfloat16


def group_total(v):
    lane = lax.broadcasted_iota(jnp.int32, v.shape, 1)
    width = v.shape[1]
    step = 1
    while step < GROUP:
        place = (lane // step) % 4
        terms = [v]
        for d in range(1, 4):
            terms.append(jnp.where(place < 4 - d, pltpu.roll(v, width - d * step, 1), 0.0))
            terms.append(jnp.where(place >= d, pltpu.roll(v, d * step, 1), 0.0))
        while len(terms) > 1:
            terms = [sum(terms[i : i + 2]) for i in range(0, len(terms), 2)]
        v = terms[0]
        step *= 4
    return v


def store_sums(ref, values):
    sums = jnp.sum(values, axis=0, keepdims=True)
    squares = jnp.sum(values * values, axis=0, keepdims=True)
    blocks, width = ref.shape[0] // 2, ref.shape[1]
    for b in range(blocks):
        ref[b : b + 1] = sums[:, b * width : (b + 1) * width]
        ref[blocks + b : blocks + b + 1] = squares[:, b * width : (b + 1) * width]


def moments(stacks, population):
    size = stacks[0].shape[0]
    blocks = size // 2
    count = len(stacks) * size
    rows = 8 * pl.cdiv(count, 8)
    padding = [jnp.zeros((rows - count, LANES), F32)] if rows > count else []
    grouped = group_total(jnp.concatenate([*stacks, *padding], axis=0)) / population
    variance = jnp.maximum(pltpu.roll(grouped, rows - blocks, 0) - grouped * grouped, 0.0)
    scale = lax.rsqrt(variance + EPSILON)
    picks = [i * size + b for i in range(len(stacks)) for b in range(blocks)]
    return [jnp.concatenate([v[k : k + 1] for k in picks], axis=1) for v in (grouped, scale)]


def kernel(
    S, T, C, W,
    x_hbm, g1, g2, wq_hbm, wk_hbm, wv_hbm, wo_hbm, wc_hbm,
    att_out, conv_out,
    x, projections, wo, wc,
    stat1_src, row_sum, stat1, stat2_src, stat2, gall,
    xall, tokens, keyed, valued, att_src, att_in, dsrc, dall, act, own_total, part_src, part,
    xload, wsem, insem, gsend, gsem, raw_sem, s1send, s1sem, xsend, xsem, s2send, s2sem,
    asend, asem, dsend, dsem, direct_sem, share_sem, psend, psem,
):
    g = lax.axis_index("groups")
    h = lax.axis_index("space")
    t = lax.axis_index("tm")
    c = lax.axis_index("chan")
    attending = (S - 2) * T * C
    me = (h * T + t) * C + c - T * C
    half = D // C
    Kc = D // T
    NF = T * C
    other = lax.rem(c + 1, C)
    attends = (h > 0) & (h < S - 1)
    at_edge = (h == 1) | (h == S - 2)
    side = jnp.where(h == 1, -1, 1)

    def rows_apart(sign, act_on):
        def row(d):
            @pl.when((h + sign * d >= 0) & (h + sign * d < S))
            def _():
                act_on(h + sign * d, d)

        pl.loop(1, S, unroll=S <= 4)(row)

    def row_devices(r, act_on):
        for dt in range(T):
            for dc in range(C):
                act_on((g, r, lax.rem(t + dt, T), lax.rem(c + dc, C)))

    def row_where(r, sign, act_on):
        for dt in range(1, T):

            @pl.when((t + sign * dt >= 0) & (t + sign * dt < T))
            def _():
                for dc in range(C):
                    act_on((g, r, t + sign * dt, lax.rem(c + dc, C)))

    def beside(sign, act_on):
        row_where(h, sign, act_on)

    def mates(act_on):
        for dc in range(1, C):
            act_on((g, h, t, lax.rem(c + dc, C)))

    def signal(sem):
        return lambda where: pl.semaphore_signal(sem, inc=1, device_id=where, device_id_type=MESH)

    def drain(ref, sem):
        pltpu.make_async_copy(ref, ref, sem).wait()

    def send(src, dst, sends, recvs, where):
        copy = pltpu.make_async_remote_copy(
            src_ref=src, dst_ref=dst, send_sem=sends, recv_sem=recvs, device_id=where, device_id_type=MESH,
        )
        copy.start()

    x_load = pltpu.make_async_copy(x_hbm, x, xload.at[0])
    x_load.start()
    for k, gain in enumerate((g1, g2)):
        pltpu.make_async_copy(gain, gall.at[c, k], xload.at[1]).start()
    stat1[...] = jnp.zeros(stat1.shape, F32)
    barrier = pltpu.get_barrier_semaphore()
    mates(signal(barrier))
    beside(1, signal(barrier))

    def column(r, act_on):
        for dc in range(C):
            act_on((g, r, t, lax.rem(c + dc, C)))

    def greet(r, d):
        column(r, signal(barrier))
        row_where(r, 1, signal(barrier))

    rows_apart(1, greet)
    pl.semaphore_wait(barrier, (h * (t + 1) + t) * C + C - 1)
    pl.when(h < S - 1)(lambda: rows_apart(-1, lambda r, d: column(r, signal(insem.at[d]))))
    beside(-1, signal(insem.at[0]))

    loads = [
        pltpu.make_async_copy(src, dst, wsem.at[i])
        for i, (src, dst) in zip((0, 0, 0, 1, 2), [(wq_hbm, projections.at[0]), (wk_hbm, projections.at[1]), (wv_hbm, projections.at[2]), (wo_hbm, wo), (wc_hbm, wc)])
    ]

    @pl.when(attends)
    def _():
        for load in loads[:4]:
            load.start()

    loads[4].start()

    x_load.wait()
    store_sums(stat1_src, x[...].reshape(C * W, half).astype(F32))
    at = (h * T + t) * C + c

    def send_stat(where, src=stat1_src, recvs=s1sem):
        send(src, stat1.at[at], s1send, recvs, where)

    def same_row(sign):
        for dt in range(1, T):

            @pl.when((t + sign * dt >= 0) & (t + sign * dt < T))
            def _():
                send_stat((g, h, t + sign * dt, c), recvs=raw_sem)

                @pl.when(attends)
                def _():
                    for dc in range(1, C):
                        send_stat((g, h, t + sign * dt, lax.rem(c + dc, C)))

    def send_x(r, dc):
        frame = lax.rem(c + dc, C)
        send(x.at[frame, 0], xall.at[h * C + c], xsend, xsem.at[h], (g, r, t, frame))

    def column_x(r):
        for dc in range(C):
            send_x(r, dc)

    for r in range(1, S - 1):

        @pl.when(r < h)
        def _():
            column(r, send_stat)
            row_where(r, -1, send_stat)

    pl.when(h < S - 1)(lambda: same_row(-1))
    stat1[at] = stat1_src[...]

    @pl.when(attends)
    def _():
        mates(send_stat)
        xall[h * C + c] = x[c, 0]
        for dc in range(1, C):
            send_x(h, dc)

    for r in range(1, S - 1):
        pl.when(r < h)(lambda: column_x(r))

    drain(gall.at[c], xload.at[1])
    mates(lambda where: send(gall.at[c], gall.at[c], gsend, gsem, where))

    @pl.when(h < S - 2)
    def _():
        pl.semaphore_wait(insem.at[1], C)
        column_x(h + 1)

    @pl.when(t < T - 1)
    def _():
        pl.semaphore_wait(insem.at[0], (T - 1 - t) * C)
        for r in range(1, S - 1):
            pl.when(r < h)(lambda: row_where(r, 1, send_stat))
        pl.when(h < S - 1)(lambda: same_row(1))

    @pl.when(h < S - 1)
    def _():
        if T > 1:
            drain(stat1.at[pl.ds(0, T - 1)], raw_sem)

    @pl.when(h < S - 2)
    def _():
        total = stat1_src[...]
        for dt in range(1, T):
            total = total + stat1[(h * T + lax.rem(t + dt, T)) * C + c]
        row_sum[...] = total

        def send_sum(where):
            send_stat(where, src=row_sum)

        column(h + 1, send_sum)

        def upward(d):
            @pl.when(h + d < S - 1)
            def _():
                pl.semaphore_wait(insem.at[d], C)
                column(h + d, send_sum)
                column_x(h + d)

        pl.loop(2, S - 1, unroll=S <= 4)(upward)

    drain(gall.at[pl.ds(0, C - 1)], gsem)
    population = float(S * T * C * W * GROUP)
    frame_at = t * C + c

    def send_attended(i, k, r, core):
        send(att_src.at[i, k], att_in.at[c], asend, asem, (g, r, t, core))

    def attend(R):
        outer = h + side
        mine = [h, outer][:R]
        skipped = jnp.where(h == 1, R, 0) if R == 2 else None

        def rest(i):
            return i + skipped if R == 2 else i + jnp.where(i >= h, 1, 0)

        def slots_in(r):
            drain(xall.at[pl.ds(r * C, C)], xsem.at[r])

        for r in range(1, S - 1):

            @pl.when(h == r)
            def _():
                drain(stat1.at[pl.ds(0, r * C + T * (C - 1) + (S - 1 - r) * T * C)], s1sem)

        drain(xall.at[pl.ds(0, C - 1)], xsem.at[h])
        if R == 2:
            slots_in(outer)
        for i in range(S - R):
            slots_in(rest(i))
        drain(projections, wsem.at[0])
        drain(wo, wsem.at[1])
        totals = jnp.sum(stat1[...].reshape(S * T, C, *stat1.shape[1:]), axis=0)
        mean1, scale1 = moments([totals[k] for k in range(C)], population)
        factor1 = scale1 * jnp.concatenate([gall[k, 0] for k in range(C)], axis=1)

        def row_tokens(r):
            pieces = []
            for k in range(C):
                lanes = slice(k * half, (k + 1) * half)
                value = xall[r * C + k].astype(F32)
                pieces.append(((value - mean1[:, lanes]) * factor1[:, lanes]).astype(BF16))
            return jnp.concatenate(pieces, axis=1)

        def project(weight, first, stop):
            rows = tokens[first:stop].reshape((stop - first) * W, D)
            return jnp.dot(rows, weight[...], preferred_element_type=F32).astype(BF16)

        for i in range(R):
            tokens[i] = row_tokens(mine[i])
        for i in range(S - R):
            tokens[R + i] = row_tokens(rest(i))
        queries = project(projections.at[0], 0, R)
        keyed[...] = project(projections.at[1], 0, S)
        valued[...] = project(projections.at[2], 0, S)

        scores = lax.dot_general(
            queries, keyed[...], (((1,), (1,)), ((), ())), preferred_element_type=F32
        ) * (D ** (-0.5))
        weights = jnp.exp(scores - jnp.max(scores, axis=1, keepdims=True))
        mass = jnp.sum(weights, axis=1, keepdims=True)
        mixed = jnp.dot(weights.astype(BF16), valued[...], preferred_element_type=F32)
        mixed = (mixed * (1.0 / mass)).astype(BF16)
        attended = jnp.dot(mixed, wo[...], preferred_element_type=F32).astype(BF16)

        source = jnp.concatenate(
            [jnp.concatenate([xall[r * C + k] for k in range(C)], axis=1) for r in mine], axis=0
        ).astype(F32)
        resid = (source - mean1) + attended.astype(F32)
        for i in range(R):
            for k in range(T):
                dsrc[i, k] = resid[i * W : (i + 1) * W, k * Kc : (k + 1) * Kc].astype(BF16)

        def send_row(i, r, columns, sends):
            for dt in columns:
                to = lax.rem(t + dt, T)
                row = mine[i] - r + 1
                send(
                    dsrc.at[i, to], dall.at[row * NF + frame_at], sends, direct_sem.at[row, t], (g, r, to, c),
                )

        others = range(1, T)
        for k in range(T):
            store_sums(stat2_src.at[k], resid[:, k * Kc : (k + 1) * Kc])

        def send_stat2(where):
            send(stat2_src.at[where[2]], stat2.at[me], s2send, s2sem, where)

        rows_apart(-1, lambda r, d: row_devices(r, send_stat2))
        rows_apart(1, lambda r, d: row_devices(r, send_stat2))
        beside(-1, send_stat2)
        beside(1, send_stat2)
        mates(send_stat2)
        if R == 2:
            for i in range(2):
                send_row(i, outer, others, dsend.at[0])
            send_row(0, h - side, [*others, 0], dsend.at[1])
        else:
            for r in (h - 1, h + 1):
                send_row(0, r, [*others, 0], dsend.at[1])
        for i in range(R):
            send_row(i, h, others, dsend.at[1])
            slot = (mine[i] - h + 1) * NF + frame_at
            mates(lambda where: send(dsrc.at[i, t], dall.at[slot], dsend.at[1], dsem.at[mine[i] - h + 1, t], where))
            dall[slot] = dsrc[i, t]
        for i in range(R):
            for k in range(C):
                att_src[i, k] = attended[i * W : (i + 1) * W, k * half : (k + 1) * half]
        stat2[me] = stat2_src[t]
        att_out[c, 0] = att_src[0, c]
        if R == 2:
            if T > 1:
                drain(dall.at[pl.ds(0, 2 * (T - 1))], dsend.at[0])
            for i in range(2):
                send_row(i, outer, [0], dsend.at[2])

    if S > 4:
        pl.when(attends & jnp.logical_not(at_edge))(lambda: attend(1))
    pl.when(at_edge)(lambda: attend(2))
    act[0:2] = jnp.zeros((2,) + act.shape[1:], BF16)
    gain2 = jnp.concatenate([gall[k, 1] for k in range(C)], axis=1)

    rows = [(0, h > 0, h == 1), (1, h >= 0, attends), (2, h < S - 1, h == S - 2)]

    def forward(k):
        for row, there, made_here in rows:

            @pl.when(there & jnp.logical_not(made_here & (t == k)))
            def _():
                slot = row * NF + k * C + c
                drain(dall.at[slot], direct_sem.at[row, k])
                mates(lambda where: send(dall.at[slot], dall.at[slot], share_sem, dsem.at[row, k], where))


    forward(0)
    for k in range(1, T):
        pl.when(t < k)(lambda: forward(k))

    @pl.when(jnp.logical_not(attends))
    def _():
        drain(stat2.at[pl.ds(0, attending)], s2sem)

    @pl.when(attends)
    def _():
        drain(stat2.at[pl.ds(0, attending - 1)], s2sem)
        send_attended(0, other, h, other)

    @pl.when(at_edge)
    def _():
        for k in range(C):
            send_attended(1, k, h + side, k)


    def sliced(v):
        out = v[:, 0:Kc]
        for k in range(1, T):
            out = jnp.where(t == k, v[:, k * Kc : (k + 1) * Kc], out)
        return out

    mean2, scale2 = slice_moments(jnp.sum(stat2[0:attending], axis=0), population)
    factor2 = scale2 * sliced(gain2)
    column = lax.broadcasted_iota(jnp.int32, (W, Kc), 0)

    def activate(row, k):
        for f in range(k * C, (k + 1) * C):
            v = (dall[row * NF + f].astype(F32) - mean2) * factor2
            a = v / (1.0 + jnp.exp(-v))
            left = jnp.where(column == 0, 0.0, pltpu.roll(a, 1, 0))
            right = jnp.where(column == W - 1, 0.0, pltpu.roll(a, W - 1, 0))
            for e, piece in enumerate((left, a, right)):
                place = row * 3 + e
                act[f + 2, :, place * Kc : (place + 1) * Kc] = piece.astype(BF16)

    skips = (3 * Kc) % LANES == 0

    def blank(row):
        act[2:, :, row * 3 * Kc : (row + 1) * 3 * Kc] = jnp.zeros((NF, W, 3 * Kc), BF16)

    if not skips:
        pl.when(h == 0)(lambda: blank(0))
        pl.when(h == S - 1)(lambda: blank(2))

    def block_in(k):
        if k:
            pl.when(t >= k)(lambda: forward(k))
        for row, there, _ in rows:

            @pl.when(there)
            def _():
                drain(dall.at[pl.ds(0, C - 1)], dsem.at[row, k])
                activate(row, k)

    wide = half // CHUNKS

    def product(to, b0, b1, chunk):
        total = None
        taps = slice(b0 * 3 * Kc, b1 * 3 * Kc)
        for a in range(0 if to else max(0, 3 - C), 3):
            window = act[to * C + a : to * C + a + C, :, taps].reshape(C * W, (b1 - b0) * 3 * Kc)
            weight = wc[a, taps, chunk * wide : (chunk + 1) * wide]
            term = jnp.dot(window, weight, preferred_element_type=F32)
            total = term if total is None else total + term
        return total

    if not skips:
        edges = [(t >= 0, 0, 3)]
    else:
        edges = [(h == 0, 1, 3), (h == S - 1, 0, 2), (attends, 0, 3)]

    def convolve(to, store):
        for here, b0, b1 in edges:

            @pl.when(here)
            def _():
                for chunk in range(CHUNKS):
                    store(chunk, product(to, b0, b1, chunk))

    def convolve_away(to):
        away = lax.rem(to - t + T, T) - 1

        def store(chunk, value):
            part_src[away, chunk] = value.astype(BF16)
            send(part_src.at[away, chunk], part.at[away, chunk], psend, psem.at[away, chunk], (g, h, to, c))

        convolve(to, store)

    def keep(chunk, value):
        own_total[chunk] = value

    loads[4].wait()
    for k in range(T):
        block_in(k)
        pl.when(t != k)(lambda: convolve_away(k))

    for k in range(T):
        pl.when(t == k)(lambda: convolve(k, keep))

    @pl.when(attends)
    def _():
        drain(att_in.at[pl.ds(0, C - 1)], asem)
        att_out[other, 0] = att_in[other]
        drain(xall.at[pl.ds(0, (S - 2) * C - 1)], xsend)
        drain(stat2.at[pl.ds(0, S * T * C - 1)], s2send)

    @pl.when(jnp.logical_not(attends))
    def _():
        drain(att_in, asem)
        for k in range(C):
            att_out[k, 0] = att_in[k]
        drain(xall.at[pl.ds(0, (S - 2) * C)], xsend)
        drain(dall.at[pl.ds(0, 2 * T * (C - 1))], share_sem)

    for r in range(S):

        @pl.when(h == r)
        def _():
            below = max(r - 1, 0) if r < S - 1 else S - 2
            level = (T - 1 if r == 0 else T * C - 1) if r < S - 1 else 0
            above = max(S - 2 - r, 0)
            drain(stat1.at[pl.ds(0, below * T * C + level + above * C)], s1send)

    @pl.when(attends & jnp.logical_not(at_edge))
    def _():
        drain(dall.at[pl.ds(0, 3 * T + C - 2)], dsend.at[1])
        drain(dall.at[pl.ds(0, (3 * T - 1) * (C - 1))], share_sem)
        drain(att_src.at[0, 0], asend)

    @pl.when(at_edge)
    def _():
        drain(dall.at[pl.ds(0, 2)], dsend.at[2])
        drain(dall.at[pl.ds(0, 3 * T + 2 * C - 4)], dsend.at[1])
        drain(dall.at[pl.ds(0, (3 * T - 2) * (C - 1))], share_sem)
        drain(xall.at[pl.ds(0, C + 1)], asend)

    drain(gall.at[pl.ds(0, C - 1)], gsend)
    for chunk in range(CHUNKS):
        total = own_total[chunk]
        for dt in range(1, T):
            drain(part.at[dt - 1, chunk], psem.at[dt - 1, chunk])
            total = total + part[dt - 1, chunk].astype(F32)
        conv_out[:, 0, :, chunk * wide : (chunk + 1) * wide] = total.reshape(C, W, wide).astype(BF16)
    if T > 1:
        drain(part_src, psend)


def slice_moments(totals, population):
    width = totals.shape[1]
    if width == LANES:
        return moments([totals], population)
    mean, scale = moments([jnp.concatenate([totals] * (LANES // width), axis=1)], population)
    return mean[:, :width], scale[:, :width]


def hand_over(att_in, conv_in, att_out, conv_out):
    att_out[...] = att_in[...]
    conv_out[...] = conv_in[...]


def on_device(S, T, C, x, g1, g2, wq, wk, wv, wo, wc):
    frames, rows, W, half = x.shape
    assert frames == C and rows == 1 and half * C == D
    Kc = wc.shape[3]
    assert Kc * T == D and S > 3
    n, NF = S * T * C, T * C
    wide = half // CHUNKS
    wc = wc.reshape(3, 9 * Kc, half)
    vmem = pl.BlockSpec(memory_space=pltpu.VMEM)
    hbm = pl.BlockSpec(memory_space=pl.ANY)
    out = jax.ShapeDtypeStruct(x.shape, BF16)
    dma = pltpu.SemaphoreType.DMA
    kept = pltpu.VMEM(x.shape, BF16)
    links = max(T - 1, 1)
    stats = (2 * max(Kc // LANES, 1), min(Kc, LANES))
    results = pl.pallas_call(
        functools.partial(kernel, S, T, C, W),
        out_shape=(kept, kept),
        in_specs=[hbm] * 8,
        out_specs=(vmem, vmem),
        scratch_shapes=[
            pltpu.VMEM(x.shape, BF16),
            pltpu.VMEM((3, D, D), BF16),
            pltpu.VMEM((D, D), BF16),
            pltpu.VMEM(wc.shape, BF16),
            pltpu.VMEM((half // 64, LANES), F32),
            pltpu.VMEM((half // 64, LANES), F32),
            pltpu.VMEM((n, half // 64, LANES), F32),
            pltpu.VMEM((T, *stats), F32),
            pltpu.VMEM((n, *stats), F32),
            pltpu.VMEM((C, 2, 1, half), F32),
            pltpu.VMEM((S * C, W, half), BF16),
            pltpu.VMEM((S, W, D), BF16),
            pltpu.VMEM((S * W, D), BF16),
            pltpu.VMEM((S * W, D), BF16),
            pltpu.VMEM((2, C, W, half), BF16),
            pltpu.VMEM((C, W, half), BF16),
            pltpu.VMEM((2, T, W, Kc), BF16),
            pltpu.VMEM((3 * NF, W, Kc), BF16),
            pltpu.VMEM((NF + 2, W, 9 * Kc), BF16),
            pltpu.VMEM((CHUNKS, C * W, wide), F32),
            pltpu.VMEM((links, CHUNKS, C * W, wide), BF16),
            pltpu.VMEM((links, CHUNKS, C * W, wide), BF16),
            dma((2,)),
            dma((3,)),
            pltpu.SemaphoreType.REGULAR((S - 1,)),
            dma(()),
            dma(()),
            dma(()),
            dma(()),
            dma(()),
            dma(()),
            dma((S,)),
            dma(()),
            dma(()),
            dma(()),
            dma(()),
            dma((3,)),
            dma((3, T)),
            dma((3, T)),
            dma(()),
            dma(()),
            dma((links, CHUNKS)),
        ],
        compiler_params=pltpu.CompilerParams(collective_id=0, has_side_effects=True),
    )(x, g1.reshape(1, half), g2.reshape(1, half), wq, wk, wv, wo, wc)
    return pl.pallas_call(
        hand_over, out_shape=(out, out), in_specs=[vmem] * 2, out_specs=(vmem, vmem),
    )(*[pltpu.with_memory_space_constraint(r, pltpu.VMEM) for r in results])


def solution(mesh):
    S, T, C = mesh.shape["space"], mesh.shape["tm"], mesh.shape["chan"]
    placed = (
        P(("groups", "tm"), "space", None, "chan"),
        P("chan"),
        P("chan"),
        P(),
        P(),
        P(),
        P(),
        P(None, None, None, "tm", "chan"),
    )
    return jax.shard_map(
        functools.partial(on_device, S, T, C),
        mesh=mesh,
        in_specs=placed,
        out_specs=(
            P(("groups", "tm"), "space", None, "chan"),
            P(("groups", "tm"), "space", None, "chan"),
        ),
        check_vma=False,
    )
```

```python
import functools

import jax
import jax.numpy as jnp
from jax import lax
from jax.experimental import pallas as pl
from jax.experimental.pallas import tpu as pltpu
from jax.sharding import PartitionSpec as P

D = 512
NGROUP = 32
EPSILON = 1e-06
LANES = 128
CHUNKS = 2
GROUP = D // NGROUP
MESH = pl.DeviceIdType.MESH
F32 = jnp.float32
BF16 = jnp.bfloat16


def group_total(v):
    lane = lax.broadcasted_iota(jnp.int32, v.shape, 1)
    width = v.shape[1]
    step = 1
    while step < GROUP:
        place = (lane // step) % 4
        terms = [v]
        for d in range(1, 4):
            terms.append(jnp.where(place < 4 - d, pltpu.roll(v, width - d * step, 1), 0.0))
            terms.append(jnp.where(place >= d, pltpu.roll(v, d * step, 1), 0.0))
        while len(terms) > 1:
            terms = [sum(terms[i : i + 2]) for i in range(0, len(terms), 2)]
        v = terms[0]
        step *= 4
    return v


def store_sums(ref, values):
    sums = jnp.sum(values, axis=0, keepdims=True)
    squares = jnp.sum(values * values, axis=0, keepdims=True)
    blocks, width = ref.shape[0] // 2, ref.shape[1]
    for b in range(blocks):
        ref[b : b + 1] = sums[:, b * width : (b + 1) * width]
        ref[blocks + b : blocks + b + 1] = squares[:, b * width : (b + 1) * width]


def moments(stacks, population):
    size = stacks[0].shape[0]
    blocks = size // 2
    count = len(stacks) * size
    rows = 8 * pl.cdiv(count, 8)
    padding = [jnp.zeros((rows - count, LANES), F32)] if rows > count else []
    grouped = group_total(jnp.concatenate([*stacks, *padding], axis=0)) / population
    variance = jnp.maximum(pltpu.roll(grouped, rows - blocks, 0) - grouped * grouped, 0.0)
    scale = lax.rsqrt(variance + EPSILON)
    picks = [i * size + b for i in range(len(stacks)) for b in range(blocks)]
    return [jnp.concatenate([v[k : k + 1] for k in picks], axis=1) for v in (grouped, scale)]


def kernel(
    S, T, C, W,
    x_hbm, g1, g2, wq_hbm, wk_hbm, wv_hbm, wo_hbm, wc_hbm,
    att_out, conv_out,
    x, projections, wo, wc,
    stat1_src, row_sum, stat1, stat2_src, stat2, gall,
    xall, tokens, keyed, valued, att_src, att_in, dsrc, dall, act, own_total, part_src, part,
    xload, wsem, insem, gsend, gsem, raw_sem, s1send, s1sem, xsend, xsem, s2send, s2sem,
    asend, asem, dsend, dsem, direct_sem, share_sem, psend, psem,
):
    g = lax.axis_index("groups")
    h = lax.axis_index("space")
    t = lax.axis_index("tm")
    c = lax.axis_index("chan")
    attending = (S - 2) * T * C
    me = (h * T + t) * C + c - T * C
    half = D // C
    Kc = D // T
    NF = T * C
    other = lax.rem(c + 1, C)
    attends = (h > 0) & (h < S - 1)
    at_edge = (h == 1) | (h == S - 2)
    side = jnp.where(h == 1, -1, 1)

    def rows_apart(sign, act_on):
        def row(d):
            @pl.when((h + sign * d >= 0) & (h + sign * d < S))
            def _():
                act_on(h + sign * d, d)

        pl.loop(1, S, unroll=S <= 4)(row)

    def row_devices(r, act_on):
        for dt in range(T):
            for dc in range(C):
                act_on((g, r, lax.rem(t + dt, T), lax.rem(c + dc, C)))

    def row_where(r, sign, act_on):
        for dt in range(1, T):

            @pl.when((t + sign * dt >= 0) & (t + sign * dt < T))
            def _():
                for dc in range(C):
                    act_on((g, r, t + sign * dt, lax.rem(c + dc, C)))

    def beside(sign, act_on):
        row_where(h, sign, act_on)

    def mates(act_on):
        for dc in range(1, C):
            act_on((g, h, t, lax.rem(c + dc, C)))

    def signal(sem):
        return lambda where: pl.semaphore_signal(sem, inc=1, device_id=where, device_id_type=MESH)

    def drain(ref, sem):
        pltpu.make_async_copy(ref, ref, sem).wait()

    def send(src, dst, sends, recvs, where):
        copy = pltpu.make_async_remote_copy(
            src_ref=src, dst_ref=dst, send_sem=sends, recv_sem=recvs, device_id=where, device_id_type=MESH,
        )
        copy.start()

    x_load = pltpu.make_async_copy(x_hbm, x, xload.at[0])
    x_load.start()
    for k, gain in enumerate((g1, g2)):
        pltpu.make_async_copy(gain, gall.at[c, k], xload.at[1]).start()
    stat1[...] = jnp.zeros(stat1.shape, F32)
    barrier = pltpu.get_barrier_semaphore()
    mates(signal(barrier))
    beside(1, signal(barrier))

    def column(r, act_on):
        for dc in range(C):
            act_on((g, r, t, lax.rem(c + dc, C)))

    def greet(r, d):
        column(r, signal(barrier))
        row_where(r, 1, signal(barrier))

    rows_apart(1, greet)
    pl.semaphore_wait(barrier, (h * (t + 1) + t) * C + C - 1)
    pl.when(h < S - 1)(lambda: rows_apart(-1, lambda r, d: column(r, signal(insem.at[d]))))
    beside(-1, signal(insem.at[0]))

    loads = [
        pltpu.make_async_copy(src, dst, wsem.at[i])
        for i, (src, dst) in zip((0, 0, 0, 1, 2), [(wq_hbm, projections.at[0]), (wk_hbm, projections.at[1]), (wv_hbm, projections.at[2]), (wo_hbm, wo), (wc_hbm, wc)])
    ]

    @pl.when(attends)
    def _():
        for load in loads[:4]:
            load.start()

    loads[4].start()

    x_load.wait()
    store_sums(stat1_src, x[...].reshape(C * W, half).astype(F32))
    at = (h * T + t) * C + c

    def send_stat(where, src=stat1_src, recvs=s1sem):
        send(src, stat1.at[at], s1send, recvs, where)

    def same_row(sign):
        for dt in range(1, T):

            @pl.when((t + sign * dt >= 0) & (t + sign * dt < T))
            def _():
                send_stat((g, h, t + sign * dt, c), recvs=raw_sem)

                @pl.when(attends)
                def _():
                    for dc in range(1, C):
                        send_stat((g, h, t + sign * dt, lax.rem(c + dc, C)))

    def send_x(r, dc):
        frame = lax.rem(c + dc, C)
        send(x.at[frame, 0], xall.at[h * C + c], xsend, xsem.at[h], (g, r, t, frame))

    def column_x(r):
        for dc in range(C):
            send_x(r, dc)

    for r in range(1, S - 1):

        @pl.when(r < h)
        def _():
            column(r, send_stat)
            row_where(r, -1, send_stat)

    pl.when(h < S - 1)(lambda: same_row(-1))
    stat1[at] = stat1_src[...]

    @pl.when(attends)
    def _():
        mates(send_stat)
        xall[h * C + c] = x[c, 0]
        for dc in range(1, C):
            send_x(h, dc)

    for r in range(1, S - 1):
        pl.when(r < h)(lambda: column_x(r))

    drain(gall.at[c], xload.at[1])
    mates(lambda where: send(gall.at[c], gall.at[c], gsend, gsem, where))

    @pl.when(h < S - 2)
    def _():
        pl.semaphore_wait(insem.at[1], C)
        column_x(h + 1)

    @pl.when(t < T - 1)
    def _():
        pl.semaphore_wait(insem.at[0], (T - 1 - t) * C)
        for r in range(1, S - 1):
            pl.when(r < h)(lambda: row_where(r, 1, send_stat))
        pl.when(h < S - 1)(lambda: same_row(1))

    @pl.when(h < S - 1)
    def _():
        if T > 1:
            drain(stat1.at[pl.ds(0, T - 1)], raw_sem)

    @pl.when(h < S - 2)
    def _():
        total = stat1_src[...]
        for dt in range(1, T):
            total = total + stat1[(h * T + lax.rem(t + dt, T)) * C + c]
        row_sum[...] = total

        def send_sum(where):
            send_stat(where, src=row_sum)

        column(h + 1, send_sum)

        def upward(d):
            @pl.when(h + d < S - 1)
            def _():
                pl.semaphore_wait(insem.at[d], C)
                column(h + d, send_sum)
                column_x(h + d)

        pl.loop(2, S - 1, unroll=S <= 4)(upward)

    drain(gall.at[pl.ds(0, C - 1)], gsem)
    population = float(S * T * C * W * GROUP)
    frame_at = t * C + c

    def send_attended(i, k, r, core):
        send(att_src.at[i, k], att_in.at[c], asend, asem, (g, r, t, core))

    def attend(R):
        outer = h + side
        mine = [h, outer][:R]
        skipped = jnp.where(h == 1, R, 0) if R == 2 else None

        def rest(i):
            return i + skipped if R == 2 else i + jnp.where(i >= h, 1, 0)

        def slots_in(r):
            drain(xall.at[pl.ds(r * C, C)], xsem.at[r])

        for r in range(1, S - 1):

            @pl.when(h == r)
            def _():
                drain(stat1.at[pl.ds(0, r * C + T * (C - 1) + (S - 1 - r) * T * C)], s1sem)

        drain(xall.at[pl.ds(0, C - 1)], xsem.at[h])
        if R == 2:
            slots_in(outer)
        for i in range(S - R):
            slots_in(rest(i))
        drain(projections, wsem.at[0])
        drain(wo, wsem.at[1])
        totals = jnp.sum(stat1[...].reshape(S * T, C, *stat1.shape[1:]), axis=0)
        mean1, scale1 = moments([totals[k] for k in range(C)], population)
        factor1 = scale1 * jnp.concatenate([gall[k, 0] for k in range(C)], axis=1)

        def row_tokens(r):
            pieces = []
            for k in range(C):
                lanes = slice(k * half, (k + 1) * half)
                value = xall[r * C + k].astype(F32)
                pieces.append(((value - mean1[:, lanes]) * factor1[:, lanes]).astype(BF16))
            return jnp.concatenate(pieces, axis=1)

        def project(weight, first, stop):
            rows = tokens[first:stop].reshape((stop - first) * W, D)
            return jnp.dot(rows, weight[...], preferred_element_type=F32).astype(BF16)

        for i in range(R):
            tokens[i] = row_tokens(mine[i])
        for i in range(S - R):
            tokens[R + i] = row_tokens(rest(i))
        queries = project(projections.at[0], 0, R)
        keyed[...] = project(projections.at[1], 0, S)
        valued[...] = project(projections.at[2], 0, S)

        scores = lax.dot_general(
            queries, keyed[...], (((1,), (1,)), ((), ())), preferred_element_type=F32
        ) * (D ** (-0.5))
        weights = jnp.exp(scores - jnp.max(scores, axis=1, keepdims=True))
        mass = jnp.sum(weights, axis=1, keepdims=True)
        mixed = jnp.dot(weights.astype(BF16), valued[...], preferred_element_type=F32)
        mixed = (mixed * (1.0 / mass)).astype(BF16)
        attended = jnp.dot(mixed, wo[...], preferred_element_type=F32).astype(BF16)

        source = jnp.concatenate(
            [jnp.concatenate([xall[r * C + k] for k in range(C)], axis=1) for r in mine], axis=0
        ).astype(F32)
        resid = (source - mean1) + attended.astype(F32)
        for i in range(R):
            for k in range(T):
                dsrc[i, k] = resid[i * W : (i + 1) * W, k * Kc : (k + 1) * Kc].astype(BF16)

        def send_row(i, r, columns, sends):
            for dt in columns:
                to = lax.rem(t + dt, T)
                row = mine[i] - r + 1
                send(
                    dsrc.at[i, to], dall.at[row * NF + frame_at], sends, direct_sem.at[row, t], (g, r, to, c),
                )

        others = range(1, T)
        for k in range(T):
            store_sums(stat2_src.at[k], resid[:, k * Kc : (k + 1) * Kc])

        def send_stat2(where):
            send(stat2_src.at[where[2]], stat2.at[me], s2send, s2sem, where)

        rows_apart(-1, lambda r, d: row_devices(r, send_stat2))
        rows_apart(1, lambda r, d: row_devices(r, send_stat2))
        beside(-1, send_stat2)
        beside(1, send_stat2)
        mates(send_stat2)
        if R == 2:
            for i in range(2):
                send_row(i, outer, others, dsend.at[0])

            def own_column():
                for i in range(2):
                    send_row(i, outer, [0], dsend.at[2])

            pl.when(t == 0)(own_column)
            send_row(0, h - side, [*others, 0], dsend.at[1])
        else:
            for r in (h - 1, h + 1):
                send_row(0, r, [*others, 0], dsend.at[1])
        for i in range(R):
            send_row(i, h, others, dsend.at[1])
            slot = (mine[i] - h + 1) * NF + frame_at
            mates(lambda where: send(dsrc.at[i, t], dall.at[slot], dsend.at[1], dsem.at[mine[i] - h + 1, t], where))
            dall[slot] = dsrc[i, t]
        for i in range(R):
            for k in range(C):
                att_src[i, k] = attended[i * W : (i + 1) * W, k * half : (k + 1) * half]
        stat2[me] = stat2_src[t]
        att_out[c, 0] = att_src[0, c]
        if R == 2:
            if T > 1:
                drain(dall.at[pl.ds(0, 2 * (T - 1))], dsend.at[0])
            pl.when(t > 0)(own_column)

    if S > 4:
        pl.when(attends & jnp.logical_not(at_edge))(lambda: attend(1))
    pl.when(at_edge)(lambda: attend(2))
    act[0:2] = jnp.zeros((2,) + act.shape[1:], BF16)
    gain2 = jnp.concatenate([gall[k, 1] for k in range(C)], axis=1)

    rows = [(0, h > 0, h == 1), (1, h >= 0, attends), (2, h < S - 1, h == S - 2)]

    def forward(k):
        for row, there, made_here in rows:

            @pl.when(there & jnp.logical_not(made_here & (t == k)))
            def _():
                slot = row * NF + k * C + c
                drain(dall.at[slot], direct_sem.at[row, k])
                mates(lambda where: send(dall.at[slot], dall.at[slot], share_sem, dsem.at[row, k], where))


    forward(0)

    @pl.when(jnp.logical_not(attends))
    def _():
        drain(stat2.at[pl.ds(0, attending)], s2sem)

    @pl.when(attends)
    def _():
        drain(stat2.at[pl.ds(0, attending - 1)], s2sem)
        send_attended(0, other, h, other)

    @pl.when(at_edge)
    def _():
        for k in range(C):
            send_attended(1, k, h + side, k)


    def sliced(v):
        out = v[:, 0:Kc]
        for k in range(1, T):
            out = jnp.where(t == k, v[:, k * Kc : (k + 1) * Kc], out)
        return out

    mean2, scale2 = slice_moments(jnp.sum(stat2[0:attending], axis=0), population)
    factor2 = scale2 * sliced(gain2)
    column = lax.broadcasted_iota(jnp.int32, (W, Kc), 0)
    for k in range(1, T):
        pl.when(t < k)(lambda: forward(k))


    def activate(row, k):
        for f in range(k * C, (k + 1) * C):
            v = (dall[row * NF + f].astype(F32) - mean2) * factor2
            a = v / (1.0 + jnp.exp(-v))
            left = jnp.where(column == 0, 0.0, pltpu.roll(a, 1, 0))
            right = jnp.where(column == W - 1, 0.0, pltpu.roll(a, W - 1, 0))
            for e, piece in enumerate((left, a, right)):
                place = row * 3 + e
                act[f + 2, :, place * Kc : (place + 1) * Kc] = piece.astype(BF16)

    skips = (3 * Kc) % LANES == 0

    def blank(row):
        act[2:, :, row * 3 * Kc : (row + 1) * 3 * Kc] = jnp.zeros((NF, W, 3 * Kc), BF16)

    if not skips:
        pl.when(h == 0)(lambda: blank(0))
        pl.when(h == S - 1)(lambda: blank(2))

    def block_in(k):
        if k:
            pl.when(t >= k)(lambda: forward(k))
        for row, there, _ in rows:

            @pl.when(there)
            def _():
                drain(dall.at[pl.ds(0, C - 1)], dsem.at[row, k])
                activate(row, k)

    wide = half // CHUNKS

    def product(to, b0, b1, chunk):
        total = None
        taps = slice(b0 * 3 * Kc, b1 * 3 * Kc)
        for a in range(0 if to else max(0, 3 - C), 3):
            window = act[to * C + a : to * C + a + C, :, taps].reshape(C * W, (b1 - b0) * 3 * Kc)
            weight = wc[a, taps, chunk * wide : (chunk + 1) * wide]
            term = jnp.dot(window, weight, preferred_element_type=F32)
            total = term if total is None else total + term
        return total

    if not skips:
        edges = [(t >= 0, 0, 3)]
    else:
        edges = [(h == 0, 1, 3), (h == S - 1, 0, 2), (attends, 0, 3)]

    def convolve(to, store):
        for here, b0, b1 in edges:

            @pl.when(here)
            def _():
                for chunk in range(CHUNKS):
                    store(chunk, product(to, b0, b1, chunk))

    def convolve_away(to):
        away = lax.rem(to - t + T, T) - 1

        def store(chunk, value):
            part_src[away, chunk] = value.astype(BF16)
            send(part_src.at[away, chunk], part.at[away, chunk], psend, psem.at[away, chunk], (g, h, to, c))

        convolve(to, store)

    def keep(chunk, value):
        own_total[chunk] = value

    loads[4].wait()
    for k in range(T):
        block_in(k)
        pl.when(t != k)(lambda: convolve_away(k))

    for k in range(T):
        pl.when(t == k)(lambda: convolve(k, keep))

    @pl.when(attends)
    def _():
        drain(att_in.at[pl.ds(0, C - 1)], asem)
        att_out[other, 0] = att_in[other]
        drain(xall.at[pl.ds(0, (S - 2) * C - 1)], xsend)
        drain(stat2.at[pl.ds(0, S * T * C - 1)], s2send)

    @pl.when(jnp.logical_not(attends))
    def _():
        drain(att_in, asem)
        for k in range(C):
            att_out[k, 0] = att_in[k]
        drain(xall.at[pl.ds(0, (S - 2) * C)], xsend)
        drain(dall.at[pl.ds(0, 2 * T * (C - 1))], share_sem)

    for r in range(S):

        @pl.when(h == r)
        def _():
            below = max(r - 1, 0) if r < S - 1 else S - 2
            level = (T - 1 if r == 0 else T * C - 1) if r < S - 1 else 0
            above = max(S - 2 - r, 0)
            drain(stat1.at[pl.ds(0, below * T * C + level + above * C)], s1send)

    @pl.when(attends & jnp.logical_not(at_edge))
    def _():
        drain(dall.at[pl.ds(0, 3 * T + C - 2)], dsend.at[1])
        drain(dall.at[pl.ds(0, (3 * T - 1) * (C - 1))], share_sem)
        drain(att_src.at[0, 0], asend)

    @pl.when(at_edge)
    def _():
        drain(dall.at[pl.ds(0, 2)], dsend.at[2])
        drain(dall.at[pl.ds(0, 3 * T + 2 * C - 4)], dsend.at[1])
        drain(dall.at[pl.ds(0, (3 * T - 2) * (C - 1))], share_sem)
        drain(xall.at[pl.ds(0, C + 1)], asend)

    drain(gall.at[pl.ds(0, C - 1)], gsend)
    for chunk in range(CHUNKS):
        total = own_total[chunk]
        for dt in range(1, T):
            drain(part.at[dt - 1, chunk], psem.at[dt - 1, chunk])
            total = total + part[dt - 1, chunk].astype(F32)
        conv_out[:, 0, :, chunk * wide : (chunk + 1) * wide] = total.reshape(C, W, wide).astype(BF16)
    if T > 1:
        drain(part_src, psend)


def slice_moments(totals, population):
    width = totals.shape[1]
    if width == LANES:
        return moments([totals], population)
    mean, scale = moments([jnp.concatenate([totals] * (LANES // width), axis=1)], population)
    return mean[:, :width], scale[:, :width]


def hand_over(att_in, conv_in, att_out, conv_out):
    att_out[...] = att_in[...]
    conv_out[...] = conv_in[...]


def on_device(S, T, C, x, g1, g2, wq, wk, wv, wo, wc):
    frames, rows, W, half = x.shape
    assert frames == C and rows == 1 and half * C == D
    Kc = wc.shape[3]
    assert Kc * T == D and S > 3
    n, NF = S * T * C, T * C
    wide = half // CHUNKS
    wc = wc.reshape(3, 9 * Kc, half)
    vmem = pl.BlockSpec(memory_space=pltpu.VMEM)
    hbm = pl.BlockSpec(memory_space=pl.ANY)
    out = jax.ShapeDtypeStruct(x.shape, BF16)
    dma = pltpu.SemaphoreType.DMA
    kept = pltpu.VMEM(x.shape, BF16)
    links = max(T - 1, 1)
    stats = (2 * max(Kc // LANES, 1), min(Kc, LANES))
    results = pl.pallas_call(
        functools.partial(kernel, S, T, C, W),
        out_shape=(kept, kept),
        in_specs=[hbm] * 8,
        out_specs=(vmem, vmem),
        scratch_shapes=[
            pltpu.VMEM(x.shape, BF16),
            pltpu.VMEM((3, D, D), BF16),
            pltpu.VMEM((D, D), BF16),
            pltpu.VMEM(wc.shape, BF16),
            pltpu.VMEM((half // 64, LANES), F32),
            pltpu.VMEM((half // 64, LANES), F32),
            pltpu.VMEM((n, half // 64, LANES), F32),
            pltpu.VMEM((T, *stats), F32),
            pltpu.VMEM((n, *stats), F32),
            pltpu.VMEM((C, 2, 1, half), F32),
            pltpu.VMEM((S * C, W, half), BF16),
            pltpu.VMEM((S, W, D), BF16),
            pltpu.VMEM((S * W, D), BF16),
            pltpu.VMEM((S * W, D), BF16),
            pltpu.VMEM((2, C, W, half), BF16),
            pltpu.VMEM((C, W, half), BF16),
            pltpu.VMEM((2, T, W, Kc), BF16),
            pltpu.VMEM((3 * NF, W, Kc), BF16),
            pltpu.VMEM((NF + 2, W, 9 * Kc), BF16),
            pltpu.VMEM((CHUNKS, C * W, wide), F32),
            pltpu.VMEM((links, CHUNKS, C * W, wide), BF16),
            pltpu.VMEM((links, CHUNKS, C * W, wide), BF16),
            dma((2,)),
            dma((3,)),
            pltpu.SemaphoreType.REGULAR((S - 1,)),
            dma(()),
            dma(()),
            dma(()),
            dma(()),
            dma(()),
            dma(()),
            dma((S,)),
            dma(()),
            dma(()),
            dma(()),
            dma(()),
            dma((3,)),
            dma((3, T)),
            dma((3, T)),
            dma(()),
            dma(()),
            dma((links, CHUNKS)),
        ],
        compiler_params=pltpu.CompilerParams(collective_id=0, has_side_effects=True),
    )(x, g1.reshape(1, half), g2.reshape(1, half), wq, wk, wv, wo, wc)
    return pl.pallas_call(
        hand_over, out_shape=(out, out), in_specs=[vmem] * 2, out_specs=(vmem, vmem),
    )(*[pltpu.with_memory_space_constraint(r, pltpu.VMEM) for r in results])


def solution(mesh):
    S, T, C = mesh.shape["space"], mesh.shape["tm"], mesh.shape["chan"]
    placed = (
        P(("groups", "tm"), "space", None, "chan"),
        P("chan"),
        P("chan"),
        P(),
        P(),
        P(),
        P(),
        P(None, None, None, "tm", "chan"),
    )
    return jax.shard_map(
        functools.partial(on_device, S, T, C),
        mesh=mesh,
        in_specs=placed,
        out_specs=(
            P(("groups", "tm"), "space", None, "chan"),
            P(("groups", "tm"), "space", None, "chan"),
        ),
        check_vma=False,
    )
```

```python
import functools

import jax
import jax.numpy as jnp
from jax import lax
from jax.experimental import pallas as pl
from jax.experimental.pallas import tpu as pltpu
from jax.sharding import PartitionSpec as P

D = 512
NGROUP = 32
EPSILON = 1e-06
LANES = 128
CHUNKS = 2
GROUP = D // NGROUP
MESH = pl.DeviceIdType.MESH
F32 = jnp.float32
BF16 = jnp.bfloat16


def group_total(v):
    lane = lax.broadcasted_iota(jnp.int32, v.shape, 1)
    width = v.shape[1]
    step = 1
    while step < GROUP:
        place = (lane // step) % 4
        terms = [v]
        for d in range(1, 4):
            terms.append(jnp.where(place < 4 - d, pltpu.roll(v, width - d * step, 1), 0.0))
            terms.append(jnp.where(place >= d, pltpu.roll(v, d * step, 1), 0.0))
        while len(terms) > 1:
            terms = [sum(terms[i : i + 2]) for i in range(0, len(terms), 2)]
        v = terms[0]
        step *= 4
    return v


def store_sums(ref, values):
    sums = jnp.sum(values, axis=0, keepdims=True)
    squares = jnp.sum(values * values, axis=0, keepdims=True)
    blocks, width = ref.shape[0] // 2, ref.shape[1]
    for b in range(blocks):
        ref[b : b + 1] = sums[:, b * width : (b + 1) * width]
        ref[blocks + b : blocks + b + 1] = squares[:, b * width : (b + 1) * width]


def moments(stacks, population):
    size = stacks[0].shape[0]
    blocks = size // 2
    count = len(stacks) * size
    rows = 8 * pl.cdiv(count, 8)
    padding = [jnp.zeros((rows - count, LANES), F32)] if rows > count else []
    grouped = group_total(jnp.concatenate([*stacks, *padding], axis=0)) / population
    variance = jnp.maximum(pltpu.roll(grouped, rows - blocks, 0) - grouped * grouped, 0.0)
    scale = lax.rsqrt(variance + EPSILON)
    picks = [i * size + b for i in range(len(stacks)) for b in range(blocks)]
    return [jnp.concatenate([v[k : k + 1] for k in picks], axis=1) for v in (grouped, scale)]


def kernel(
    S, T, C, W,
    x_hbm, g1, g2, wq_hbm, wk_hbm, wv_hbm, wo_hbm, wc_hbm,
    att_out, conv_out,
    x, projections, wo, wc,
    stat1_src, row_sum, stat1, stat2_src, stat2, gall,
    xall, tokens, keyed, valued, att_src, att_in, dsrc, dall, act, own_total, part_src, part,
    xload, wsem, insem, gsend, gsem, raw_sem, s1send, s1sem, xsend, xsem, s2send, s2sem,
    asend, asem, dsend, dsem, direct_sem, share_sem, psend, psem,
):
    g = lax.axis_index("groups")
    h = lax.axis_index("space")
    t = lax.axis_index("tm")
    c = lax.axis_index("chan")
    attending = (S - 2) * T * C
    me = (h * T + t) * C + c - T * C
    half = D // C
    Kc = D // T
    NF = T * C
    other = lax.rem(c + 1, C)
    attends = (h > 0) & (h < S - 1)
    at_edge = (h == 1) | (h == S - 2)
    side = jnp.where(h == 1, -1, 1)

    def rows_apart(sign, act_on):
        def row(d):
            @pl.when((h + sign * d >= 0) & (h + sign * d < S))
            def _():
                act_on(h + sign * d, d)

        pl.loop(1, S, unroll=S <= 4)(row)

    def row_devices(r, act_on):
        for dt in range(T):
            for dc in range(C):
                act_on((g, r, lax.rem(t + dt, T), lax.rem(c + dc, C)))

    def row_where(r, sign, act_on):
        for dt in range(1, T):

            @pl.when((t + sign * dt >= 0) & (t + sign * dt < T))
            def _():
                for dc in range(C):
                    act_on((g, r, t + sign * dt, lax.rem(c + dc, C)))

    def beside(sign, act_on):
        row_where(h, sign, act_on)

    def mates(act_on):
        for dc in range(1, C):
            act_on((g, h, t, lax.rem(c + dc, C)))

    def signal(sem):
        return lambda where: pl.semaphore_signal(sem, inc=1, device_id=where, device_id_type=MESH)

    def drain(ref, sem):
        pltpu.make_async_copy(ref, ref, sem).wait()

    def send(src, dst, sends, recvs, where):
        copy = pltpu.make_async_remote_copy(
            src_ref=src, dst_ref=dst, send_sem=sends, recv_sem=recvs, device_id=where, device_id_type=MESH,
        )
        copy.start()

    x_load = pltpu.make_async_copy(x_hbm, x, xload.at[0])
    x_load.start()
    for k, gain in enumerate((g1, g2)):
        pltpu.make_async_copy(gain, gall.at[c, k], xload.at[1]).start()
    stat1[...] = jnp.zeros(stat1.shape, F32)
    barrier = pltpu.get_barrier_semaphore()
    mates(signal(barrier))
    beside(1, signal(barrier))

    def column(r, act_on):
        for dc in range(C):
            act_on((g, r, t, lax.rem(c + dc, C)))

    def greet(r, d):
        column(r, signal(barrier))
        row_where(r, 1, signal(barrier))

    rows_apart(1, greet)
    pl.semaphore_wait(barrier, (h * (t + 1) + t) * C + C - 1)
    pl.when(h < S - 1)(lambda: rows_apart(-1, lambda r, d: column(r, signal(insem.at[d]))))
    beside(-1, signal(insem.at[0]))

    loads = [
        pltpu.make_async_copy(src, dst, wsem.at[i])
        for i, (src, dst) in zip((0, 0, 0, 1, 2), [(wq_hbm, projections.at[0]), (wk_hbm, projections.at[1]), (wv_hbm, projections.at[2]), (wo_hbm, wo), (wc_hbm, wc)])
    ]


    x_load.wait()
    store_sums(stat1_src, x[...].reshape(C * W, half).astype(F32))
    at = (h * T + t) * C + c

    def send_stat(where, src=stat1_src, recvs=s1sem):
        send(src, stat1.at[at], s1send, recvs, where)

    def same_row(sign):
        for dt in range(1, T):

            @pl.when((t + sign * dt >= 0) & (t + sign * dt < T))
            def _():
                send_stat((g, h, t + sign * dt, c), recvs=raw_sem)

                @pl.when(attends)
                def _():
                    for dc in range(1, C):
                        send_stat((g, h, t + sign * dt, lax.rem(c + dc, C)))

    def send_x(r, dc):
        frame = lax.rem(c + dc, C)
        send(x.at[frame, 0], xall.at[h * C + c], xsend, xsem.at[h], (g, r, t, frame))

    def column_x(r):
        for dc in range(C):
            send_x(r, dc)

    for r in range(1, S - 1):

        @pl.when(r < h)
        def _():
            column(r, send_stat)
            row_where(r, -1, send_stat)

    pl.when(h < S - 1)(lambda: same_row(-1))
    stat1[at] = stat1_src[...]

    @pl.when(attends)
    def _():
        mates(send_stat)
        xall[h * C + c] = x[c, 0]
        for dc in range(1, C):
            send_x(h, dc)

    for r in range(1, S - 1):
        pl.when(r < h)(lambda: column_x(r))

    drain(gall.at[c], xload.at[1])
    mates(lambda where: send(gall.at[c], gall.at[c], gsend, gsem, where))
    @pl.when(attends)
    def _():
        for load in loads[:4]:
            load.start()

    loads[4].start()

    @pl.when(h < S - 2)
    def _():
        pl.semaphore_wait(insem.at[1], C)
        column_x(h + 1)

    @pl.when(t < T - 1)
    def _():
        pl.semaphore_wait(insem.at[0], (T - 1 - t) * C)
        for r in range(1, S - 1):
            pl.when(r < h)(lambda: row_where(r, 1, send_stat))
        pl.when(h < S - 1)(lambda: same_row(1))

    @pl.when(h < S - 1)
    def _():
        if T > 1:
            drain(stat1.at[pl.ds(0, T - 1)], raw_sem)

    @pl.when(h < S - 2)
    def _():
        total = stat1_src[...]
        for dt in range(1, T):
            total = total + stat1[(h * T + lax.rem(t + dt, T)) * C + c]
        row_sum[...] = total

        def send_sum(where):
            send_stat(where, src=row_sum)

        column(h + 1, send_sum)

        def upward(d):
            @pl.when(h + d < S - 1)
            def _():
                pl.semaphore_wait(insem.at[d], C)
                column(h + d, send_sum)
                column_x(h + d)

        pl.loop(2, S - 1, unroll=S <= 4)(upward)

    drain(gall.at[pl.ds(0, C - 1)], gsem)
    population = float(S * T * C * W * GROUP)
    frame_at = t * C + c

    def send_attended(i, k, r, core):
        send(att_src.at[i, k], att_in.at[c], asend, asem, (g, r, t, core))

    def attend(R):
        outer = h + side
        mine = [h, outer][:R]
        skipped = jnp.where(h == 1, R, 0) if R == 2 else None

        def rest(i):
            return i + skipped if R == 2 else i + jnp.where(i >= h, 1, 0)

        def slots_in(r):
            drain(xall.at[pl.ds(r * C, C)], xsem.at[r])

        for r in range(1, S - 1):

            @pl.when(h == r)
            def _():
                drain(stat1.at[pl.ds(0, r * C + T * (C - 1) + (S - 1 - r) * T * C)], s1sem)

        drain(xall.at[pl.ds(0, C - 1)], xsem.at[h])
        if R == 2:
            slots_in(outer)
        for i in range(S - R):
            slots_in(rest(i))
        drain(projections, wsem.at[0])
        drain(wo, wsem.at[1])
        totals = jnp.sum(stat1[...].reshape(S * T, C, *stat1.shape[1:]), axis=0)
        mean1, scale1 = moments([totals[k] for k in range(C)], population)
        factor1 = scale1 * jnp.concatenate([gall[k, 0] for k in range(C)], axis=1)

        def row_tokens(r):
            pieces = []
            for k in range(C):
                lanes = slice(k * half, (k + 1) * half)
                value = xall[r * C + k].astype(F32)
                pieces.append(((value - mean1[:, lanes]) * factor1[:, lanes]).astype(BF16))
            return jnp.concatenate(pieces, axis=1)

        def project(weight, first, stop):
            rows = tokens[first:stop].reshape((stop - first) * W, D)
            return jnp.dot(rows, weight[...], preferred_element_type=F32).astype(BF16)

        for i in range(R):
            tokens[i] = row_tokens(mine[i])
        for i in range(S - R):
            tokens[R + i] = row_tokens(rest(i))
        queries = project(projections.at[0], 0, R)
        keyed[...] = project(projections.at[1], 0, S)
        valued[...] = project(projections.at[2], 0, S)

        scores = lax.dot_general(
            queries, keyed[...], (((1,), (1,)), ((), ())), preferred_element_type=F32
        ) * (D ** (-0.5))
        weights = jnp.exp(scores - jnp.max(scores, axis=1, keepdims=True))
        mass = jnp.sum(weights, axis=1, keepdims=True)
        mixed = jnp.dot(weights.astype(BF16), valued[...], preferred_element_type=F32)
        mixed = (mixed * (1.0 / mass)).astype(BF16)
        attended = jnp.dot(mixed, wo[...], preferred_element_type=F32).astype(BF16)

        source = jnp.concatenate(
            [jnp.concatenate([xall[r * C + k] for k in range(C)], axis=1) for r in mine], axis=0
        ).astype(F32)
        resid = (source - mean1) + attended.astype(F32)
        for i in range(R):
            for k in range(T):
                dsrc[i, k] = resid[i * W : (i + 1) * W, k * Kc : (k + 1) * Kc].astype(BF16)

        def send_row(i, r, columns, sends):
            for dt in columns:
                to = lax.rem(t + dt, T)
                row = mine[i] - r + 1
                send(
                    dsrc.at[i, to], dall.at[row * NF + frame_at], sends, direct_sem.at[row, t], (g, r, to, c),
                )

        others = range(1, T)
        for k in range(T):
            store_sums(stat2_src.at[k], resid[:, k * Kc : (k + 1) * Kc])

        def send_stat2(where):
            send(stat2_src.at[where[2]], stat2.at[me], s2send, s2sem, where)

        if R == 2:
            row_devices(outer, send_stat2)
            for i in range(2):
                send_row(i, outer, others, dsend.at[0])

            def own_column():
                for i in range(2):
                    send_row(i, outer, [0], dsend.at[2])

            pl.when(t == 0)(own_column)
        def beyond_outer(r, d):
            if R == 2:
                pl.when(r != outer)(lambda: row_devices(r, send_stat2))
            else:
                row_devices(r, send_stat2)

        rows_apart(-1, beyond_outer)
        rows_apart(1, beyond_outer)
        beside(-1, send_stat2)
        beside(1, send_stat2)
        mates(send_stat2)
        if R == 2:
            send_row(0, h - side, [*others, 0], dsend.at[1])
        else:
            for r in (h - 1, h + 1):
                send_row(0, r, [*others, 0], dsend.at[1])
        for i in range(R):
            send_row(i, h, others, dsend.at[1])
            slot = (mine[i] - h + 1) * NF + frame_at
            mates(lambda where: send(dsrc.at[i, t], dall.at[slot], dsend.at[1], dsem.at[mine[i] - h + 1, t], where))
            dall[slot] = dsrc[i, t]
        for i in range(R):
            for k in range(C):
                att_src[i, k] = attended[i * W : (i + 1) * W, k * half : (k + 1) * half]
        stat2[me] = stat2_src[t]
        att_out[c, 0] = att_src[0, c]
        if R == 2:
            if T > 1:
                drain(dall.at[pl.ds(0, 2 * (T - 1))], dsend.at[0])
            pl.when(t > 0)(own_column)

    if S > 4:
        pl.when(attends & jnp.logical_not(at_edge))(lambda: attend(1))
    pl.when(at_edge)(lambda: attend(2))
    act[0:2] = jnp.zeros((2,) + act.shape[1:], BF16)
    gain2 = jnp.concatenate([gall[k, 1] for k in range(C)], axis=1)

    rows = [(0, h > 0, h == 1), (1, h >= 0, attends), (2, h < S - 1, h == S - 2)]

    def forward(k):
        for row, there, made_here in rows:

            @pl.when(there & jnp.logical_not(made_here & (t == k)))
            def _():
                slot = row * NF + k * C + c
                drain(dall.at[slot], direct_sem.at[row, k])
                mates(lambda where: send(dall.at[slot], dall.at[slot], share_sem, dsem.at[row, k], where))


    forward(0)

    @pl.when(jnp.logical_not(attends))
    def _():
        drain(stat2.at[pl.ds(0, attending)], s2sem)

    @pl.when(attends)
    def _():
        drain(stat2.at[pl.ds(0, attending - 1)], s2sem)
        send_attended(0, other, h, other)

    @pl.when(at_edge)
    def _():
        for k in range(C):
            send_attended(1, k, h + side, k)


    def sliced(v):
        out = v[:, 0:Kc]
        for k in range(1, T):
            out = jnp.where(t == k, v[:, k * Kc : (k + 1) * Kc], out)
        return out

    mean2, scale2 = slice_moments(jnp.sum(stat2[0:attending], axis=0), population)
    factor2 = scale2 * sliced(gain2)
    column = lax.broadcasted_iota(jnp.int32, (W, Kc), 0)

    def activate(row, k):
        for f in range(k * C, (k + 1) * C):
            v = (dall[row * NF + f].astype(F32) - mean2) * factor2
            a = v / (1.0 + jnp.exp(-v))
            left = jnp.where(column == 0, 0.0, pltpu.roll(a, 1, 0))
            right = jnp.where(column == W - 1, 0.0, pltpu.roll(a, W - 1, 0))
            for e, piece in enumerate((left, a, right)):
                place = row * 3 + e
                act[f + 2, :, place * Kc : (place + 1) * Kc] = piece.astype(BF16)

    skips = (3 * Kc) % LANES == 0

    def blank(row):
        act[2:, :, row * 3 * Kc : (row + 1) * 3 * Kc] = jnp.zeros((NF, W, 3 * Kc), BF16)

    if not skips:
        pl.when(h == 0)(lambda: blank(0))
        pl.when(h == S - 1)(lambda: blank(2))

    def block_in(k):
        if k:
            pl.when(t >= k)(lambda: forward(k))
        for row, there, _ in rows:

            @pl.when(there)
            def _():
                drain(dall.at[pl.ds(0, C - 1)], dsem.at[row, k])
                activate(row, k)

    wide = half // CHUNKS

    def product(to, b0, b1, chunk):
        total = None
        taps = slice(b0 * 3 * Kc, b1 * 3 * Kc)
        for a in range(0 if to else max(0, 3 - C), 3):
            window = act[to * C + a : to * C + a + C, :, taps].reshape(C * W, (b1 - b0) * 3 * Kc)
            weight = wc[a, taps, chunk * wide : (chunk + 1) * wide]
            term = jnp.dot(window, weight, preferred_element_type=F32)
            total = term if total is None else total + term
        return total

    if not skips:
        edges = [(t >= 0, 0, 3)]
    else:
        edges = [(h == 0, 1, 3), (h == S - 1, 0, 2), (attends, 0, 3)]

    def convolve(to, store):
        for here, b0, b1 in edges:

            @pl.when(here)
            def _():
                for chunk in range(CHUNKS):
                    store(chunk, product(to, b0, b1, chunk))

    def convolve_away(to):
        away = lax.rem(to - t + T, T) - 1

        def store(chunk, value):
            part_src[away, chunk] = value.astype(BF16)
            send(part_src.at[away, chunk], part.at[away, chunk], psend, psem.at[away, chunk], (g, h, to, c))

        convolve(to, store)

    def keep(chunk, value):
        own_total[chunk] = value

    pl.when(c == 0)(lambda: block_in(0))
    for k in range(1, T):
        pl.when(t < k)(lambda: forward(k))

    pl.when(c > 0)(lambda: block_in(0))
    loads[4].wait()
    for k in range(T):
        if k:
            block_in(k)
        pl.when(t != k)(lambda: convolve_away(k))

    for k in range(T):
        pl.when(t == k)(lambda: convolve(k, keep))

    @pl.when(attends)
    def _():
        drain(att_in.at[pl.ds(0, C - 1)], asem)
        att_out[other, 0] = att_in[other]
        drain(xall.at[pl.ds(0, (S - 2) * C - 1)], xsend)
        drain(stat2.at[pl.ds(0, S * T * C - 1)], s2send)

    @pl.when(jnp.logical_not(attends))
    def _():
        drain(att_in, asem)
        for k in range(C):
            att_out[k, 0] = att_in[k]
        drain(xall.at[pl.ds(0, (S - 2) * C)], xsend)
        drain(dall.at[pl.ds(0, 2 * T * (C - 1))], share_sem)

    for r in range(S):

        @pl.when(h == r)
        def _():
            below = max(r - 1, 0) if r < S - 1 else S - 2
            level = (T - 1 if r == 0 else T * C - 1) if r < S - 1 else 0
            above = max(S - 2 - r, 0)
            drain(stat1.at[pl.ds(0, below * T * C + level + above * C)], s1send)

    @pl.when(attends & jnp.logical_not(at_edge))
    def _():
        drain(dall.at[pl.ds(0, 3 * T + C - 2)], dsend.at[1])
        drain(dall.at[pl.ds(0, (3 * T - 1) * (C - 1))], share_sem)
        drain(att_src.at[0, 0], asend)

    @pl.when(at_edge)
    def _():
        drain(dall.at[pl.ds(0, 2)], dsend.at[2])
        drain(dall.at[pl.ds(0, 3 * T + 2 * C - 4)], dsend.at[1])
        drain(dall.at[pl.ds(0, (3 * T - 2) * (C - 1))], share_sem)
        drain(xall.at[pl.ds(0, C + 1)], asend)

    drain(gall.at[pl.ds(0, C - 1)], gsend)
    for chunk in range(CHUNKS):
        total = own_total[chunk]
        for dt in range(1, T):
            drain(part.at[dt - 1, chunk], psem.at[dt - 1, chunk])
            total = total + part[dt - 1, chunk].astype(F32)
        conv_out[:, 0, :, chunk * wide : (chunk + 1) * wide] = total.reshape(C, W, wide).astype(BF16)
    if T > 1:
        drain(part_src, psend)


def slice_moments(totals, population):
    width = totals.shape[1]
    if width == LANES:
        return moments([totals], population)
    mean, scale = moments([jnp.concatenate([totals] * (LANES // width), axis=1)], population)
    return mean[:, :width], scale[:, :width]


def hand_over(att_in, conv_in, att_out, conv_out):
    att_out[...] = att_in[...]
    conv_out[...] = conv_in[...]


def on_device(S, T, C, x, g1, g2, wq, wk, wv, wo, wc):
    frames, rows, W, half = x.shape
    assert frames == C and rows == 1 and half * C == D
    Kc = wc.shape[3]
    assert Kc * T == D and S > 3
    n, NF = S * T * C, T * C
    wide = half // CHUNKS
    wc = wc.reshape(3, 9 * Kc, half)
    vmem = pl.BlockSpec(memory_space=pltpu.VMEM)
    hbm = pl.BlockSpec(memory_space=pl.ANY)
    out = jax.ShapeDtypeStruct(x.shape, BF16)
    dma = pltpu.SemaphoreType.DMA
    kept = pltpu.VMEM(x.shape, BF16)
    links = max(T - 1, 1)
    stats = (2 * max(Kc // LANES, 1), min(Kc, LANES))
    results = pl.pallas_call(
        functools.partial(kernel, S, T, C, W),
        out_shape=(kept, kept),
        in_specs=[hbm] * 8,
        out_specs=(vmem, vmem),
        scratch_shapes=[
            pltpu.VMEM(x.shape, BF16),
            pltpu.VMEM((3, D, D), BF16),
            pltpu.VMEM((D, D), BF16),
            pltpu.VMEM(wc.shape, BF16),
            pltpu.VMEM((half // 64, LANES), F32),
            pltpu.VMEM((half // 64, LANES), F32),
            pltpu.VMEM((n, half // 64, LANES), F32),
            pltpu.VMEM((T, *stats), F32),
            pltpu.VMEM((n, *stats), F32),
            pltpu.VMEM((C, 2, 1, half), F32),
            pltpu.VMEM((S * C, W, half), BF16),
            pltpu.VMEM((S, W, D), BF16),
            pltpu.VMEM((S * W, D), BF16),
            pltpu.VMEM((S * W, D), BF16),
            pltpu.VMEM((2, C, W, half), BF16),
            pltpu.VMEM((C, W, half), BF16),
            pltpu.VMEM((2, T, W, Kc), BF16),
            pltpu.VMEM((3 * NF, W, Kc), BF16),
            pltpu.VMEM((NF + 2, W, 9 * Kc), BF16),
            pltpu.VMEM((CHUNKS, C * W, wide), F32),
            pltpu.VMEM((links, CHUNKS, C * W, wide), BF16),
            pltpu.VMEM((links, CHUNKS, C * W, wide), BF16),
            dma((2,)),
            dma((3,)),
            pltpu.SemaphoreType.REGULAR((S - 1,)),
            dma(()),
            dma(()),
            dma(()),
            dma(()),
            dma(()),
            dma(()),
            dma((S,)),
            dma(()),
            dma(()),
            dma(()),
            dma(()),
            dma((3,)),
            dma((3, T)),
            dma((3, T)),
            dma(()),
            dma(()),
            dma((links, CHUNKS)),
        ],
        compiler_params=pltpu.CompilerParams(collective_id=0, has_side_effects=True),
    )(x, g1.reshape(1, half), g2.reshape(1, half), wq, wk, wv, wo, wc)
    return pl.pallas_call(
        hand_over, out_shape=(out, out), in_specs=[vmem] * 2, out_specs=(vmem, vmem),
    )(*[pltpu.with_memory_space_constraint(r, pltpu.VMEM) for r in results])


def solution(mesh):
    S, T, C = mesh.shape["space"], mesh.shape["tm"], mesh.shape["chan"]
    placed = (
        P(("groups", "tm"), "space", None, "chan"),
        P("chan"),
        P("chan"),
        P(),
        P(),
        P(),
        P(),
        P(None, None, None, "tm", "chan"),
    )
    return jax.shard_map(
        functools.partial(on_device, S, T, C),
        mesh=mesh,
        in_specs=placed,
        out_specs=(
            P(("groups", "tm"), "space", None, "chan"),
            P(("groups", "tm"), "space", None, "chan"),
        ),
        check_vma=False,
    )
```

```python
import functools

import jax
import jax.numpy as jnp
from jax import lax
from jax.experimental import pallas as pl
from jax.experimental.pallas import tpu as pltpu
from jax.sharding import PartitionSpec as P

D = 512
NGROUP = 32
EPSILON = 1e-06
LANES = 128
CHUNKS = 2
GROUP = D // NGROUP
MESH = pl.DeviceIdType.MESH
F32 = jnp.float32
BF16 = jnp.bfloat16


def group_total(v):
    lane = lax.broadcasted_iota(jnp.int32, v.shape, 1)
    width = v.shape[1]
    step = 1
    while step < GROUP:
        place = (lane // step) % 4
        terms = [v]
        for d in range(1, 4):
            terms.append(jnp.where(place < 4 - d, pltpu.roll(v, width - d * step, 1), 0.0))
            terms.append(jnp.where(place >= d, pltpu.roll(v, d * step, 1), 0.0))
        while len(terms) > 1:
            terms = [sum(terms[i : i + 2]) for i in range(0, len(terms), 2)]
        v = terms[0]
        step *= 4
    return v


def store_sums(ref, values):
    sums = jnp.sum(values, axis=0, keepdims=True)
    squares = jnp.sum(values * values, axis=0, keepdims=True)
    blocks, width = ref.shape[0] // 2, ref.shape[1]
    for b in range(blocks):
        ref[b : b + 1] = sums[:, b * width : (b + 1) * width]
        ref[blocks + b : blocks + b + 1] = squares[:, b * width : (b + 1) * width]


def moments(stacks, population):
    size = stacks[0].shape[0]
    blocks = size // 2
    count = len(stacks) * size
    rows = 8 * pl.cdiv(count, 8)
    padding = [jnp.zeros((rows - count, LANES), F32)] if rows > count else []
    grouped = group_total(jnp.concatenate([*stacks, *padding], axis=0)) / population
    variance = jnp.maximum(pltpu.roll(grouped, rows - blocks, 0) - grouped * grouped, 0.0)
    scale = lax.rsqrt(variance + EPSILON)
    picks = [i * size + b for i in range(len(stacks)) for b in range(blocks)]
    return [jnp.concatenate([v[k : k + 1] for k in picks], axis=1) for v in (grouped, scale)]


def kernel(
    S, T, C, W,
    x_hbm, g1, g2, wq_hbm, wk_hbm, wv_hbm, wo_hbm, wc_hbm,
    att_out, conv_out,
    x, projections, wc,
    stat1_src, row_sum, stat1, stat2_src, stat2, gall,
    xall, tokens, keyed, valued, att_src, att_in, dsrc, dall, act, own_total, part_src, part,
    xload, wsem, insem, gsend, gsem, raw_sem, s1send, s1sem, xsend, xsem, s2send, s2sem,
    asend, asem, dsend, dsem, direct_sem, psend, psem,
):
    g = lax.axis_index("groups")
    h = lax.axis_index("space")
    t = lax.axis_index("tm")
    c = lax.axis_index("chan")
    attending = (S - 2) * T * C
    me = (h * T + t) * C + c - T * C
    half = D // C
    Kc = D // T
    NF = T * C
    other = lax.rem(c + 1, C)
    attends = (h > 0) & (h < S - 1)
    at_edge = (h == 1) | (h == S - 2)
    side = jnp.where(h == 1, -1, 1)

    def rows_apart(sign, act_on):
        def row(d):
            @pl.when((h + sign * d >= 0) & (h + sign * d < S))
            def _():
                act_on(h + sign * d, d)

        pl.loop(1, S, unroll=S <= 4)(row)

    def row_devices(r, act_on):
        for dt in range(T):
            for dc in range(C):
                act_on((g, r, lax.rem(t + dt, T), lax.rem(c + dc, C)))

    def row_where(r, sign, act_on):
        for dt in range(1, T):

            @pl.when((t + sign * dt >= 0) & (t + sign * dt < T))
            def _():
                for dc in range(C):
                    act_on((g, r, t + sign * dt, lax.rem(c + dc, C)))

    def beside(sign, act_on):
        row_where(h, sign, act_on)

    def mates(act_on):
        for dc in range(1, C):
            act_on((g, h, t, lax.rem(c + dc, C)))

    def signal(sem):
        return lambda where: pl.semaphore_signal(sem, inc=1, device_id=where, device_id_type=MESH)

    def drain(ref, sem):
        pltpu.make_async_copy(ref, ref, sem).wait()

    def send(src, dst, sends, recvs, where):
        copy = pltpu.make_async_remote_copy(
            src_ref=src, dst_ref=dst, send_sem=sends, recv_sem=recvs, device_id=where, device_id_type=MESH,
        )
        copy.start()

    x_load = pltpu.make_async_copy(x_hbm, x, xload.at[0])
    x_load.start()
    for k, gain in enumerate((g1, g2)):
        pltpu.make_async_copy(gain, gall.at[c, k], xload.at[1]).start()
    stat1[...] = jnp.zeros(stat1.shape, F32)
    barrier = pltpu.get_barrier_semaphore()
    mates(signal(barrier))
    beside(1, signal(barrier))

    def column(r, act_on):
        for dc in range(C):
            act_on((g, r, t, lax.rem(c + dc, C)))

    def greet(r, d):
        column(r, signal(barrier))
        row_where(r, 1, signal(barrier))

    rows_apart(1, greet)
    pl.semaphore_wait(barrier, (h * (t + 1) + t) * C + C - 1)
    pl.when(h < S - 1)(lambda: rows_apart(-1, lambda r, d: column(r, signal(insem.at[d]))))
    beside(-1, signal(insem.at[0]))

    loads = [
        pltpu.make_async_copy(src, dst, wsem.at[i])
        for i, (src, dst) in zip((0, 0, 0, 0, 1), [(wq_hbm, projections.at[0]), (wk_hbm, projections.at[1]), (wv_hbm, projections.at[2]), (wo_hbm, projections.at[3]), (wc_hbm, wc)])
    ]


    x_load.wait()
    store_sums(stat1_src, x[...].reshape(C * W, half).astype(F32))
    at = (h * T + t) * C + c

    def send_stat(where, src=stat1_src, recvs=s1sem):
        send(src, stat1.at[at], s1send, recvs, where)

    def same_row(sign):
        for dt in range(1, T):

            @pl.when((t + sign * dt >= 0) & (t + sign * dt < T))
            def _():
                send_stat((g, h, t + sign * dt, c), recvs=raw_sem)

                @pl.when(attends)
                def _():
                    for dc in range(1, C):
                        send_stat((g, h, t + sign * dt, lax.rem(c + dc, C)))

    def send_x(r, dc):
        frame = lax.rem(c + dc, C)
        send(x.at[frame, 0], xall.at[h * C + c], xsend, xsem, (g, r, t, frame))

    def column_x(r):
        for dc in range(C):
            send_x(r, dc)

    for r in range(1, S - 1):

        @pl.when(r < h)
        def _():
            column(r, send_stat)
            row_where(r, -1, send_stat)

    pl.when(h < S - 1)(lambda: same_row(-1))
    stat1[at] = stat1_src[...]

    @pl.when(attends)
    def _():
        mates(send_stat)
        xall[h * C + c] = x[c, 0]
        for dc in range(1, C):
            send_x(h, dc)

    for r in range(1, S - 1):
        pl.when(r < h)(lambda: column_x(r))

    drain(gall.at[c], xload.at[1])
    mates(lambda where: send(gall.at[c], gall.at[c], gsend, gsem, where))
    @pl.when(attends)
    def _():
        for load in loads[:4]:
            load.start()

    loads[4].start()

    @pl.when(h < S - 2)
    def _():
        pl.semaphore_wait(insem.at[1], C)
        column_x(h + 1)

    @pl.when(t < T - 1)
    def _():
        pl.semaphore_wait(insem.at[0], (T - 1 - t) * C)
        for r in range(1, S - 1):
            pl.when(r < h)(lambda: row_where(r, 1, send_stat))
        pl.when(h < S - 1)(lambda: same_row(1))

    @pl.when(h < S - 1)
    def _():
        if T > 1:
            drain(stat1.at[pl.ds(0, T - 1)], raw_sem)

    @pl.when(h < S - 2)
    def _():
        total = stat1_src[...]
        for dt in range(1, T):
            total = total + stat1[(h * T + lax.rem(t + dt, T)) * C + c]
        row_sum[...] = total

        def send_sum(where):
            send_stat(where, src=row_sum)

        column(h + 1, send_sum)

        def upward(d):
            @pl.when(h + d < S - 1)
            def _():
                pl.semaphore_wait(insem.at[d], C)
                column(h + d, send_sum)
                column_x(h + d)

        pl.loop(2, S - 1, unroll=S <= 4)(upward)

    drain(gall.at[pl.ds(0, C - 1)], gsem)
    population = float(S * T * C * W * GROUP)
    frame_at = t * C + c

    def send_attended(i, k, r, core):
        send(att_src.at[i, k], att_in.at[c], asend, asem, (g, r, t, core))

    def attend(R):
        outer = h + side
        mine = [h, outer][:R]
        skipped = jnp.where(h == 1, R, 0) if R == 2 else None

        def rest(i):
            return i + skipped if R == 2 else i + jnp.where(i >= h, 1, 0)

        for r in range(1, S - 1):

            @pl.when(h == r)
            def _():
                drain(stat1.at[pl.ds(0, r * C + T * (C - 1) + (S - 1 - r) * T * C)], s1sem)

        drain(xall.at[pl.ds(0, S * C - 1)], xsem)
        drain(projections, wsem.at[0])
        totals = jnp.sum(stat1[...].reshape(S * T, C, *stat1.shape[1:]), axis=0)
        mean1, scale1 = moments([totals[k] for k in range(C)], population)
        factor1 = scale1 * jnp.concatenate([gall[k, 0] for k in range(C)], axis=1)

        def row_tokens(r):
            pieces = []
            for k in range(C):
                lanes = slice(k * half, (k + 1) * half)
                value = xall[r * C + k].astype(F32)
                pieces.append(((value - mean1[:, lanes]) * factor1[:, lanes]).astype(BF16))
            return jnp.concatenate(pieces, axis=1)

        def project(weight, first, stop):
            rows = tokens[first:stop].reshape((stop - first) * W, D)
            return jnp.dot(rows, weight[...], preferred_element_type=F32).astype(BF16)

        for i in range(R):
            tokens[i] = row_tokens(mine[i])
        for i in range(S - R):
            tokens[R + i] = row_tokens(rest(i))
        queries = project(projections.at[0], 0, R)
        keyed[...] = project(projections.at[1], 0, S)
        valued[...] = project(projections.at[2], 0, S)

        scores = lax.dot_general(
            queries, keyed[...], (((1,), (1,)), ((), ())), preferred_element_type=F32
        ) * (D ** (-0.5))
        weights = jnp.exp(scores - jnp.max(scores, axis=1, keepdims=True))
        mass = jnp.sum(weights, axis=1, keepdims=True)
        mixed = jnp.dot(weights.astype(BF16), valued[...], preferred_element_type=F32)
        mixed = (mixed * (1.0 / mass)).astype(BF16)
        attended = jnp.dot(mixed, projections[3], preferred_element_type=F32).astype(BF16)

        source = jnp.concatenate(
            [jnp.concatenate([xall[r * C + k] for k in range(C)], axis=1) for r in mine], axis=0
        ).astype(F32)
        resid = (source - mean1) + attended.astype(F32)
        for i in range(R):
            for k in range(T):
                dsrc[i, k] = resid[i * W : (i + 1) * W, k * Kc : (k + 1) * Kc].astype(BF16)

        def send_row(i, r, columns, sends):
            for dt in columns:
                to = lax.rem(t + dt, T)
                row = mine[i] - r + 1
                send(
                    dsrc.at[i, to], dall.at[row * NF + frame_at], sends, direct_sem.at[row, t], (g, r, to, c),
                )

        others = range(1, T)
        for k in range(T):
            store_sums(stat2_src.at[k], resid[:, k * Kc : (k + 1) * Kc])

        def send_stat2(where):
            send(stat2_src.at[where[2]], stat2.at[me], s2send, s2sem, where)

        if R == 2:
            row_devices(outer, send_stat2)
            for i in range(2):
                send_row(i, outer, others, dsend.at[0])

            def own_column():
                for i in range(2):
                    send_row(i, outer, [0], dsend.at[1])

            pl.when(t == 0)(own_column)
        def beyond_outer(r, d):
            if R == 2:
                pl.when(r != outer)(lambda: row_devices(r, send_stat2))
            else:
                row_devices(r, send_stat2)

        rows_apart(-1, beyond_outer)
        rows_apart(1, beyond_outer)
        beside(-1, send_stat2)
        beside(1, send_stat2)
        mates(send_stat2)
        if R == 2:
            send_row(0, h - side, [*others, 0], dsend.at[1])
        else:
            for r in (h - 1, h + 1):
                send_row(0, r, [*others, 0], dsend.at[1])
        for i in range(R):
            send_row(i, h, others, dsend.at[1])
            slot = (mine[i] - h + 1) * NF + frame_at
            mates(lambda where: send(dsrc.at[i, t], dall.at[slot], dsend.at[1], dsem.at[mine[i] - h + 1, t], where))
            dall[slot] = dsrc[i, t]
        for i in range(R):
            for k in range(C):
                att_src[i, k] = attended[i * W : (i + 1) * W, k * half : (k + 1) * half]
        stat2[me] = stat2_src[t]
        att_out[c, 0] = att_src[0, c]
        if R == 2:
            if T > 1:
                drain(dall.at[pl.ds(0, 2 * (T - 1))], dsend.at[0])
            pl.when(t > 0)(own_column)

    if S > 4:
        pl.when(attends & jnp.logical_not(at_edge))(lambda: attend(1))
    pl.when(at_edge)(lambda: attend(2))
    act[0:2] = jnp.zeros((2,) + act.shape[1:], BF16)
    gain2 = jnp.concatenate([gall[k, 1] for k in range(C)], axis=1)

    rows = [(0, h > 0, h == 1), (1, h >= 0, attends), (2, h < S - 1, h == S - 2)]

    def forward(k):
        for row, there, made_here in rows:

            @pl.when(there & jnp.logical_not(made_here & (t == k)))
            def _():
                slot = row * NF + k * C + c
                drain(dall.at[slot], direct_sem.at[row, k])
                mates(lambda where: send(dall.at[slot], dall.at[slot], dsend.at[1], dsem.at[row, k], where))


    forward(0)

    @pl.when(jnp.logical_not(attends))
    def _():
        drain(stat2.at[pl.ds(0, attending)], s2sem)

    @pl.when(attends)
    def _():
        drain(stat2.at[pl.ds(0, attending - 1)], s2sem)
        send_attended(0, other, h, other)

    @pl.when(at_edge)
    def _():
        for k in range(C):
            send_attended(1, k, h + side, k)


    def sliced(v):
        out = v[:, 0:Kc]
        for k in range(1, T):
            out = jnp.where(t == k, v[:, k * Kc : (k + 1) * Kc], out)
        return out

    mean2, scale2 = slice_moments(jnp.sum(stat2[0:attending], axis=0), population)
    factor2 = scale2 * sliced(gain2)
    column = lax.broadcasted_iota(jnp.int32, (W, Kc), 0)

    def activate(row, k):
        for f in range(k * C, (k + 1) * C):
            v = (dall[row * NF + f].astype(F32) - mean2) * factor2
            a = v / (1.0 + jnp.exp(-v))
            left = jnp.where(column == 0, 0.0, pltpu.roll(a, 1, 0))
            right = jnp.where(column == W - 1, 0.0, pltpu.roll(a, W - 1, 0))
            for e, piece in enumerate((left, a, right)):
                place = row * 3 + e
                act[f + 2, :, place * Kc : (place + 1) * Kc] = piece.astype(BF16)

    skips = (3 * Kc) % LANES == 0

    def blank(row):
        act[2:, :, row * 3 * Kc : (row + 1) * 3 * Kc] = jnp.zeros((NF, W, 3 * Kc), BF16)

    if not skips:
        pl.when(h == 0)(lambda: blank(0))
        pl.when(h == S - 1)(lambda: blank(2))

    def block_in(k):
        if k:
            pl.when(t >= k)(lambda: forward(k))
        for row, there, _ in rows:

            @pl.when(there)
            def _():
                drain(dall.at[pl.ds(0, C - 1)], dsem.at[row, k])
                activate(row, k)

    wide = half // CHUNKS

    def product(to, b0, b1, chunk):
        total = None
        taps = slice(b0 * 3 * Kc, b1 * 3 * Kc)
        for a in range(0 if to else max(0, 3 - C), 3):
            window = act[to * C + a : to * C + a + C, :, taps].reshape(C * W, (b1 - b0) * 3 * Kc)
            weight = wc[a, taps, chunk * wide : (chunk + 1) * wide]
            term = jnp.dot(window, weight, preferred_element_type=F32)
            total = term if total is None else total + term
        return total

    if not skips:
        edges = [(t >= 0, 0, 3)]
    else:
        edges = [(h == 0, 1, 3), (h == S - 1, 0, 2), (attends, 0, 3)]

    def convolve(to, store):
        for here, b0, b1 in edges:

            @pl.when(here)
            def _():
                for chunk in range(CHUNKS):
                    store(chunk, product(to, b0, b1, chunk))

    def convolve_away(to):
        away = lax.rem(to - t + T, T) - 1

        def store(chunk, value):
            part_src[away, chunk] = value.astype(BF16)
            send(part_src.at[away, chunk], part.at[away, chunk], psend, psem.at[away, chunk], (g, h, to, c))

        convolve(to, store)

    def keep(chunk, value):
        own_total[chunk] = value

    pl.when(c == 0)(lambda: block_in(0))
    for k in range(1, T):
        pl.when(t < k)(lambda: forward(k))

    pl.when(c > 0)(lambda: block_in(0))
    loads[4].wait()
    for k in range(T):
        if k:
            block_in(k)
        pl.when(t != k)(lambda: convolve_away(k))

    for k in range(T):
        pl.when(t == k)(lambda: convolve(k, keep))

    @pl.when(attends)
    def _():
        drain(att_in.at[pl.ds(0, C - 1)], asem)
        att_out[other, 0] = att_in[other]
        drain(xall.at[pl.ds(0, (S - 2) * C - 1)], xsend)
        drain(stat2.at[pl.ds(0, S * T * C - 1)], s2send)

    @pl.when(jnp.logical_not(attends))
    def _():
        drain(att_in, asem)
        for k in range(C):
            att_out[k, 0] = att_in[k]
        drain(xall.at[pl.ds(0, (S - 2) * C)], xsend)
        drain(dall.at[pl.ds(0, 2 * T * (C - 1))], dsend.at[1])

    for r in range(S):

        @pl.when(h == r)
        def _():
            below = max(r - 1, 0) if r < S - 1 else S - 2
            level = (T - 1 if r == 0 else T * C - 1) if r < S - 1 else 0
            above = max(S - 2 - r, 0)
            drain(stat1.at[pl.ds(0, below * T * C + level + above * C)], s1send)

    @pl.when(attends & jnp.logical_not(at_edge))
    def _():
        drain(dall.at[pl.ds(0, 3 * T + C - 2 + (3 * T - 1) * (C - 1))], dsend.at[1])
        drain(att_src.at[0, 0], asend)

    @pl.when(at_edge)
    def _():
        drain(dall.at[pl.ds(0, 3 * T + 2 * C - 2 + (3 * T - 2) * (C - 1))], dsend.at[1])
        drain(xall.at[pl.ds(0, C + 1)], asend)

    drain(gall.at[pl.ds(0, C - 1)], gsend)
    for chunk in range(CHUNKS):
        total = own_total[chunk]
        for dt in range(1, T):
            drain(part.at[dt - 1, chunk], psem.at[dt - 1, chunk])
            total = total + part[dt - 1, chunk].astype(F32)
        conv_out[:, 0, :, chunk * wide : (chunk + 1) * wide] = total.reshape(C, W, wide).astype(BF16)
    if T > 1:
        drain(part_src, psend)


def slice_moments(totals, population):
    width = totals.shape[1]
    if width == LANES:
        return moments([totals], population)
    mean, scale = moments([jnp.concatenate([totals] * (LANES // width), axis=1)], population)
    return mean[:, :width], scale[:, :width]


def hand_over(att_in, conv_in, att_out, conv_out):
    att_out[...] = att_in[...]
    conv_out[...] = conv_in[...]


def on_device(S, T, C, x, g1, g2, wq, wk, wv, wo, wc):
    frames, rows, W, half = x.shape
    assert frames == C and rows == 1 and half * C == D
    Kc = wc.shape[3]
    assert Kc * T == D and S > 3
    n, NF = S * T * C, T * C
    wide = half // CHUNKS
    wc = wc.reshape(3, 9 * Kc, half)
    vmem = pl.BlockSpec(memory_space=pltpu.VMEM)
    hbm = pl.BlockSpec(memory_space=pl.ANY)
    out = jax.ShapeDtypeStruct(x.shape, BF16)
    dma = pltpu.SemaphoreType.DMA
    kept = pltpu.VMEM(x.shape, BF16)
    links = max(T - 1, 1)
    stats = (2 * max(Kc // LANES, 1), min(Kc, LANES))
    results = pl.pallas_call(
        functools.partial(kernel, S, T, C, W),
        out_shape=(kept, kept),
        in_specs=[hbm] * 8,
        out_specs=(vmem, vmem),
        scratch_shapes=[
            pltpu.VMEM(x.shape, BF16),
            pltpu.VMEM((4, D, D), BF16),
            pltpu.VMEM(wc.shape, BF16),
            pltpu.VMEM((half // 64, LANES), F32),
            pltpu.VMEM((half // 64, LANES), F32),
            pltpu.VMEM((n, half // 64, LANES), F32),
            pltpu.VMEM((T, *stats), F32),
            pltpu.VMEM((n, *stats), F32),
            pltpu.VMEM((C, 2, 1, half), F32),
            pltpu.VMEM((S * C, W, half), BF16),
            pltpu.VMEM((S, W, D), BF16),
            pltpu.VMEM((S * W, D), BF16),
            pltpu.VMEM((S * W, D), BF16),
            pltpu.VMEM((2, C, W, half), BF16),
            pltpu.VMEM((C, W, half), BF16),
            pltpu.VMEM((2, T, W, Kc), BF16),
            pltpu.VMEM((3 * NF, W, Kc), BF16),
            pltpu.VMEM((NF + 2, W, 9 * Kc), BF16),
            pltpu.VMEM((CHUNKS, C * W, wide), F32),
            pltpu.VMEM((links, CHUNKS, C * W, wide), BF16),
            pltpu.VMEM((links, CHUNKS, C * W, wide), BF16),
            dma((2,)),
            dma((2,)),
            pltpu.SemaphoreType.REGULAR((S - 1,)),
            dma(()),
            dma(()),
            dma(()),
            dma(()),
            dma(()),
            dma(()),
            dma(()),
            dma(()),
            dma(()),
            dma(()),
            dma(()),
            dma((2,)),
            dma((3, T)),
            dma((3, T)),
            dma(()),
            dma((links, CHUNKS)),
        ],
        compiler_params=pltpu.CompilerParams(collective_id=0, has_side_effects=True),
    )(x, g1.reshape(1, half), g2.reshape(1, half), wq, wk, wv, wo, wc)
    return pl.pallas_call(
        hand_over, out_shape=(out, out), in_specs=[vmem] * 2, out_specs=(vmem, vmem),
    )(*[pltpu.with_memory_space_constraint(r, pltpu.VMEM) for r in results])


def solution(mesh):
    S, T, C = mesh.shape["space"], mesh.shape["tm"], mesh.shape["chan"]
    placed = (
        P(("groups", "tm"), "space", None, "chan"),
        P("chan"),
        P("chan"),
        P(),
        P(),
        P(),
        P(),
        P(None, None, None, "tm", "chan"),
    )
    return jax.shard_map(
        functools.partial(on_device, S, T, C),
        mesh=mesh,
        in_specs=placed,
        out_specs=(
            P(("groups", "tm"), "space", None, "chan"),
            P(("groups", "tm"), "space", None, "chan"),
        ),
        check_vma=False,
    )
```

```python
import functools

import jax
import jax.numpy as jnp
from jax import lax
from jax.experimental import pallas as pl
from jax.experimental.pallas import tpu as pltpu
from jax.sharding import PartitionSpec as P

D = 512
NGROUP = 32
EPSILON = 1e-06
LANES = 128
CHUNKS = 2
GROUP = D // NGROUP
MESH = pl.DeviceIdType.MESH
F32 = jnp.float32
BF16 = jnp.bfloat16


def group_total(v):
    lane = lax.broadcasted_iota(jnp.int32, v.shape, 1)
    width = v.shape[1]
    step = 1
    while step < GROUP:
        place = (lane // step) % 4
        terms = [v]
        for d in range(1, 4):
            terms.append(jnp.where(place < 4 - d, pltpu.roll(v, width - d * step, 1), 0.0))
            terms.append(jnp.where(place >= d, pltpu.roll(v, d * step, 1), 0.0))
        while len(terms) > 1:
            terms = [sum(terms[i : i + 2]) for i in range(0, len(terms), 2)]
        v = terms[0]
        step *= 4
    return v


def store_sums(ref, values):
    sums = jnp.sum(values, axis=0, keepdims=True)
    squares = jnp.sum(values * values, axis=0, keepdims=True)
    blocks, width = ref.shape[0] // 2, ref.shape[1]
    for b in range(blocks):
        ref[b : b + 1] = sums[:, b * width : (b + 1) * width]
        ref[blocks + b : blocks + b + 1] = squares[:, b * width : (b + 1) * width]


def moments(stacks, population):
    size = stacks[0].shape[0]
    blocks = size // 2
    count = len(stacks) * size
    rows = 8 * pl.cdiv(count, 8)
    padding = [jnp.zeros((rows - count, LANES), F32)] if rows > count else []
    grouped = group_total(jnp.concatenate([*stacks, *padding], axis=0)) / population
    variance = jnp.maximum(pltpu.roll(grouped, rows - blocks, 0) - grouped * grouped, 0.0)
    scale = lax.rsqrt(variance + EPSILON)
    picks = [i * size + b for i in range(len(stacks)) for b in range(blocks)]
    return [jnp.concatenate([v[k : k + 1] for k in picks], axis=1) for v in (grouped, scale)]


def kernel(
    S, T, C, W,
    x_hbm, g1, g2, wq_hbm, wk_hbm, wv_hbm, wo_hbm, wc_hbm,
    att_out, conv_out,
    x, projections, wc,
    stat1_src, row_sum, stat1, stat2_src, stat2, gall,
    xall, tokens, keyed, valued, att_src, att_in, dsrc, dall, act, own_total, part_src, part,
    xload, wsem, insem, gsend, gsem, raw_sem, s1send, s1sem, xsend, xsem, s2send, s2sem,
    asend, asem, dsend, dsem, direct_sem, psend, psem,
):
    g = lax.axis_index("groups")
    h = lax.axis_index("space")
    t = lax.axis_index("tm")
    c = lax.axis_index("chan")
    attending = (S - 2) * T * C
    me = (h * T + t) * C + c - T * C
    half = D // C
    Kc = D // T
    NF = T * C
    other = lax.rem(c + 1, C)
    attends = (h > 0) & (h < S - 1)
    at_edge = (h == 1) | (h == S - 2)
    side = jnp.where(h == 1, -1, 1)

    def rows_apart(sign, act_on):
        def row(d):
            @pl.when((h + sign * d >= 0) & (h + sign * d < S))
            def _():
                act_on(h + sign * d, d)

        pl.loop(1, S, unroll=S <= 4)(row)

    def row_devices(r, act_on):
        for dt in range(T):
            for dc in range(C):
                act_on((g, r, lax.rem(t + dt, T), lax.rem(c + dc, C)))

    def row_where(r, sign, act_on):
        for dt in range(1, T):

            @pl.when((t + sign * dt >= 0) & (t + sign * dt < T))
            def _():
                for dc in range(C):
                    act_on((g, r, t + sign * dt, lax.rem(c + dc, C)))

    def beside(sign, act_on):
        row_where(h, sign, act_on)

    def mates(act_on):
        for dc in range(1, C):
            act_on((g, h, t, lax.rem(c + dc, C)))

    def signal(sem):
        return lambda where: pl.semaphore_signal(sem, inc=1, device_id=where, device_id_type=MESH)

    def drain(ref, sem):
        pltpu.make_async_copy(ref, ref, sem).wait()

    def send(src, dst, sends, recvs, where):
        copy = pltpu.make_async_remote_copy(
            src_ref=src, dst_ref=dst, send_sem=sends, recv_sem=recvs, device_id=where, device_id_type=MESH,
        )
        copy.start()

    x_load = pltpu.make_async_copy(x_hbm, x, xload.at[0])
    x_load.start()
    for k, gain in enumerate((g1, g2)):
        pltpu.make_async_copy(gain, gall.at[c, k], xload.at[1]).start()
    stat1[...] = jnp.zeros(stat1.shape, F32)
    barrier = pltpu.get_barrier_semaphore()
    mates(signal(barrier))
    beside(1, signal(barrier))

    def column(r, act_on):
        for dc in range(C):
            act_on((g, r, t, lax.rem(c + dc, C)))

    def greet(r, d):
        column(r, signal(barrier))
        row_where(r, 1, signal(barrier))

    rows_apart(1, greet)
    pl.semaphore_wait(barrier, (h * (t + 1) + t) * C + C - 1)
    pl.when(h < S - 1)(lambda: rows_apart(-1, lambda r, d: column(r, signal(insem.at[d]))))
    beside(-1, signal(insem.at[0]))

    loads = [
        pltpu.make_async_copy(src, dst, wsem.at[i])
        for i, (src, dst) in zip((0, 0, 0, 0, 1), [(wq_hbm, projections.at[0]), (wk_hbm, projections.at[1]), (wv_hbm, projections.at[2]), (wo_hbm, projections.at[3]), (wc_hbm, wc)])
    ]


    x_load.wait()
    store_sums(stat1_src, x[...].reshape(C * W, half).astype(F32))
    at = (h * T + t) * C + c

    def send_stat(where, src=stat1_src, recvs=s1sem):
        send(src, stat1.at[at], s1send, recvs, where)

    def same_row(sign):
        for dt in range(1, T):

            @pl.when((t + sign * dt >= 0) & (t + sign * dt < T))
            def _():
                send_stat((g, h, t + sign * dt, c), recvs=raw_sem)

                @pl.when(attends)
                def _():
                    for dc in range(1, C):
                        send_stat((g, h, t + sign * dt, lax.rem(c + dc, C)))

    def send_x(r, dc):
        frame = lax.rem(c + dc, C)
        send(x.at[frame, 0], xall.at[h * C + c], xsend, xsem, (g, r, t, frame))

    def column_x(r):
        for dc in range(C):
            send_x(r, dc)

    for r in range(1, S - 1):

        @pl.when(r < h)
        def _():
            column(r, send_stat)
            row_where(r, -1, send_stat)

    pl.when(h < S - 1)(lambda: same_row(-1))
    stat1[at] = stat1_src[...]

    @pl.when(attends)
    def _():
        mates(send_stat)
        xall[h * C + c] = x[c, 0]
        for dc in range(1, C):
            send_x(h, dc)

    for r in range(1, S - 1):
        pl.when((r < h) & ((h < S - 1) | (r < S - 2)))(lambda: column_x(r))

    drain(gall.at[c], xload.at[1])
    mates(lambda where: send(gall.at[c], gall.at[c], gsend, gsem, where))
    @pl.when(attends)
    def _():
        for load in loads[:4]:
            load.start()

    loads[4].start()

    @pl.when(h < S - 2)
    def _():
        pl.semaphore_wait(insem.at[1], C)
        column_x(h + 1)

    @pl.when(t < T - 1)
    def _():
        pl.semaphore_wait(insem.at[0], (T - 1 - t) * C)
        for r in range(1, S - 1):
            pl.when(r < h)(lambda: row_where(r, 1, send_stat))
        pl.when(h < S - 1)(lambda: same_row(1))

    pl.when(h == S - 1)(lambda: column_x(S - 2))
    @pl.when(h < S - 1)
    def _():
        if T > 1:
            drain(stat1.at[pl.ds(0, T - 1)], raw_sem)

    @pl.when(h < S - 2)
    def _():
        total = stat1_src[...]
        for dt in range(1, T):
            total = total + stat1[(h * T + lax.rem(t + dt, T)) * C + c]
        row_sum[...] = total

        def send_sum(where):
            send_stat(where, src=row_sum)

        column(h + 1, send_sum)

        def upward(d):
            @pl.when(h + d < S - 1)
            def _():
                pl.semaphore_wait(insem.at[d], C)
                column(h + d, send_sum)
                column_x(h + d)

        pl.loop(2, S - 1, unroll=S <= 4)(upward)

    drain(gall.at[pl.ds(0, C - 1)], gsem)
    population = float(S * T * C * W * GROUP)
    frame_at = t * C + c

    def send_attended(i, k, r, core):
        send(att_src.at[i, k], att_in.at[c], asend, asem, (g, r, t, core))

    def attend(R):
        outer = h + side
        mine = [h, outer][:R]
        skipped = jnp.where(h == 1, R, 0) if R == 2 else None

        def rest(i):
            return i + skipped if R == 2 else i + jnp.where(i >= h, 1, 0)

        for r in range(1, S - 1):

            @pl.when(h == r)
            def _():
                drain(stat1.at[pl.ds(0, r * C + T * (C - 1) + (S - 1 - r) * T * C)], s1sem)

        drain(xall.at[pl.ds(0, S * C - 1)], xsem)
        drain(projections, wsem.at[0])
        totals = jnp.sum(stat1[...].reshape(S * T, C, *stat1.shape[1:]), axis=0)
        mean1, scale1 = moments([totals[k] for k in range(C)], population)
        factor1 = scale1 * jnp.concatenate([gall[k, 0] for k in range(C)], axis=1)

        def row_tokens(r):
            pieces = []
            for k in range(C):
                lanes = slice(k * half, (k + 1) * half)
                value = xall[r * C + k].astype(F32)
                pieces.append(((value - mean1[:, lanes]) * factor1[:, lanes]).astype(BF16))
            return jnp.concatenate(pieces, axis=1)

        def project(weight, first, stop):
            rows = tokens[first:stop].reshape((stop - first) * W, D)
            return jnp.dot(rows, weight[...], preferred_element_type=F32).astype(BF16)

        for i in range(R):
            tokens[i] = row_tokens(mine[i])
        for i in range(S - R):
            tokens[R + i] = row_tokens(rest(i))
        queries = project(projections.at[0], 0, R)
        keyed[...] = project(projections.at[1], 0, S)
        valued[...] = project(projections.at[2], 0, S)

        scores = lax.dot_general(
            queries, keyed[...], (((1,), (1,)), ((), ())), preferred_element_type=F32
        ) * (D ** (-0.5))
        weights = jnp.exp(scores - jnp.max(scores, axis=1, keepdims=True))
        mass = jnp.sum(weights, axis=1, keepdims=True)
        mixed = jnp.dot(weights.astype(BF16), valued[...], preferred_element_type=F32)
        mixed = (mixed * (1.0 / mass)).astype(BF16)
        attended = jnp.dot(mixed, projections[3], preferred_element_type=F32).astype(BF16)

        source = jnp.concatenate(
            [jnp.concatenate([xall[r * C + k] for k in range(C)], axis=1) for r in mine], axis=0
        ).astype(F32)
        resid = (source - mean1) + attended.astype(F32)
        for i in range(R):
            for k in range(T):
                dsrc[i, k] = resid[i * W : (i + 1) * W, k * Kc : (k + 1) * Kc].astype(BF16)

        def send_row(i, r, columns, sends):
            for dt in columns:
                to = lax.rem(t + dt, T)
                row = mine[i] - r + 1
                send(
                    dsrc.at[i, to], dall.at[row * NF + frame_at], sends, direct_sem.at[row, t], (g, r, to, c),
                )

        others = range(1, T)
        for k in range(T):
            store_sums(stat2_src.at[k], resid[:, k * Kc : (k + 1) * Kc])

        def send_stat2(where):
            send(stat2_src.at[where[2]], stat2.at[me], s2send, s2sem, where)

        if R == 2:
            row_devices(outer, send_stat2)
            for i in range(2):
                send_row(i, outer, others, dsend.at[0])

            def own_column():
                for i in range(2):
                    send_row(i, outer, [0], dsend.at[1])

            pl.when(t == 0)(own_column)
        def beyond_outer(r, d):
            if R == 2:
                pl.when(r != outer)(lambda: row_devices(r, send_stat2))
            else:
                row_devices(r, send_stat2)

        rows_apart(-1, beyond_outer)
        rows_apart(1, beyond_outer)
        beside(-1, send_stat2)
        beside(1, send_stat2)
        mates(send_stat2)
        if R == 2:
            send_row(0, h - side, [*others, 0], dsend.at[1])
        else:
            for r in (h - 1, h + 1):
                send_row(0, r, [*others, 0], dsend.at[1])
        for i in range(R):
            send_row(i, h, others, dsend.at[1])
            slot = (mine[i] - h + 1) * NF + frame_at
            mates(lambda where: send(dsrc.at[i, t], dall.at[slot], dsend.at[1], dsem.at[mine[i] - h + 1, t], where))
            dall[slot] = dsrc[i, t]
        for i in range(R):
            for k in range(C):
                att_src[i, k] = attended[i * W : (i + 1) * W, k * half : (k + 1) * half]
        stat2[me] = stat2_src[t]
        att_out[c, 0] = att_src[0, c]
        if R == 2:
            if T > 1:
                drain(dall.at[pl.ds(0, 2 * (T - 1))], dsend.at[0])
            pl.when(t > 0)(own_column)

    if S > 4:
        pl.when(attends & jnp.logical_not(at_edge))(lambda: attend(1))
    pl.when(at_edge)(lambda: attend(2))
    act[0:2] = jnp.zeros((2,) + act.shape[1:], BF16)
    gain2 = jnp.concatenate([gall[k, 1] for k in range(C)], axis=1)

    rows = [(0, h > 0, h == 1), (1, h >= 0, attends), (2, h < S - 1, h == S - 2)]

    def forward(k):
        for row, there, made_here in rows:

            @pl.when(there & jnp.logical_not(made_here & (t == k)))
            def _():
                slot = row * NF + k * C + c
                drain(dall.at[slot], direct_sem.at[row, k])
                mates(lambda where: send(dall.at[slot], dall.at[slot], dsend.at[1], dsem.at[row, k], where))


    forward(0)
    for k in range(1, T):
        pl.when((t < k) & (c > 0))(lambda: forward(k))


    @pl.when(jnp.logical_not(attends))
    def _():
        drain(stat2.at[pl.ds(0, attending)], s2sem)

    @pl.when(attends)
    def _():
        drain(stat2.at[pl.ds(0, attending - 1)], s2sem)
        send_attended(0, other, h, other)

    @pl.when(at_edge)
    def _():
        for k in range(C):
            send_attended(1, k, h + side, k)


    def sliced(v):
        out = v[:, 0:Kc]
        for k in range(1, T):
            out = jnp.where(t == k, v[:, k * Kc : (k + 1) * Kc], out)
        return out

    mean2, scale2 = slice_moments(jnp.sum(stat2[0:attending], axis=0), population)
    factor2 = scale2 * sliced(gain2)
    column = lax.broadcasted_iota(jnp.int32, (W, Kc), 0)

    def activate(row, k):
        for f in range(k * C, (k + 1) * C):
            v = (dall[row * NF + f].astype(F32) - mean2) * factor2
            a = v / (1.0 + jnp.exp(-v))
            left = jnp.where(column == 0, 0.0, pltpu.roll(a, 1, 0))
            right = jnp.where(column == W - 1, 0.0, pltpu.roll(a, W - 1, 0))
            for e, piece in enumerate((left, a, right)):
                place = row * 3 + e
                act[f + 2, :, place * Kc : (place + 1) * Kc] = piece.astype(BF16)

    skips = (3 * Kc) % LANES == 0

    def blank(row):
        act[2:, :, row * 3 * Kc : (row + 1) * 3 * Kc] = jnp.zeros((NF, W, 3 * Kc), BF16)

    if not skips:
        pl.when(h == 0)(lambda: blank(0))
        pl.when(h == S - 1)(lambda: blank(2))

    def block_in(k):
        if k:
            pl.when(t >= k)(lambda: forward(k))
        for row, there, _ in rows:

            @pl.when(there)
            def _():
                drain(dall.at[pl.ds(0, C - 1)], dsem.at[row, k])
                activate(row, k)

    wide = half // CHUNKS

    def product(to, b0, b1, chunk):
        total = None
        taps = slice(b0 * 3 * Kc, b1 * 3 * Kc)
        for a in range(0 if to else max(0, 3 - C), 3):
            window = act[to * C + a : to * C + a + C, :, taps].reshape(C * W, (b1 - b0) * 3 * Kc)
            weight = wc[a, taps, chunk * wide : (chunk + 1) * wide]
            term = jnp.dot(window, weight, preferred_element_type=F32)
            total = term if total is None else total + term
        return total

    if not skips:
        edges = [(t >= 0, 0, 3)]
    else:
        edges = [(h == 0, 1, 3), (h == S - 1, 0, 2), (attends, 0, 3)]

    def convolve(to, store):
        for here, b0, b1 in edges:

            @pl.when(here)
            def _():
                for chunk in range(CHUNKS):
                    store(chunk, product(to, b0, b1, chunk))

    def convolve_away(to):
        away = lax.rem(to - t + T, T) - 1

        def store(chunk, value):
            part_src[away, chunk] = value.astype(BF16)
            send(part_src.at[away, chunk], part.at[away, chunk], psend, psem.at[away, chunk], (g, h, to, c))

        convolve(to, store)

    def keep(chunk, value):
        own_total[chunk] = value

    pl.when(c == 0)(lambda: block_in(0))
    for k in range(1, T):
        pl.when((t < k) & (c == 0))(lambda: forward(k))

    pl.when(c > 0)(lambda: block_in(0))
    loads[4].wait()
    for k in range(T):
        if k:
            block_in(k)
        pl.when(t != k)(lambda: convolve_away(k))

    for k in range(T):
        pl.when(t == k)(lambda: convolve(k, keep))

    @pl.when(attends)
    def _():
        drain(att_in.at[pl.ds(0, C - 1)], asem)
        att_out[other, 0] = att_in[other]
        drain(xall.at[pl.ds(0, (S - 2) * C - 1)], xsend)
        drain(stat2.at[pl.ds(0, S * T * C - 1)], s2send)

    @pl.when(jnp.logical_not(attends))
    def _():
        drain(att_in, asem)
        for k in range(C):
            att_out[k, 0] = att_in[k]
        drain(xall.at[pl.ds(0, (S - 2) * C)], xsend)
        drain(dall.at[pl.ds(0, 2 * T * (C - 1))], dsend.at[1])

    for r in range(S):

        @pl.when(h == r)
        def _():
            below = max(r - 1, 0) if r < S - 1 else S - 2
            level = (T - 1 if r == 0 else T * C - 1) if r < S - 1 else 0
            above = max(S - 2 - r, 0)
            drain(stat1.at[pl.ds(0, below * T * C + level + above * C)], s1send)

    @pl.when(attends & jnp.logical_not(at_edge))
    def _():
        drain(dall.at[pl.ds(0, 3 * T + C - 2 + (3 * T - 1) * (C - 1))], dsend.at[1])
        drain(att_src.at[0, 0], asend)

    @pl.when(at_edge)
    def _():
        drain(dall.at[pl.ds(0, 3 * T + 2 * C - 2 + (3 * T - 2) * (C - 1))], dsend.at[1])
        drain(xall.at[pl.ds(0, C + 1)], asend)

    drain(gall.at[pl.ds(0, C - 1)], gsend)
    for chunk in range(CHUNKS):
        total = own_total[chunk]
        for dt in range(1, T):
            drain(part.at[dt - 1, chunk], psem.at[dt - 1, chunk])
            total = total + part[dt - 1, chunk].astype(F32)
        conv_out[:, 0, :, chunk * wide : (chunk + 1) * wide] = total.reshape(C, W, wide).astype(BF16)
    if T > 1:
        drain(part_src, psend)


def slice_moments(totals, population):
    width = totals.shape[1]
    if width == LANES:
        return moments([totals], population)
    mean, scale = moments([jnp.concatenate([totals] * (LANES // width), axis=1)], population)
    return mean[:, :width], scale[:, :width]


def hand_over(att_in, conv_in, att_out, conv_out):
    att_out[...] = att_in[...]
    conv_out[...] = conv_in[...]


def on_device(S, T, C, x, g1, g2, wq, wk, wv, wo, wc):
    frames, rows, W, half = x.shape
    assert frames == C and rows == 1 and half * C == D
    Kc = wc.shape[3]
    assert Kc * T == D and S > 3
    n, NF = S * T * C, T * C
    wide = half // CHUNKS
    wc = wc.reshape(3, 9 * Kc, half)
    vmem = pl.BlockSpec(memory_space=pltpu.VMEM)
    hbm = pl.BlockSpec(memory_space=pl.ANY)
    out = jax.ShapeDtypeStruct(x.shape, BF16)
    dma = pltpu.SemaphoreType.DMA
    kept = pltpu.VMEM(x.shape, BF16)
    links = max(T - 1, 1)
    stats = (2 * max(Kc // LANES, 1), min(Kc, LANES))
    results = pl.pallas_call(
        functools.partial(kernel, S, T, C, W),
        out_shape=(kept, kept),
        in_specs=[hbm] * 8,
        out_specs=(vmem, vmem),
        scratch_shapes=[
            pltpu.VMEM(x.shape, BF16),
            pltpu.VMEM((4, D, D), BF16),
            pltpu.VMEM(wc.shape, BF16),
            pltpu.VMEM((half // 64, LANES), F32),
            pltpu.VMEM((half // 64, LANES), F32),
            pltpu.VMEM((n, half // 64, LANES), F32),
            pltpu.VMEM((T, *stats), F32),
            pltpu.VMEM((n, *stats), F32),
            pltpu.VMEM((C, 2, 1, half), F32),
            pltpu.VMEM((S * C, W, half), BF16),
            pltpu.VMEM((S, W, D), BF16),
            pltpu.VMEM((S * W, D), BF16),
            pltpu.VMEM((S * W, D), BF16),
            pltpu.VMEM((2, C, W, half), BF16),
            pltpu.VMEM((C, W, half), BF16),
            pltpu.VMEM((2, T, W, Kc), BF16),
            pltpu.VMEM((3 * NF, W, Kc), BF16),
            pltpu.VMEM((NF + 2, W, 9 * Kc), BF16),
            pltpu.VMEM((CHUNKS, C * W, wide), F32),
            pltpu.VMEM((links, CHUNKS, C * W, wide), BF16),
            pltpu.VMEM((links, CHUNKS, C * W, wide), BF16),
            dma((2,)),
            dma((2,)),
            pltpu.SemaphoreType.REGULAR((S - 1,)),
            dma(()),
            dma(()),
            dma(()),
            dma(()),
            dma(()),
            dma(()),
            dma(()),
            dma(()),
            dma(()),
            dma(()),
            dma(()),
            dma((2,)),
            dma((3, T)),
            dma((3, T)),
            dma(()),
            dma((links, CHUNKS)),
        ],
        compiler_params=pltpu.CompilerParams(collective_id=0, has_side_effects=True),
    )(x, g1.reshape(1, half), g2.reshape(1, half), wq, wk, wv, wo, wc)
    return pl.pallas_call(
        hand_over, out_shape=(out, out), in_specs=[vmem] * 2, out_specs=(vmem, vmem),
    )(*[pltpu.with_memory_space_constraint(r, pltpu.VMEM) for r in results])


def solution(mesh):
    S, T, C = mesh.shape["space"], mesh.shape["tm"], mesh.shape["chan"]
    placed = (
        P(("groups", "tm"), "space", None, "chan"),
        P("chan"),
        P("chan"),
        P(),
        P(),
        P(),
        P(),
        P(None, None, None, "tm", "chan"),
    )
    return jax.shard_map(
        functools.partial(on_device, S, T, C),
        mesh=mesh,
        in_specs=placed,
        out_specs=(
            P(("groups", "tm"), "space", None, "chan"),
            P(("groups", "tm"), "space", None, "chan"),
        ),
        check_vma=False,
    )
```

```python
import functools

import jax
import jax.numpy as jnp
from jax import lax
from jax.experimental import pallas as pl
from jax.experimental.pallas import tpu as pltpu
from jax.sharding import PartitionSpec as P

D = 512
NGROUP = 32
EPSILON = 1e-06
LANES = 128
CHUNKS = 1
GROUP = D // NGROUP
MESH = pl.DeviceIdType.MESH
F32 = jnp.float32
BF16 = jnp.bfloat16


def group_total(v):
    lane = lax.broadcasted_iota(jnp.int32, v.shape, 1)
    width = v.shape[1]
    step = 1
    while step < GROUP:
        place = (lane // step) % 4
        terms = [v]
        for d in range(1, 4):
            terms.append(jnp.where(place < 4 - d, pltpu.roll(v, width - d * step, 1), 0.0))
            terms.append(jnp.where(place >= d, pltpu.roll(v, d * step, 1), 0.0))
        while len(terms) > 1:
            terms = [sum(terms[i : i + 2]) for i in range(0, len(terms), 2)]
        v = terms[0]
        step *= 4
    return v


def store_sums(ref, values):
    sums = jnp.sum(values, axis=0, keepdims=True)
    squares = jnp.sum(values * values, axis=0, keepdims=True)
    blocks, width = ref.shape[0] // 2, ref.shape[1]
    for b in range(blocks):
        ref[b : b + 1] = sums[:, b * width : (b + 1) * width]
        ref[blocks + b : blocks + b + 1] = squares[:, b * width : (b + 1) * width]


def moments(stacks, population):
    size = stacks[0].shape[0]
    blocks = size // 2
    count = len(stacks) * size
    rows = 8 * pl.cdiv(count, 8)
    padding = [jnp.zeros((rows - count, LANES), F32)] if rows > count else []
    grouped = group_total(jnp.concatenate([*stacks, *padding], axis=0)) / population
    variance = jnp.maximum(pltpu.roll(grouped, rows - blocks, 0) - grouped * grouped, 0.0)
    scale = lax.rsqrt(variance + EPSILON)
    picks = [i * size + b for i in range(len(stacks)) for b in range(blocks)]
    return [jnp.concatenate([v[k : k + 1] for k in picks], axis=1) for v in (grouped, scale)]


def kernel(
    S, T, C, W,
    x_hbm, g1, g2, wq_hbm, wk_hbm, wv_hbm, wo_hbm, wc_hbm,
    att_out, conv_out,
    x, projections, wc,
    stat1_src, row_sum, stat1, stat2_src, stat2, gall,
    xall, tokens, keyed, valued, att_src, att_in, dsrc, dall, act, own_total, part_src, part,
    xload, wsem, insem, gsend, gsem, raw_sem, s1send, s1sem, xsend, xsem, s2send, s2sem,
    asend, asem, dsend, dsem, direct_sem, psend, psem,
):
    g = lax.axis_index("groups")
    h = lax.axis_index("space")
    t = lax.axis_index("tm")
    c = lax.axis_index("chan")
    attending = (S - 2) * T * C
    me = (h * T + t) * C + c - T * C
    half = D // C
    Kc = D // T
    NF = T * C
    other = lax.rem(c + 1, C)
    attends = (h > 0) & (h < S - 1)
    at_edge = (h == 1) | (h == S - 2)
    side = jnp.where(h == 1, -1, 1)

    def rows_apart(sign, act_on):
        def row(d):
            @pl.when((h + sign * d >= 0) & (h + sign * d < S))
            def _():
                act_on(h + sign * d, d)

        pl.loop(1, S, unroll=S <= 4)(row)

    def row_devices(r, act_on):
        for dt in range(T):
            for dc in range(C):
                act_on((g, r, lax.rem(t + dt, T), lax.rem(c + dc, C)))

    def row_where(r, sign, act_on):
        for dt in range(1, T):

            @pl.when((t + sign * dt >= 0) & (t + sign * dt < T))
            def _():
                for dc in range(C):
                    act_on((g, r, t + sign * dt, lax.rem(c + dc, C)))

    def beside(sign, act_on):
        row_where(h, sign, act_on)

    def mates(act_on):
        for dc in range(1, C):
            act_on((g, h, t, lax.rem(c + dc, C)))

    def signal(sem):
        return lambda where: pl.semaphore_signal(sem, inc=1, device_id=where, device_id_type=MESH)

    def drain(ref, sem):
        pltpu.make_async_copy(ref, ref, sem).wait()

    def send(src, dst, sends, recvs, where):
        copy = pltpu.make_async_remote_copy(
            src_ref=src, dst_ref=dst, send_sem=sends, recv_sem=recvs, device_id=where, device_id_type=MESH,
        )
        copy.start()

    x_load = pltpu.make_async_copy(x_hbm, x, xload.at[0])
    x_load.start()
    for k, gain in enumerate((g1, g2)):
        pltpu.make_async_copy(gain, gall.at[c, k], xload.at[1]).start()
    stat1[...] = jnp.zeros(stat1.shape, F32)
    barrier = pltpu.get_barrier_semaphore()
    mates(signal(barrier))
    beside(1, signal(barrier))

    def column(r, act_on):
        for dc in range(C):
            act_on((g, r, t, lax.rem(c + dc, C)))

    def greet(r, d):
        column(r, signal(barrier))
        row_where(r, 1, signal(barrier))

    rows_apart(1, greet)
    pl.semaphore_wait(barrier, (h * (t + 1) + t) * C + C - 1)
    pl.when(h < S - 1)(lambda: rows_apart(-1, lambda r, d: column(r, signal(insem.at[d]))))
    beside(-1, signal(insem.at[0]))

    loads = [
        pltpu.make_async_copy(src, dst, wsem.at[i])
        for i, (src, dst) in zip((0, 0, 0, 0, 1), [(wq_hbm, projections.at[0]), (wk_hbm, projections.at[1]), (wv_hbm, projections.at[2]), (wo_hbm, projections.at[3]), (wc_hbm, wc)])
    ]


    x_load.wait()
    store_sums(stat1_src, x[...].reshape(C * W, half).astype(F32))
    at = (h * T + t) * C + c

    def send_stat(where, src=stat1_src, recvs=s1sem):
        send(src, stat1.at[at], s1send, recvs, where)

    def same_row(sign):
        for dt in range(1, T):

            @pl.when((t + sign * dt >= 0) & (t + sign * dt < T))
            def _():
                send_stat((g, h, t + sign * dt, c), recvs=raw_sem)

                @pl.when(attends)
                def _():
                    for dc in range(1, C):
                        send_stat((g, h, t + sign * dt, lax.rem(c + dc, C)))

    def send_x(r, dc):
        frame = lax.rem(c + dc, C)
        send(x.at[frame, 0], xall.at[h * C + c], xsend, xsem, (g, r, t, frame))

    def column_x(r):
        for dc in range(C):
            send_x(r, dc)

    for r in range(1, S - 1):

        @pl.when(r < h)
        def _():
            column(r, send_stat)
            row_where(r, -1, send_stat)

    pl.when(h < S - 1)(lambda: same_row(-1))
    stat1[at] = stat1_src[...]

    @pl.when(attends)
    def _():
        mates(send_stat)
        xall[h * C + c] = x[c, 0]
        for dc in range(1, C):
            send_x(h, dc)

    for r in range(1, S - 1):
        pl.when((r < h) & ((h < S - 1) | (r < S - 2)))(lambda: column_x(r))

    drain(gall.at[c], xload.at[1])
    mates(lambda where: send(gall.at[c], gall.at[c], gsend, gsem, where))
    @pl.when(attends)
    def _():
        for load in loads[:4]:
            load.start()

    loads[4].start()

    @pl.when(h < S - 2)
    def _():
        pl.semaphore_wait(insem.at[1], C)
        column_x(h + 1)

    @pl.when(t < T - 1)
    def _():
        pl.semaphore_wait(insem.at[0], (T - 1 - t) * C)
        for r in range(1, S - 1):
            pl.when(r < h)(lambda: row_where(r, 1, send_stat))
        pl.when(h < S - 1)(lambda: same_row(1))

    pl.when(h == S - 1)(lambda: column_x(S - 2))
    @pl.when(h < S - 1)
    def _():
        if T > 1:
            drain(stat1.at[pl.ds(0, T - 1)], raw_sem)

    @pl.when(h < S - 2)
    def _():
        total = stat1_src[...]
        for dt in range(1, T):
            total = total + stat1[(h * T + lax.rem(t + dt, T)) * C + c]
        row_sum[...] = total

        def send_sum(where):
            send_stat(where, src=row_sum)

        column(h + 1, send_sum)

        def upward(d):
            @pl.when(h + d < S - 1)
            def _():
                pl.semaphore_wait(insem.at[d], C)
                column(h + d, send_sum)
                column_x(h + d)

        pl.loop(2, S - 1, unroll=S <= 4)(upward)

    drain(gall.at[pl.ds(0, C - 1)], gsem)
    population = float(S * T * C * W * GROUP)
    frame_at = t * C + c

    def send_attended(i, k, r, core):
        send(att_src.at[i, k], att_in.at[c], asend, asem, (g, r, t, core))

    def attend(R):
        outer = h + side
        mine = [h, outer][:R]
        skipped = jnp.where(h == 1, R, 0) if R == 2 else None

        def rest(i):
            return i + skipped if R == 2 else i + jnp.where(i >= h, 1, 0)

        for r in range(1, S - 1):

            @pl.when(h == r)
            def _():
                drain(stat1.at[pl.ds(0, r * C + T * (C - 1) + (S - 1 - r) * T * C)], s1sem)

        drain(xall.at[pl.ds(0, S * C - 1)], xsem)
        drain(projections, wsem.at[0])
        totals = jnp.sum(stat1[...].reshape(S * T, C, *stat1.shape[1:]), axis=0)
        mean1, scale1 = moments([totals[k] for k in range(C)], population)
        factor1 = scale1 * jnp.concatenate([gall[k, 0] for k in range(C)], axis=1)

        def row_tokens(r):
            pieces = []
            for k in range(C):
                lanes = slice(k * half, (k + 1) * half)
                value = xall[r * C + k].astype(F32)
                pieces.append(((value - mean1[:, lanes]) * factor1[:, lanes]).astype(BF16))
            return jnp.concatenate(pieces, axis=1)

        def project(weight, first, stop):
            rows = tokens[first:stop].reshape((stop - first) * W, D)
            return jnp.dot(rows, weight[...], preferred_element_type=F32).astype(BF16)

        for i in range(R):
            tokens[i] = row_tokens(mine[i])
        for i in range(S - R):
            tokens[R + i] = row_tokens(rest(i))
        queries = project(projections.at[0], 0, R)
        keyed[...] = project(projections.at[1], 0, S)
        valued[...] = project(projections.at[2], 0, S)

        scores = lax.dot_general(
            queries, keyed[...], (((1,), (1,)), ((), ())), preferred_element_type=F32
        ) * (D ** (-0.5))
        weights = jnp.exp(scores - jnp.max(scores, axis=1, keepdims=True))
        mass = jnp.sum(weights, axis=1, keepdims=True)
        mixed = jnp.dot(weights.astype(BF16), valued[...], preferred_element_type=F32)
        mixed = (mixed * (1.0 / mass)).astype(BF16)
        attended = jnp.dot(mixed, projections[3], preferred_element_type=F32).astype(BF16)

        source = jnp.concatenate(
            [jnp.concatenate([xall[r * C + k] for k in range(C)], axis=1) for r in mine], axis=0
        ).astype(F32)
        resid = (source - mean1) + attended.astype(F32)
        for i in range(R):
            for k in range(T):
                dsrc[i, k] = resid[i * W : (i + 1) * W, k * Kc : (k + 1) * Kc].astype(BF16)

        def send_row(i, r, columns, sends):
            for dt in columns:
                to = lax.rem(t + dt, T)
                row = mine[i] - r + 1
                send(
                    dsrc.at[i, to], dall.at[row * NF + frame_at], sends, direct_sem.at[row, t], (g, r, to, c),
                )

        others = range(1, T)
        for k in range(T):
            store_sums(stat2_src.at[k], resid[:, k * Kc : (k + 1) * Kc])

        def send_stat2(where):
            send(stat2_src.at[where[2]], stat2.at[me], s2send, s2sem, where)

        if R == 2:
            row_devices(outer, send_stat2)
            for i in range(2):
                send_row(i, outer, others, dsend.at[0])

            def own_column():
                for i in range(2):
                    send_row(i, outer, [0], dsend.at[1])

            pl.when(t == 0)(own_column)
        def beyond_outer(r, d):
            if R == 2:
                pl.when(r != outer)(lambda: row_devices(r, send_stat2))
            else:
                row_devices(r, send_stat2)

        rows_apart(-1, beyond_outer)
        rows_apart(1, beyond_outer)
        beside(-1, send_stat2)
        beside(1, send_stat2)
        mates(send_stat2)
        if R == 2:
            send_row(0, h - side, [*others, 0], dsend.at[1])
        else:
            for r in (h - 1, h + 1):
                send_row(0, r, [*others, 0], dsend.at[1])
        for i in range(R):
            send_row(i, h, others, dsend.at[1])
            slot = (mine[i] - h + 1) * NF + frame_at
            mates(lambda where: send(dsrc.at[i, t], dall.at[slot], dsend.at[1], dsem.at[mine[i] - h + 1, t], where))
            dall[slot] = dsrc[i, t]
        for i in range(R):
            for k in range(C):
                att_src[i, k] = attended[i * W : (i + 1) * W, k * half : (k + 1) * half]
        stat2[me] = stat2_src[t]
        att_out[c, 0] = att_src[0, c]
        if R == 2:
            if T > 1:
                drain(dall.at[pl.ds(0, 2 * (T - 1))], dsend.at[0])
            pl.when(t > 0)(own_column)

    if S > 4:
        pl.when(attends & jnp.logical_not(at_edge))(lambda: attend(1))
    pl.when(at_edge)(lambda: attend(2))
    act[0:2] = jnp.zeros((2,) + act.shape[1:], BF16)
    gain2 = jnp.concatenate([gall[k, 1] for k in range(C)], axis=1)

    rows = [(0, h > 0, h == 1), (1, h >= 0, attends), (2, h < S - 1, h == S - 2)]

    def forward(k):
        for row, there, made_here in rows:

            @pl.when(there & jnp.logical_not(made_here & (t == k)))
            def _():
                slot = row * NF + k * C + c
                drain(dall.at[slot], direct_sem.at[row, k])
                mates(lambda where: send(dall.at[slot], dall.at[slot], dsend.at[1], dsem.at[row, k], where))


    forward(0)
    for k in range(1, T):
        pl.when((t < k) & (c > 0))(lambda: forward(k))


    @pl.when(jnp.logical_not(attends))
    def _():
        drain(stat2.at[pl.ds(0, attending)], s2sem)

    @pl.when(attends)
    def _():
        drain(stat2.at[pl.ds(0, attending - 1)], s2sem)
        send_attended(0, other, h, other)

    @pl.when(at_edge)
    def _():
        for k in range(C):
            send_attended(1, k, h + side, k)


    def sliced(v):
        out = v[:, 0:Kc]
        for k in range(1, T):
            out = jnp.where(t == k, v[:, k * Kc : (k + 1) * Kc], out)
        return out

    mean2, scale2 = slice_moments(jnp.sum(stat2[0:attending], axis=0), population)
    factor2 = scale2 * sliced(gain2)
    column = lax.broadcasted_iota(jnp.int32, (W, Kc), 0)

    def activate(row, k):
        for f in range(k * C, (k + 1) * C):
            v = (dall[row * NF + f].astype(F32) - mean2) * factor2
            a = v / (1.0 + jnp.exp(-v))
            left = jnp.where(column == 0, 0.0, pltpu.roll(a, 1, 0))
            right = jnp.where(column == W - 1, 0.0, pltpu.roll(a, W - 1, 0))
            for e, piece in enumerate((left, a, right)):
                place = row * 3 + e
                act[f + 2, :, place * Kc : (place + 1) * Kc] = piece.astype(BF16)

    skips = (3 * Kc) % LANES == 0

    def blank(row):
        act[2:, :, row * 3 * Kc : (row + 1) * 3 * Kc] = jnp.zeros((NF, W, 3 * Kc), BF16)

    if not skips:
        pl.when(h == 0)(lambda: blank(0))
        pl.when(h == S - 1)(lambda: blank(2))

    def block_in(k):
        if k:
            pl.when(t >= k)(lambda: forward(k))
        for row, there, _ in rows:

            @pl.when(there)
            def _():
                drain(dall.at[pl.ds(0, C - 1)], dsem.at[row, k])
                activate(row, k)

    wide = half // CHUNKS

    def product(to, b0, b1, chunk):
        total = None
        taps = slice(b0 * 3 * Kc, b1 * 3 * Kc)
        for a in range(0 if to else max(0, 3 - C), 3):
            window = act[to * C + a : to * C + a + C, :, taps].reshape(C * W, (b1 - b0) * 3 * Kc)
            weight = wc[a, taps, chunk * wide : (chunk + 1) * wide]
            term = jnp.dot(window, weight, preferred_element_type=F32)
            total = term if total is None else total + term
        return total

    if not skips:
        edges = [(t >= 0, 0, 3)]
    else:
        edges = [(h == 0, 1, 3), (h == S - 1, 0, 2), (attends, 0, 3)]

    def convolve(to, store):
        for here, b0, b1 in edges:

            @pl.when(here)
            def _():
                for chunk in range(CHUNKS):
                    store(chunk, product(to, b0, b1, chunk))

    def convolve_away(to):
        away = lax.rem(to - t + T, T) - 1

        def store(chunk, value):
            part_src[away, chunk] = value.astype(BF16)
            send(part_src.at[away, chunk], part.at[away, chunk], psend, psem.at[away, chunk], (g, h, to, c))

        convolve(to, store)

    def keep(chunk, value):
        own_total[chunk] = value

    pl.when(c == 0)(lambda: block_in(0))
    for k in range(1, T):
        pl.when((t < k) & (c == 0))(lambda: forward(k))

    pl.when(c > 0)(lambda: block_in(0))
    loads[4].wait()
    for k in range(T):
        if k:
            block_in(k)
        pl.when(t != k)(lambda: convolve_away(k))

    for k in range(T):
        pl.when(t == k)(lambda: convolve(k, keep))

    @pl.when(attends)
    def _():
        drain(att_in.at[pl.ds(0, C - 1)], asem)
        att_out[other, 0] = att_in[other]
        drain(xall.at[pl.ds(0, (S - 2) * C - 1)], xsend)
        drain(stat2.at[pl.ds(0, S * T * C - 1)], s2send)

    @pl.when(jnp.logical_not(attends))
    def _():
        drain(att_in, asem)
        for k in range(C):
            att_out[k, 0] = att_in[k]
        drain(xall.at[pl.ds(0, (S - 2) * C)], xsend)
        drain(dall.at[pl.ds(0, 2 * T * (C - 1))], dsend.at[1])

    for r in range(S):

        @pl.when(h == r)
        def _():
            below = max(r - 1, 0) if r < S - 1 else S - 2
            level = (T - 1 if r == 0 else T * C - 1) if r < S - 1 else 0
            above = max(S - 2 - r, 0)
            drain(stat1.at[pl.ds(0, below * T * C + level + above * C)], s1send)

    @pl.when(attends & jnp.logical_not(at_edge))
    def _():
        drain(dall.at[pl.ds(0, 3 * T + C - 2 + (3 * T - 1) * (C - 1))], dsend.at[1])
        drain(att_src.at[0, 0], asend)

    @pl.when(at_edge)
    def _():
        drain(dall.at[pl.ds(0, 3 * T + 2 * C - 2 + (3 * T - 2) * (C - 1))], dsend.at[1])
        drain(xall.at[pl.ds(0, C + 1)], asend)

    drain(gall.at[pl.ds(0, C - 1)], gsend)
    for chunk in range(CHUNKS):
        total = own_total[chunk]
        for dt in range(1, T):
            drain(part.at[dt - 1, chunk], psem.at[dt - 1, chunk])
            total = total + part[dt - 1, chunk].astype(F32)
        conv_out[:, 0, :, chunk * wide : (chunk + 1) * wide] = total.reshape(C, W, wide).astype(BF16)
    if T > 1:
        drain(part_src, psend)


def slice_moments(totals, population):
    width = totals.shape[1]
    if width == LANES:
        return moments([totals], population)
    mean, scale = moments([jnp.concatenate([totals] * (LANES // width), axis=1)], population)
    return mean[:, :width], scale[:, :width]


def hand_over(att_in, conv_in, att_out, conv_out):
    att_out[...] = att_in[...]
    conv_out[...] = conv_in[...]


def on_device(S, T, C, x, g1, g2, wq, wk, wv, wo, wc):
    frames, rows, W, half = x.shape
    assert frames == C and rows == 1 and half * C == D
    Kc = wc.shape[3]
    assert Kc * T == D and S > 3
    n, NF = S * T * C, T * C
    wide = half // CHUNKS
    wc = wc.reshape(3, 9 * Kc, half)
    vmem = pl.BlockSpec(memory_space=pltpu.VMEM)
    hbm = pl.BlockSpec(memory_space=pl.ANY)
    out = jax.ShapeDtypeStruct(x.shape, BF16)
    dma = pltpu.SemaphoreType.DMA
    kept = pltpu.VMEM(x.shape, BF16)
    links = max(T - 1, 1)
    stats = (2 * max(Kc // LANES, 1), min(Kc, LANES))
    results = pl.pallas_call(
        functools.partial(kernel, S, T, C, W),
        out_shape=(kept, kept),
        in_specs=[hbm] * 8,
        out_specs=(vmem, vmem),
        scratch_shapes=[
            pltpu.VMEM(x.shape, BF16),
            pltpu.VMEM((4, D, D), BF16),
            pltpu.VMEM(wc.shape, BF16),
            pltpu.VMEM((half // 64, LANES), F32),
            pltpu.VMEM((half // 64, LANES), F32),
            pltpu.VMEM((n, half // 64, LANES), F32),
            pltpu.VMEM((T, *stats), F32),
            pltpu.VMEM((n, *stats), F32),
            pltpu.VMEM((C, 2, 1, half), F32),
            pltpu.VMEM((S * C, W, half), BF16),
            pltpu.VMEM((S, W, D), BF16),
            pltpu.VMEM((S * W, D), BF16),
            pltpu.VMEM((S * W, D), BF16),
            pltpu.VMEM((2, C, W, half), BF16),
            pltpu.VMEM((C, W, half), BF16),
            pltpu.VMEM((2, T, W, Kc), BF16),
            pltpu.VMEM((3 * NF, W, Kc), BF16),
            pltpu.VMEM((NF + 2, W, 9 * Kc), BF16),
            pltpu.VMEM((CHUNKS, C * W, wide), F32),
            pltpu.VMEM((links, CHUNKS, C * W, wide), BF16),
            pltpu.VMEM((links, CHUNKS, C * W, wide), BF16),
            dma((2,)),
            dma((2,)),
            pltpu.SemaphoreType.REGULAR((S - 1,)),
            dma(()),
            dma(()),
            dma(()),
            dma(()),
            dma(()),
            dma(()),
            dma(()),
            dma(()),
            dma(()),
            dma(()),
            dma(()),
            dma((2,)),
            dma((3, T)),
            dma((3, T)),
            dma(()),
            dma((links, CHUNKS)),
        ],
        compiler_params=pltpu.CompilerParams(collective_id=0, has_side_effects=True),
    )(x, g1.reshape(1, half), g2.reshape(1, half), wq, wk, wv, wo, wc)
    return pl.pallas_call(
        hand_over, out_shape=(out, out), in_specs=[vmem] * 2, out_specs=(vmem, vmem),
    )(*[pltpu.with_memory_space_constraint(r, pltpu.VMEM) for r in results])


def solution(mesh):
    S, T, C = mesh.shape["space"], mesh.shape["tm"], mesh.shape["chan"]
    placed = (
        P(("groups", "tm"), "space", None, "chan"),
        P("chan"),
        P("chan"),
        P(),
        P(),
        P(),
        P(),
        P(None, None, None, "tm", "chan"),
    )
    return jax.shard_map(
        functools.partial(on_device, S, T, C),
        mesh=mesh,
        in_specs=placed,
        out_specs=(
            P(("groups", "tm"), "space", None, "chan"),
            P(("groups", "tm"), "space", None, "chan"),
        ),
        check_vma=False,
    )
```
